32 devices in a mesh: fsdp: 8 (over y, x, core), tensor: 4 (over z).
Axes of the slice: x: 2, y: 2, z: 4, core: 2. Of those that a mesh axis runs over, the one named last changes fastest.
Arguments:
- inputs: bfloat16 [32, 577, 1024], P('fsdp'), may hold values from -6 to 6
- lengths: int32 [32], P('fsdp'), may hold values from 144 to 577, as said below
- norm_gains: bfloat16 [2, 1024], P(None, 'fsdp'), may hold values from 0.5 to 1.5
- norm_shifts: bfloat16 [2, 1024], P(None, 'fsdp'), may hold values from -1.5 to 1.5
- w_qkv: bfloat16 [3, 1024, 1024], P(None, 'fsdp', 'tensor'), may hold values from -0.1875 to 0.1875
- bias_qv: bfloat16 [2, 1024], P(None, 'tensor'), may hold values from -3 to 3
- w_out: bfloat16 [1024, 1024], P('tensor', 'fsdp'), may hold values from -1.5 to 1.5
- out_bias: bfloat16 [2, 1024], P(None, 'fsdp'), may hold values from -1.5 to 1.5
- w_up: bfloat16 [1024, 4096], P('fsdp', 'tensor'), may hold values from -0.1875 to 0.1875
- b_up: bfloat16 [4096], P('tensor'), may hold values from -3 to 3
- w_down: bfloat16 [4096, 1024], P('tensor', 'fsdp'), may hold values from -0.375 to 0.375
- cotangent: bfloat16 [32, 577, 1024], P('fsdp'), may hold values from -6 to 6
Outputs:
- output: bfloat16 [32, 577, 1024], P('fsdp')
- grad_input: float32 [32, 577, 1024], P('fsdp')
- grad_gains: float32 [2, 1024], P(None, 'fsdp')
- grad_shifts: float32 [2, 1024], P(None, 'fsdp')
- grad_qkv: float32 [3, 1024, 1024], P(None, 'fsdp', 'tensor')
- grad_bias_qv: float32 [2, 1024], P(None, 'tensor')
- grad_out: float32 [1024, 1024], P('tensor', 'fsdp')
- grad_out_bias: float32 [2, 1024], P(None, 'fsdp')
- grad_up: float32 [1024, 4096], P('fsdp', 'tensor')
- grad_b_up: float32 [4096], P('tensor')
- grad_down: float32 [4096, 1024], P('tensor', 'fsdp')
The draws below stay inside these ranges and needn't reach their ends.
Inputs may be any that keep to these rules, and one draw needn't show every extreme that they name: lengths[b] counts the valid leading tokens of image b; some image has all 577 valid and some has 144.
All inputs are finite; a program needn't handle non-finite values.
Results may differ from the reference program's by a relative error of at most 0.02.
Values may be sent and summed in bfloat16 or wider, within the bound.
A program may use at most 256 MiB of HBM per device.

```python
import jax
import jax.numpy as jnp
from jax import lax

D = 1024
FF = 4096
HEAD = 64
SEQ = 577
IMAGES = 32
N_TENSOR = 4


def draw_lengths(key, part):
    counts = jax.random.randint(key, (IMAGES,), SEQ // 4, SEQ + 1)
    counts = counts.at[0].set(SEQ)
    counts = counts.at[1].set(SEQ // 4)
    return counts.astype(jnp.int32)


def level_of(stream_key, dims, cuts, smallest, largest):
    def one(position, parts):
        steps = jax.random.uniform(jax.random.fold_in(jax.random.fold_in(stream_key, 6), position), (parts,), jnp.float32, smallest / len(cuts), largest / len(cuts))
        return jnp.repeat(jnp.exp(steps), dims[position] // parts).reshape((-1,) + (1,) * (len(dims) - position - 1))

    level = one(*cuts[0])
    for cut in cuts[1:]:
        level = level * one(*cut)
    return level


def noise(key, extent, scale, most, split=(), held_as=jnp.bfloat16):
    drawn = scale * jax.random.normal(key, extent, jnp.float32)
    if split:
        drawn = drawn * level_of(key, extent, split, -0.22, 0.18)
    return jnp.clip(drawn, -most, most).astype(held_as)


def setup_inputs(seed: int = 0) -> dict:
    splits = jax.random.split(jax.random.key(seed), 13)
    inputs = noise(splits[0], (IMAGES, SEQ, D), 1.0, 6.0, ((0, 8),))
    lengths = draw_lengths(jax.random.fold_in(splits[12], 71), 0)
    norm_gains = jnp.clip(1.0 + 0.1 * jax.random.normal(splits[2], (2, D), jnp.float32), 0.5, 1.5).astype(jnp.bfloat16)
    norm_shifts = noise(splits[3], (2, D), 0.3, 1.5, ((1, 8),))
    w_qkv = noise(splits[4], (3, D, D), D ** -0.5, 0.1875, ((1, 8), (2, 4)))
    bias_qv = noise(splits[5], (2, D), 0.5, 3.0, ((1, 4),))
    w_out = noise(splits[6], (D, D), (D // 64) ** -0.5, 1.5, ((0, 4), (1, 8)))
    out_bias = noise(splits[7], (2, D), 0.3, 1.5, ((1, 8),))
    w_up = noise(splits[8], (D, FF), D ** -0.5, 0.1875, ((0, 8), (1, 4)))
    b_up = noise(splits[9], (FF,), 0.5, 3.0, ((0, 4),))
    w_down = noise(splits[10], (FF, D), (FF // 16) ** -0.5, 0.375, ((0, 4), (1, 8)))
    cotangent = noise(splits[11], (IMAGES, SEQ, D), 1.0, 6.0, ((0, 8),))
    return dict(inputs=inputs, lengths=lengths, norm_gains=norm_gains, norm_shifts=norm_shifts, w_qkv=w_qkv, bias_qv=bias_qv, w_out=w_out, out_bias=out_bias, w_up=w_up, b_up=b_up, w_down=w_down, cotangent=cotangent)


epsilon = 1e-06
half_root = 0.7071067811865476
density_scale = 0.3989422804014327

def normalize(tokens):
    average = lax.optimization_barrier(jnp.mean(tokens, axis=-1, keepdims=True))
    centred = tokens - average
    spread = lax.optimization_barrier(jnp.mean(centred * centred, axis=-1, keepdims=True))
    inverse = lax.rsqrt(spread + epsilon)
    return (centred * inverse, inverse)

def normalize_back(incoming, normed, inverse, gain):
    scaled = incoming * gain
    return inverse * (scaled - lax.optimization_barrier(jnp.mean(scaled, axis=-1, keepdims=True)) - normed * lax.optimization_barrier(jnp.mean(scaled * normed, axis=-1, keepdims=True)))

def rounded(value):
    return lax.optimization_barrier(value.astype(jnp.bfloat16)).astype(jnp.float32)

def group_sum(left, right):
    count, inner = left.shape
    part_width = inner // N_TENSOR
    pieces = jnp.einsum('sgk,gkd->gsd', left.reshape(count, N_TENSOR, part_width).astype(jnp.float32), right.reshape(N_TENSOR, part_width, right.shape[1]).astype(jnp.float32))
    return lax.optimization_barrier(jnp.sum(rounded(pieces), axis=0))

def qkv_back_sum(stacked, weights):
    count = stacked.shape[1]
    part_width = stacked.shape[2] // N_TENSOR
    pieces = jnp.einsum('csgk,cdgk->gsd', stacked.reshape(3, count, N_TENSOR, part_width).astype(jnp.float32), weights.reshape(3, weights.shape[1], N_TENSOR, part_width).astype(jnp.float32))
    return lax.optimization_barrier(jnp.sum(rounded(pieces), axis=0))

def one_image(image, length, grad_rows, norm_gains, norm_shifts, w_qkv, bias_qv, w_out, out_bias, w_up, b_up, w_down):
    seq_len, width = image.shape
    heads = width // HEAD
    scale = HEAD ** (-0.5)
    gains = norm_gains.astype(jnp.float32)
    shifts = norm_shifts.astype(jnp.float32)
    biases = out_bias.astype(jnp.float32)
    proj_bias = bias_qv.astype(jnp.float32)
    hidden_bias = b_up.astype(jnp.float32)
    flat_in = image.astype(jnp.float32)
    normed_one, inverse_one = normalize(flat_in)
    hidden_one = (normed_one * gains[0] + shifts[0]).astype(jnp.bfloat16)
    queries = rounded(jnp.dot(hidden_one, w_qkv[0], preferred_element_type=jnp.float32) + proj_bias[0])
    key_rows = rounded(jnp.dot(hidden_one, w_qkv[1], preferred_element_type=jnp.float32))
    value_rows = rounded(jnp.dot(hidden_one, w_qkv[2], preferred_element_type=jnp.float32) + proj_bias[1])
    query_heads = queries.reshape(seq_len, heads, HEAD)
    key_heads = key_rows.reshape(seq_len, heads, HEAD)
    value_heads = value_rows.reshape(seq_len, heads, HEAD)
    valid = jnp.arange(seq_len) < length
    scores = jnp.einsum('qhe,khe->hqk', query_heads, key_heads) * scale
    scores = jnp.where(valid[None, None, :], scores, -jnp.inf)
    top = lax.optimization_barrier(jnp.max(scores, axis=-1, keepdims=True))
    log_total = top + jnp.log(lax.optimization_barrier(jnp.sum(jnp.exp(scores - top), axis=-1, keepdims=True)))
    prob = jnp.exp(scores - log_total)
    weights_f = rounded(prob)
    attended_f = rounded(jnp.einsum('hqk,khe->qhe', weights_f, value_heads))
    attended = attended_f.reshape(seq_len, width).astype(jnp.bfloat16)
    middle = flat_in + (group_sum(attended, w_out) + biases[0])
    normed_two, inverse_two = normalize(middle)
    hidden_two = (normed_two * gains[1] + shifts[1]).astype(jnp.bfloat16)
    before = jnp.dot(hidden_two, w_up, preferred_element_type=jnp.float32) + hidden_bias
    activated = jax.nn.gelu(before, approximate=False).astype(jnp.bfloat16)
    result = (middle + (group_sum(activated, w_down) + biases[1])).astype(jnp.bfloat16)
    grad_f = grad_rows.astype(jnp.float32)
    grad_down = jnp.dot(activated.T, grad_rows, preferred_element_type=jnp.float32)
    dact = jnp.dot(grad_rows, w_down.T, preferred_element_type=jnp.float32)
    normal_cdf = 0.5 * (1.0 + jax.scipy.special.erf(before * half_root))
    density = jnp.exp(-0.5 * before * before) * density_scale
    dbefore = dact * (normal_cdf + before * density)
    dbefore_b = dbefore.astype(jnp.bfloat16)
    grad_b_up = lax.optimization_barrier(jnp.sum(dbefore, axis=0))
    grad_up = jnp.dot(hidden_two.T, dbefore_b, preferred_element_type=jnp.float32)
    dhidden_two = group_sum(dbefore_b, w_up.T)
    dmiddle = grad_f + normalize_back(dhidden_two, normed_two, inverse_two, gains[1])
    dmiddle_b = dmiddle.astype(jnp.bfloat16)
    grad_out = jnp.dot(attended.T, dmiddle_b, preferred_element_type=jnp.float32)
    grad_out_bias = jnp.stack([lax.optimization_barrier(jnp.sum(dmiddle, axis=0)), lax.optimization_barrier(jnp.sum(grad_f, axis=0))])
    dattended = rounded(jnp.dot(dmiddle_b, w_out.T, preferred_element_type=jnp.float32))
    dattended_heads = dattended.reshape(seq_len, heads, HEAD)
    dprob = jnp.einsum('qhe,khe->hqk', dattended_heads, value_heads)
    delta = jnp.einsum('qhe,qhe->hq', dattended_heads, attended_f)[:, :, None]
    dscores = rounded(prob * (dprob - delta) * scale)
    dqueries = jnp.einsum('hqk,khe->qhe', dscores, key_heads).reshape(seq_len, width)
    dkeys = jnp.einsum('hqk,qhe->khe', dscores, query_heads).reshape(seq_len, width)
    dvalues = jnp.einsum('hqk,qhe->khe', weights_f, dattended_heads).reshape(seq_len, width)
    grad_bias_qv = jnp.stack([lax.optimization_barrier(jnp.sum(dqueries, axis=0)), lax.optimization_barrier(jnp.sum(dvalues, axis=0))])
    stacked = jnp.stack([dqueries, dkeys, dvalues]).astype(jnp.bfloat16)
    grad_qkv = jnp.stack([jnp.dot(hidden_one.T, stacked[0], preferred_element_type=jnp.float32), jnp.dot(hidden_one.T, stacked[1], preferred_element_type=jnp.float32), jnp.dot(hidden_one.T, stacked[2], preferred_element_type=jnp.float32)])
    dhidden_one = qkv_back_sum(stacked, w_qkv)
    grad_input = dmiddle + normalize_back(dhidden_one, normed_one, inverse_one, gains[0])
    grad_gains = jnp.stack([lax.optimization_barrier(jnp.sum(dhidden_one * normed_one, axis=0)), lax.optimization_barrier(jnp.sum(dhidden_two * normed_two, axis=0))])
    grad_shifts = jnp.stack([lax.optimization_barrier(jnp.sum(dhidden_one, axis=0)), lax.optimization_barrier(jnp.sum(dhidden_two, axis=0))])
    grads = (grad_gains, grad_shifts, grad_qkv, grad_bias_qv, grad_out, grad_out_bias, grad_up, grad_b_up, grad_down)
    return (result, grad_input, grads)

def reference(inputs, lengths, norm_gains, norm_shifts, w_qkv, bias_qv, w_out, out_bias, w_up, b_up, w_down, cotangent):
    width = inputs.shape[2]
    hidden_width = w_up.shape[1]
    start = (jnp.zeros((2, width), jnp.float32), jnp.zeros((2, width), jnp.float32), jnp.zeros((3, width, width), jnp.float32), jnp.zeros((2, width), jnp.float32), jnp.zeros((width, width), jnp.float32), jnp.zeros((2, width), jnp.float32), jnp.zeros((width, hidden_width), jnp.float32), jnp.zeros((hidden_width,), jnp.float32), jnp.zeros((hidden_width, width), jnp.float32))

    def advance(carry, item):
        image, length, grad_rows = item
        result, grad_input, grads = one_image(image, length, grad_rows, norm_gains, norm_shifts, w_qkv, bias_qv, w_out, out_bias, w_up, b_up, w_down)
        return (jax.tree.map(lambda left, right: left + right, carry, grads), (result, grad_input))
    totals, (outputs, grad_inputs) = lax.scan(advance, start, (inputs, lengths, cotangent))
    return (outputs, grad_inputs, totals[0], totals[1], totals[2], totals[3], totals[4], totals[5], totals[6], totals[7], totals[8])
```

```python
import functools

import jax
import jax.numpy as jnp
from jax import lax
from jax.experimental import pallas as pl
from jax.experimental.pallas import tpu as pltpu
from jax.sharding import PartitionSpec as P

HEAD = 64
GROUPS = 8
epsilon = 1e-06
half_root = 0.7071067811865476
density_scale = 0.3989422804014327
MESH = pl.DeviceIdType.MESH
bf16 = jnp.bfloat16
f32 = jnp.float32
VMEM_LIMIT = 66_500_000


def aligned(value, multiple):
    return pl.multiple_of(value, multiple)


class Place:
    def __init__(self, ratio, length):
        f = lax.axis_index("fsdp")
        self.t = lax.axis_index("tensor")
        self.length = length
        self.ratio = ratio
        self.r = lax.rem(f, ratio)
        g = lax.div(f, ratio)
        self.g = g
        self.core = lax.rem(g, 2)
        self.x = lax.rem(lax.div(g, 2), 2)
        self.y = lax.div(g, 4)
        self.gs = self.sib(g)
        self.gx = g + 2 - 4 * self.x
        self.gy = g + 4 - 8 * self.y
        self.gd = self.gx + 4 - 8 * self.y

    def sib(self, g):
        return g + 1 - 2 * self.core

    def dev(self, g, t):
        return (g * self.ratio + self.r, t)

    def order(self, i):
        half = self.length // 2
        step = 1 - 2 * lax.div(self.t, half)
        return lax.rem(self.t + i * step + self.length, self.length)


def remote(src, dst, send, recv, dev):
    return pltpu.make_async_remote_copy(
        src_ref=src, dst_ref=dst, send_sem=send, recv_sem=recv, device_id=dev, device_id_type=MESH
    )


def enter(place, partners):
    barrier = pltpu.get_barrier_semaphore()
    count = 0
    for cond, dev in partners:
        if cond is None:
            pl.semaphore_signal(barrier, inc=1, device_id=dev, device_id_type=MESH)
            count = count + 1
        else:

            @pl.when(cond)
            def _(dev=dev):
                pl.semaphore_signal(barrier, inc=1, device_id=dev, device_id_type=MESH)

            count = count + jnp.where(cond, 1, 0)
    pl.semaphore_wait(barrier, count)


def neighbours(place):
    g, t = place.g, place.t
    return [
        (None, place.dev(place.gs, t)),
        (None, place.dev(place.gx, t)),
        (None, place.dev(place.gy, t)),
        (t < place.length - 1, place.dev(g, t + 1)),
        (t > 0, place.dev(g, t - 1)),
    ]


def piece(kind, ref, g, t, n, half=None):
    size = n if half is None else n // 2
    off = 0 if half in (None, 0) else n // 2
    if kind == "q":
        return ref.at[:, t, pl.ds(aligned(g * n + off, size), size), :]
    if kind == "u":
        return ref.at[t, pl.ds(aligned(g * n + off, size), size), :]
    if kind in ("o", "d"):
        return ref.at[g, pl.ds(aligned(t * n + off, size), size), :]
    return ref.at[g, t, pl.ds(off, size), :]


class Gather:
    def __init__(self, place, index, kind, shard, full, n, sems):
        self.p, self.a, self.kind, self.shard, self.full, self.n = place, index, kind, shard, full, n
        self.s_z, self.s_xy, self.s_sib, self.r_z, self.r_xy, self.r_sib, self.loc = sems

    def view(self, g, o, half=None):
        return piece(self.kind, self.full, g, o, self.n, half)

    def put(self, src, g, o, half, send, recv, dev):
        return remote(src, self.view(g, o, half), send, recv, dev)

    def c_up(self, src, o):
        p = self.p
        return self.put(src, p.g, o, None, self.s_z.at[self.a, 0, o], self.r_z.at[self.a, o], p.dev(p.g, p.t + 1))

    def c_down(self, src, o):
        p = self.p
        return self.put(src, p.g, o, None, self.s_z.at[self.a, 1, o], self.r_z.at[self.a, o], p.dev(p.g, p.t - 1))

    def c_xy(self, src, which, o):
        p = self.p
        g = (p.g, p.g, p.gx, p.gy)[which]
        half = (None, None, 0, 1)[which]
        to = (p.gx, p.gy, p.gy, p.gx)[which]
        return self.put(src, g, o, half, self.s_xy.at[self.a, which, o], self.r_xy.at[self.a, which, o], p.dev(to, p.t))

    def c_sib(self, src, which, o):
        p = self.p
        g = (p.g, p.gx, p.gy, p.gd, p.gd)[which]
        half = (None, None, None, 0, 1)[which]
        return self.put(src, g, o, half, self.s_sib.at[self.a, which, o], self.r_sib.at[self.a, which, o], p.dev(p.gs, p.t))

    def own(self):
        p = self.p
        src, t = self.shard, p.t
        pltpu.make_async_copy(src, self.view(p.g, t), self.loc.at[self.a]).start()

        @pl.when(t < p.length - 1)
        def _():
            self.c_up(src, t).start()

        @pl.when(t > 0)
        def _():
            self.c_down(src, t).start()

        self.c_xy(src, 0, t).start()
        self.c_xy(src, 1, t).start()
        self.c_sib(src, 0, t).start()

    def spread(self, o):
        src = self.view(self.p.g, o)
        self.c_xy(src, 0, o).start()
        self.c_xy(src, 1, o).start()
        self.c_sib(src, 0, o).start()

    def z(self, d):
        p = self.p
        t, last = p.t, p.length - 1

        @pl.when(t - d >= 0)
        def _():
            o = t - d
            src = self.view(p.g, o)
            self.c_up(src, o).wait_recv()

            @pl.when(t < last)
            def _():
                self.c_up(src, o).start()

            self.spread(o)

        @pl.when(t + d <= last)
        def _():
            o = t + d
            src = self.view(p.g, o)
            self.c_down(src, o).wait_recv()

            @pl.when(t > 0)
            def _():
                self.c_down(src, o).start()

            self.spread(o)

    def side(self, which, i):
        p = self.p
        o = p.order(i)
        g = (p.gx, p.gy)[which]
        full = self.view(g, o)
        self.wait_xy(which, g, o, None)
        self.c_xy(self.view(g, o, which), 2 + which, o).start()
        self.c_sib(full, 1 + which, o).start()

    def wait_xy(self, which, g, o, half):
        v = self.view(g, o, half)
        p = self.p
        remote(v, v, self.s_xy.at[self.a, which, o], self.r_xy.at[self.a, which, o], p.dev(p.gx, p.t)).wait_recv()

    def diag(self, which, i):
        p = self.p
        o = p.order(i)
        self.wait_xy(2 + which, p.gd, o, which)
        self.c_sib(self.view(p.gd, o, which), 3 + which, o).start()

    def finish(self):
        p = self.p

        @pl.loop(0, p.length)
        def _(o):
            for which in range(5):
                g = p.sib((p.g, p.gx, p.gy, p.gd, p.gd)[which])
                half = (None, None, None, 0, 1)[which]
                v = self.view(g, o, half)
                remote(v, v, self.s_sib.at[self.a, which, o], self.r_sib.at[self.a, which, o], p.dev(p.gs, p.t)).wait_recv()

        pltpu.make_async_copy(self.shard, self.view(p.g, p.t), self.loc.at[self.a]).wait()

    def drain(self):
        p = self.p

        @pl.loop(0, p.length)
        def _(o):
            src = self.view(p.g, o)

            @pl.when(jnp.logical_and(o <= p.t, p.t < p.length - 1))
            def _():
                self.c_up(src, o).wait_send()

            @pl.when(jnp.logical_and(o >= p.t, p.t > 0))
            def _():
                self.c_down(src, o).wait_send()

            self.c_xy(src, 0, o).wait_send()
            self.c_xy(src, 1, o).wait_send()
            self.c_xy(self.view(p.gx, o, 0), 2, o).wait_send()
            self.c_xy(self.view(p.gy, o, 1), 3, o).wait_send()
            for which in range(5):
                g = (p.g, p.gx, p.gy, p.gd, p.gd)[which]
                half = (None, None, None, 0, 1)[which]
                self.c_sib(self.view(g, o, half), which, o).wait_send()

    def middle(self):
        for d in range(1, self.p.length):
            yield self.z(d)
        for i in range(self.p.length):
            yield self.side(0, i)
            yield self.side(1, i)
        for i in range(self.p.length):
            yield self.diag(0, i)
            yield self.diag(1, i)


def gather_sems(arrays, length):
    dma = pltpu.SemaphoreType.DMA
    return [
        dma((arrays, 2, length)),
        dma((arrays, 4, length)),
        dma((arrays, 5, length)),
        dma((arrays, length)),
        dma((arrays, 4, length)),
        dma((arrays, 5, length)),
        dma((arrays,)),
    ]


def step(gen, count=1):
    for _ in range(count):
        next(gen, None)


def chain(*gens):
    for g in gens:
        yield from g


def statistics(tokens):
    average = jnp.mean(tokens, axis=-1, keepdims=True)
    centred = tokens - average
    inverse = lax.rsqrt(jnp.mean(centred * centred, axis=-1, keepdims=True) + epsilon)
    return centred * inverse, inverse


def nt(a, b):
    return lax.dot_general(a, b, (((1,), (1,)), ((), ())), preferred_element_type=f32)


def tn(a, b):
    return lax.dot_general(a, b, (((0,), (0,)), ((), ())), preferred_element_type=f32)


def nn(a, b):
    return jnp.dot(a, b, preferred_element_type=f32)


def wide(ref, lead, rows=slice(None)):
    return jnp.concatenate([ref[i, rows, :] for i in lead], axis=1)


def store_out(copies, src, dst, sem):
    c = pltpu.make_async_copy(src, dst, sem)
    c.start()
    copies.append(c)


def forward_kernel(ratio, length, x, mask, s_s, q_s, o_s, u_s, d_s,
                   vec_o, wq_o, wo_o, wu_o, wd_o, hid1_o, qkv_o, att_o, lse_o, mid_o, hid2_o, act_o, g_o, out_o,
                   ws, wq, wo, wu, wd, smf, vec, hid1, qkv, att, lse, mid, hid2, act, gg, pre, outb,
                   s_z, s_xy, s_sib, r_z, r_xy, r_sib, loc, outs):
    place = Place(ratio, length)
    rows, width = hid1.shape
    keys = qkv.shape[1]
    hidden = act.shape[1]
    nb = rows // 16
    sems = (s_z, s_xy, s_sib, r_z, r_xy, r_sib, loc)
    small = Gather(place, 0, "s", s_s, ws, s_s.shape[0], sems)
    gq = Gather(place, 1, "q", q_s, wq, q_s.shape[1], sems)
    go = Gather(place, 2, "o", o_s, wo, o_s.shape[0], sems)
    gu = Gather(place, 3, "u", u_s, wu, u_s.shape[0], sems)
    gd = Gather(place, 4, "d", d_s, wd, d_s.shape[0], sems)
    everything = (small, gq, go, gu, gd)
    enter(place, neighbours(place))
    small.own()
    gq.own()
    go.own()
    for _ in small.middle():
        pass
    gu.own()
    first = gq.middle()
    step(first, 3)
    small.finish()
    copies = []

    for g in range(GROUPS):
        for t in range(length):
            smf[g, t] = ws[g, t].astype(f32)
    per = width // GROUPS
    for row in range(6):
        vec[row : row + 1, 0:width] = jnp.concatenate([smf[g, 0, row : row + 1, :] for g in range(GROUPS)], axis=1)
    local = width // length
    for c in range(2):
        parts = []
        for t in range(length):
            for j in range(local // 128):
                r = 6 + c * (local // 128) + j
                parts.append(smf[0, t, r : r + 1, :])
        vec[6 + c : 7 + c, 0:width] = jnp.concatenate(parts, axis=1)
    base = 6 + 2 * (local // 128)
    nh = hidden // length // 128
    for t in range(length):
        vec[8 : 9, t * (hidden // length) : (t + 1) * (hidden // length)] = jnp.concatenate(
            [smf[0, t, base + j : base + j + 1, :] for j in range(nh)], axis=1
        )
    store_out(copies, vec, vec_o, outs.at[13])

    gain, shift = vec[0:1, 0:width], vec[2:3, 0:width]

    @pl.loop(0, nb)
    def _(i):
        r = pl.ds(aligned(i * 16, 16), 16)
        n, _inv = statistics(x[r, :].astype(f32))
        hid1[r, :] = (n * gain + shift).astype(bf16)

    store_out(copies, hid1, hid1_o, outs.at[0])
    qkv[:, rows:keys, :] = jnp.zeros((3, keys - rows, width), bf16)
    for _ in first:
        pass
    second = chain(go.middle(), gu.middle(), gd.middle())
    step(second, 3)
    gq.finish()
    store_out(copies, wq, wq_o, outs.at[1])
    step(second, 8)
    gd.own()

    scale = HEAD ** (-0.5)
    for c in range(3):
        r = nn(hid1[...], wide(wq.at[c], range(length)))
        if c == 0:
            r = (r + vec[6:7, 0:width]).astype(bf16) * jnp.asarray(scale, bf16)
        elif c == 2:
            r = (r + vec[7:8, 0:width]).astype(bf16)
        else:
            r = r.astype(bf16)
        qkv[c, 0:rows, :] = r
        step(second, 3)
    store_out(copies, qkv, qkv_o, outs.at[2])

    pairs = width // 128
    low = lax.broadcasted_iota(jnp.int32, (128, 128), 1) < HEAD

    def attend(p):
        cols = pl.ds(aligned(p * 128, 128), 128)
        k2 = qkv[1, :, cols]
        v2 = qkv[2, :, cols]
        for r0 in range(0, keys, 128):
            n = min(128, rows - r0)
            q2 = qkv[0, r0 : r0 + 128, cols]
            done = []
            for h in range(2):
                mine = low if h == 0 else jnp.logical_not(low)
                s = nt(jnp.where(mine, q2, jnp.zeros_like(q2)), k2) + mask[...]
                m = jnp.max(s, axis=-1, keepdims=True)
                e = jnp.exp(s - m)
                total = jnp.sum(e, axis=-1, keepdims=True)
                done.append(nn(e.astype(bf16), v2) * (1.0 / total))
                flat = jnp.transpose(jnp.broadcast_to(m + jnp.log(total), (128, 128)))
                lse[p, h : h + 1, r0 : r0 + 128] = flat[0:1, :]
            a2 = jnp.where(low, done[0], done[1]).astype(bf16)
            att[r0 : r0 + n, cols] = a2[0:n, :]

    for part in range(4):

        @pl.loop(0, pairs // 4)
        def _(j):
            attend(part * (pairs // 4) + j)

        step(second, 6)
    store_out(copies, att, att_o, outs.at[3])
    store_out(copies, lse, lse_o, outs.at[4])
    go.finish()
    store_out(copies, wo, wo_o, outs.at[5])
    step(second, 2)

    mid[...] = nn(att[...], wide(wo, range(GROUPS))) + vec[4:5, 0:width]
    step(second, 2)
    gain2, shift2 = vec[1:2, 0:width], vec[3:4, 0:width]

    @pl.loop(0, nb)
    def _(i):
        r = pl.ds(aligned(i * 16, 16), 16)
        m = x[r, :].astype(f32) + mid[r, :]
        mid[r, :] = m
        n, _inv = statistics(m)
        hid2[r, :] = (n * gain2 + shift2).astype(bf16)

    store_out(copies, mid, mid_o, outs.at[6])
    store_out(copies, hid2, hid2_o, outs.at[7])
    left = length * 4 + length - 1
    for _ in range(200):
        step(second)
    gu.finish()
    store_out(copies, wu, wu_o, outs.at[8])

    part = pre.shape[1]
    for t in range(hidden // part):
        cols = slice(t * part, (t + 1) * part)
        each = wu.shape[2]
        blk, off = (t * part) // each, (t * part) % each
        pre[...] = nn(hid2[...], wu[blk, :, off : off + part])

        @pl.loop(0, nb)
        def _(i):
            r = pl.ds(aligned(i * 16, 16), 16)
            z = pre[r, :] + vec[8:9, cols]
            cdf = 0.5 * (1.0 + lax.erf(z * half_root))
            act[r, cols] = (z * cdf).astype(bf16)
            gg[r, cols] = (cdf + z * (jnp.exp(-0.5 * z * z) * density_scale)).astype(bf16)

    store_out(copies, act, act_o, outs.at[9])
    store_out(copies, gg, g_o, outs.at[10])
    gd.finish()
    store_out(copies, wd, wd_o, outs.at[11])

    for j in range(GROUPS // 2):
        cols = slice(2 * j * per, 2 * (j + 1) * per)
        r = nn(act[...], wide(wd, (2 * j, 2 * j + 1)))
        outb[:, cols] = (mid[:, cols] + (r + vec[5:6, cols])).astype(bf16)
    store_out(copies, outb, out_o, outs.at[12])
    for a in everything:
        a.drain()
    for c in copies:
        c.wait()


def any_spec():
    return pl.BlockSpec(memory_space=pl.ANY)


def vmem_spec():
    return pl.BlockSpec(memory_space=pltpu.VMEM)


def forward(ratio, length, x, mask, small, q_s, o_s, u_s, d_s):
    rows, width = x.shape
    keys = mask.shape[1]
    hidden = u_s.shape[1] * length
    sds = jax.ShapeDtypeStruct
    n_q, n_o, n_u, n_d = q_s.shape[1], o_s.shape[0], u_s.shape[0], d_s.shape[0]
    wq = ((3, length, GROUPS * n_q, q_s.shape[2]), bf16)
    wo = ((GROUPS, length * n_o, o_s.shape[1]), bf16)
    wu = ((length, GROUPS * n_u, u_s.shape[1]), bf16)
    wd = ((GROUPS, length * n_d, d_s.shape[1]), bf16)
    pairs = width // 128
    vec = ((16, hidden), f32)
    hid = ((rows, width), bf16)
    qkv = ((3, keys, width), bf16)
    lse = ((pairs, 8, keys), f32)
    mid = ((rows, width), f32)
    act = ((rows, hidden), bf16)
    outs = [vec, wq, wo, wu, wd, hid, qkv, hid, lse, mid, hid, act, act, hid]
    scratch = [((GROUPS, length) + small.shape, bf16), wq, wo, wu, wd, ((GROUPS, length) + small.shape, f32), vec,
               hid, qkv, hid, lse, mid, hid, act, act, ((rows, 512), f32), hid]
    return pl.pallas_call(
        functools.partial(forward_kernel, ratio, length),
        out_shape=[sds(*o) for o in outs],
        in_specs=[vmem_spec(), vmem_spec()] + [any_spec()] * 5,
        out_specs=[any_spec()] * len(outs),
        scratch_shapes=[pltpu.VMEM(*s) for s in scratch] + gather_sems(5, length) + [pltpu.SemaphoreType.DMA((14,))],
        compiler_params=pltpu.CompilerParams(collective_id=0, has_side_effects=True, vmem_limit_bytes=VMEM_LIMIT),
        name="forward",
    )(x, mask, small, q_s, o_s, u_s, d_s)


def prepare(length, inputs, lengths, norm_gains, norm_shifts, w_qkv, bias_qv, w_out, out_bias, w_up, b_up, w_down, cotangent, fsdp):
    ratio = fsdp // GROUPS
    if ratio > 1:
        groups = [[g * ratio + r for r in range(ratio)] for g in range(GROUPS)]

        def join(a, axis):
            return lax.all_gather(a, "fsdp", axis=axis, tiled=True, axis_index_groups=groups)

        norm_gains, norm_shifts, out_bias = join(norm_gains, 1), join(norm_shifts, 1), join(out_bias, 1)
        w_qkv, w_out, w_up, w_down = join(w_qkv, 1), join(w_out, 1), join(w_up, 0), join(w_down, 1)
    t = lax.axis_index("tensor")
    batch, seq, width = inputs.shape
    rows = -(-seq // 16) * 16
    keys = -(-seq // 128) * 128

    def mine(a):
        a = lax.dynamic_index_in_dim(a, t, 0, keepdims=False)
        return jnp.pad(a, ((0, rows - seq), (0, 0)))

    count = lax.dynamic_index_in_dim(lengths, t, 0, keepdims=False)
    mask = jnp.where(jnp.arange(keys) < count, 0.0, -jnp.inf).astype(f32)
    small = jnp.concatenate(
        [norm_gains, norm_shifts, out_bias, bias_qv.reshape(-1, 128), b_up.reshape(-1, 128)], axis=0
    )
    small = jnp.pad(small, ((0, 32 - small.shape[0]), (0, 0)))
    return ratio, mine(inputs), mine(cotangent), mask, small, w_qkv, w_out, w_up, w_down


def normalize(tokens):
    average = jnp.mean(tokens, axis=-1, keepdims=True)
    centred = tokens - average
    spread = jnp.mean(centred * centred, axis=-1, keepdims=True)
    inverse = lax.rsqrt(spread + epsilon)
    return (centred * inverse, inverse)


def normalize_back(incoming, normed, inverse, gain):
    scaled = incoming * gain
    return inverse * (
        scaled
        - jnp.mean(scaled, axis=-1, keepdims=True)
        - normed * jnp.mean(scaled * normed, axis=-1, keepdims=True)
    )


def masked_scores(query_heads, key_heads, valid, scale):
    scores = (
        jnp.einsum("bqhe,bkhe->bhqk", query_heads, key_heads, preferred_element_type=jnp.float32)
        * scale
    )
    return jnp.where(valid[:, None, None, :], scores, -jnp.inf)


def local(
    inputs,
    lengths,
    norm_gains,
    norm_shifts,
    w_qkv,
    bias_qv,
    w_out,
    out_bias,
    w_up,
    b_up,
    w_down,
    cotangent,
):
    batch, seq_len, width = inputs.shape
    tokens = batch * seq_len
    local_width = w_qkv.shape[2]
    local_heads = local_width // HEAD
    scale = HEAD ** (-0.5)
    gathered = (
        lax.all_gather(w_qkv, "fsdp", axis=1, tiled=True),
        lax.all_gather(w_out, "fsdp", axis=1, tiled=True),
        lax.all_gather(w_up, "fsdp", axis=0, tiled=True),
        lax.all_gather(w_down, "fsdp", axis=1, tiled=True),
        lax.all_gather(norm_gains, "fsdp", axis=1, tiled=True),
        lax.all_gather(norm_shifts, "fsdp", axis=1, tiled=True),
        lax.all_gather(out_bias, "fsdp", axis=1, tiled=True),
    )
    full_qkv, full_out, full_up, full_down, all_gains, all_shifts, all_bias = gathered
    gain_rows = all_gains.astype(jnp.float32)
    shift_rows = all_shifts.astype(jnp.float32)
    bias_rows = all_bias.astype(jnp.float32)
    proj_bias = bias_qv.astype(jnp.float32)
    hidden_bias = b_up.astype(jnp.float32)
    flat_in = inputs.reshape(tokens, width).astype(jnp.float32)
    normed_one, inverse_one = normalize(flat_in)
    hidden_one = (normed_one * gain_rows[0] + shift_rows[0]).astype(jnp.bfloat16)
    projected = jnp.einsum("rd,cde->cre", hidden_one, full_qkv, preferred_element_type=jnp.float32)
    queries = (projected[0] + proj_bias[0]).astype(jnp.bfloat16)
    key_rows = projected[1].astype(jnp.bfloat16)
    value_rows = (projected[2] + proj_bias[1]).astype(jnp.bfloat16)
    head_shape = (batch, seq_len, local_heads, HEAD)
    query_heads = queries.reshape(head_shape)
    key_heads = key_rows.reshape(head_shape)
    value_heads = value_rows.reshape(head_shape)
    valid = lax.broadcasted_iota(jnp.int32, (batch, seq_len), 1) < lengths[:, None]
    scores = masked_scores(query_heads, key_heads, valid, scale)
    top = jnp.max(scores, axis=-1, keepdims=True)
    log_total = top + jnp.log(jnp.sum(jnp.exp(scores - top), axis=-1, keepdims=True))
    weights_b = jnp.exp(scores - log_total).astype(jnp.bfloat16)
    attended_heads = jnp.einsum(
        "bhqk,bkhe->bqhe", weights_b, value_heads, preferred_element_type=jnp.float32
    ).astype(jnp.bfloat16)
    attended = attended_heads.reshape(tokens, local_width)
    attn_total = lax.psum(
        jnp.dot(attended, full_out, preferred_element_type=jnp.float32).astype(jnp.bfloat16),
        "tensor",
    ).astype(jnp.float32)
    middle = flat_in + (attn_total + bias_rows[0])
    normed_two, inverse_two = normalize(middle)
    hidden_two = (normed_two * gain_rows[1] + shift_rows[1]).astype(jnp.bfloat16)
    before = jnp.dot(hidden_two, full_up, preferred_element_type=jnp.float32) + hidden_bias
    activated = jax.nn.gelu(before, approximate=False).astype(jnp.bfloat16)
    mlp_total = lax.psum(
        jnp.dot(activated, full_down, preferred_element_type=jnp.float32).astype(jnp.bfloat16),
        "tensor",
    ).astype(jnp.float32)
    ratio, x_own, _ct, mask, small, q_s, o_s, u_s, d_s = prepare(
        w_qkv.shape[2] and lax.axis_size("tensor"), inputs, lengths, norm_gains, norm_shifts, w_qkv, bias_qv, w_out, out_bias,
        w_up, b_up, w_down, cotangent, lax.axis_size("fsdp"))
    own = forward(ratio, lax.axis_size("tensor"), x_own, mask[None, :], small, q_s, o_s, u_s, d_s)[-1]
    result = lax.all_gather(own[:seq_len], "tensor", axis=0)
    back_qkv, back_out, back_up, back_down = (full_qkv, full_out, full_up, full_down)
    grad_rows = cotangent.reshape(tokens, width)
    grad_f = grad_rows.astype(jnp.float32)
    grad_down = jnp.einsum("rf,rd->fd", activated, grad_rows, preferred_element_type=jnp.float32)
    dact = jnp.einsum("rd,fd->rf", grad_rows, back_down, preferred_element_type=jnp.float32)
    normal_cdf = 0.5 * (1.0 + jax.scipy.special.erf(before * half_root))
    density = jnp.exp(-0.5 * before * before) * density_scale
    dbefore = dact * (normal_cdf + before * density)
    dbefore_b = dbefore.astype(jnp.bfloat16)
    grad_b_up = jnp.sum(dbefore, axis=0)
    grad_up = jnp.einsum("rd,rf->df", hidden_two, dbefore_b, preferred_element_type=jnp.float32)
    dhidden_two = lax.psum(
        jnp.einsum("rf,df->rd", dbefore_b, back_up, preferred_element_type=jnp.float32).astype(
            jnp.bfloat16
        ),
        "tensor",
    ).astype(jnp.float32)
    dmiddle = grad_f + normalize_back(dhidden_two, normed_two, inverse_two, gain_rows[1])
    dmiddle_b = dmiddle.astype(jnp.bfloat16)
    grad_out = jnp.einsum("rk,rd->kd", attended, dmiddle_b, preferred_element_type=jnp.float32)
    grad_out_bias = jnp.stack([jnp.sum(dmiddle, axis=0), jnp.sum(grad_f, axis=0)])
    dattended = jnp.einsum(
        "rd,kd->rk", dmiddle_b, back_out, preferred_element_type=jnp.float32
    ).astype(jnp.bfloat16)
    dattended_heads = dattended.reshape(head_shape)
    again_scores = masked_scores(query_heads, key_heads, valid, scale)
    prob = jnp.exp(again_scores - log_total)
    again_weights = prob.astype(jnp.bfloat16)
    dprob = jnp.einsum(
        "bqhe,bkhe->bhqk", dattended_heads, value_heads, preferred_element_type=jnp.float32
    )
    delta = jnp.einsum(
        "bqhe,bqhe->bhq", dattended_heads, attended_heads, preferred_element_type=jnp.float32
    )[..., None]
    dscores = (prob * (dprob - delta) * scale).astype(jnp.bfloat16)
    dqueries = jnp.einsum(
        "bhqk,bkhe->bqhe", dscores, key_heads, preferred_element_type=jnp.float32
    ).reshape(tokens, local_width)
    dkeys = jnp.einsum(
        "bhqk,bqhe->bkhe", dscores, query_heads, preferred_element_type=jnp.float32
    ).reshape(tokens, local_width)
    dvalues = jnp.einsum(
        "bhqk,bqhe->bkhe", again_weights, dattended_heads, preferred_element_type=jnp.float32
    ).reshape(tokens, local_width)
    grad_bias_part = jnp.stack([jnp.sum(dqueries, axis=0), jnp.sum(dvalues, axis=0)])
    stacked = jnp.stack([dqueries, dkeys, dvalues]).astype(jnp.bfloat16)
    grad_qkv = jnp.einsum("rd,cre->cde", hidden_one, stacked, preferred_element_type=jnp.float32)
    dhidden_one = lax.psum(
        jnp.einsum("cre,cde->rd", stacked, back_qkv, preferred_element_type=jnp.float32).astype(
            jnp.bfloat16
        ),
        "tensor",
    ).astype(jnp.float32)
    grad_input = dmiddle + normalize_back(dhidden_one, normed_one, inverse_one, gain_rows[0])
    grad_gains = jnp.stack(
        [jnp.sum(dhidden_one * normed_one, axis=0), jnp.sum(dhidden_two * normed_two, axis=0)]
    )
    grad_shifts = jnp.stack([jnp.sum(dhidden_one, axis=0), jnp.sum(dhidden_two, axis=0)])
    owned_qkv, owned_out, owned_up, owned_down, owned_gains, owned_shifts, owned_bias = (
        lax.psum_scatter(
            grad_qkv.astype(jnp.bfloat16), "fsdp", scatter_dimension=1, tiled=True
        ).astype(jnp.float32),
        lax.psum_scatter(
            grad_out.astype(jnp.bfloat16), "fsdp", scatter_dimension=1, tiled=True
        ).astype(jnp.float32),
        lax.psum_scatter(
            grad_up.astype(jnp.bfloat16), "fsdp", scatter_dimension=0, tiled=True
        ).astype(jnp.float32),
        lax.psum_scatter(
            grad_down.astype(jnp.bfloat16), "fsdp", scatter_dimension=1, tiled=True
        ).astype(jnp.float32),
        lax.psum_scatter(
            grad_gains.astype(jnp.bfloat16), "fsdp", scatter_dimension=1, tiled=True
        ).astype(jnp.float32),
        lax.psum_scatter(
            grad_shifts.astype(jnp.bfloat16), "fsdp", scatter_dimension=1, tiled=True
        ).astype(jnp.float32),
        lax.psum_scatter(
            grad_out_bias.astype(jnp.bfloat16), "fsdp", scatter_dimension=1, tiled=True
        ).astype(jnp.float32),
    )
    summed_bias_qv, summed_b_up = lax.psum((grad_bias_part, grad_b_up), "fsdp")
    return (
        result.reshape(batch, seq_len, width),
        grad_input.reshape(batch, seq_len, width),
        owned_gains,
        owned_shifts,
        owned_qkv,
        summed_bias_qv,
        owned_out,
        owned_bias,
        owned_up,
        summed_b_up,
        owned_down,
    )


def solution(mesh):
    placed = (
        P("fsdp", None, None),
        P("fsdp"),
        P(None, "fsdp"),
        P(None, "fsdp"),
        P(None, "fsdp", "tensor"),
        P(None, "tensor"),
        P("tensor", "fsdp"),
        P(None, "fsdp"),
        P("fsdp", "tensor"),
        P("tensor"),
        P("tensor", "fsdp"),
        P("fsdp", None, None),
    )
    return jax.shard_map(
        local,
        mesh=mesh,
        in_specs=placed,
        out_specs=(
            P("fsdp", None, None),
            P("fsdp", None, None),
            P(None, "fsdp"),
            P(None, "fsdp"),
            P(None, "fsdp", "tensor"),
            P(None, "tensor"),
            P("tensor", "fsdp"),
            P(None, "fsdp"),
            P("fsdp", "tensor"),
            P("tensor"),
            P("tensor", "fsdp"),
        ),
        check_vma=False,
    )
```

```python
import functools

import jax
import jax.numpy as jnp
from jax import lax
from jax.experimental import pallas as pl
from jax.experimental.pallas import tpu as pltpu
from jax.sharding import PartitionSpec as P

HEAD = 64
GROUPS = 8
epsilon = 1e-06
half_root = 0.7071067811865476
density_scale = 0.3989422804014327
MESH = pl.DeviceIdType.MESH
bf16 = jnp.bfloat16
f32 = jnp.float32
VMEM_LIMIT = 66_500_000


def aligned(value, multiple):
    return pl.multiple_of(value, multiple)


class Place:
    def __init__(self, ratio, length):
        f = lax.axis_index("fsdp")
        self.t = lax.axis_index("tensor")
        self.length = length
        self.ratio = ratio
        self.r = lax.rem(f, ratio)
        g = lax.div(f, ratio)
        self.g = g
        self.core = lax.rem(g, 2)
        self.x = lax.rem(lax.div(g, 2), 2)
        self.y = lax.div(g, 4)
        self.gs = self.sib(g)
        self.gx = g + 2 - 4 * self.x
        self.gy = g + 4 - 8 * self.y
        self.gd = self.gx + 4 - 8 * self.y

    def sib(self, g):
        return g + 1 - 2 * self.core

    def dev(self, g, t):
        return (g * self.ratio + self.r, t)

    def order(self, i):
        half = self.length // 2
        step = 1 - 2 * lax.div(self.t, half)
        return lax.rem(self.t + i * step + self.length, self.length)


def remote(src, dst, send, recv, dev):
    return pltpu.make_async_remote_copy(
        src_ref=src, dst_ref=dst, send_sem=send, recv_sem=recv, device_id=dev, device_id_type=MESH
    )


def enter(place, partners):
    barrier = pltpu.get_barrier_semaphore()
    count = 0
    for cond, dev in partners:
        if cond is None:
            pl.semaphore_signal(barrier, inc=1, device_id=dev, device_id_type=MESH)
            count = count + 1
        else:

            @pl.when(cond)
            def _(dev=dev):
                pl.semaphore_signal(barrier, inc=1, device_id=dev, device_id_type=MESH)

            count = count + jnp.where(cond, 1, 0)
    pl.semaphore_wait(barrier, count)


def neighbours(place):
    g, t = place.g, place.t
    return [
        (None, place.dev(place.gs, t)),
        (None, place.dev(place.gx, t)),
        (None, place.dev(place.gy, t)),
        (t < place.length - 1, place.dev(g, t + 1)),
        (t > 0, place.dev(g, t - 1)),
    ]


def piece(kind, ref, g, t, n, half=None):
    size = n if half is None else n // 2
    off = 0 if half in (None, 0) else n // 2
    if kind == "q":
        return ref.at[:, t, pl.ds(aligned(g * n + off, size), size), :]
    if kind == "u":
        return ref.at[t, pl.ds(aligned(g * n + off, size), size), :]
    if kind in ("o", "d"):
        return ref.at[g, pl.ds(aligned(t * n + off, size), size), :]
    return ref.at[g, t, pl.ds(off, size), :]


class Gather:
    def __init__(self, place, index, kind, shard, full, n, sems):
        self.p, self.a, self.kind, self.shard, self.full, self.n = place, index, kind, shard, full, n
        self.s_z, self.s_xy, self.s_sib, self.r_z, self.r_xy, self.r_sib, self.loc = sems

    def view(self, g, o, half=None):
        return piece(self.kind, self.full, g, o, self.n, half)

    def put(self, src, g, o, half, send, recv, dev):
        return remote(src, self.view(g, o, half), send, recv, dev)

    def c_up(self, src, o):
        p = self.p
        return self.put(src, p.g, o, None, self.s_z.at[self.a, 0, o], self.r_z.at[self.a, o], p.dev(p.g, p.t + 1))

    def c_down(self, src, o):
        p = self.p
        return self.put(src, p.g, o, None, self.s_z.at[self.a, 1, o], self.r_z.at[self.a, o], p.dev(p.g, p.t - 1))

    def c_xy(self, src, which, o):
        p = self.p
        g = (p.g, p.g, p.gx, p.gy)[which]
        half = (None, None, 0, 1)[which]
        to = (p.gx, p.gy, p.gy, p.gx)[which]
        return self.put(src, g, o, half, self.s_xy.at[self.a, which, o], self.r_xy.at[self.a, which, o], p.dev(to, p.t))

    def c_sib(self, src, which, o):
        p = self.p
        g = (p.g, p.gx, p.gy, p.gd, p.gd)[which]
        half = (None, None, None, 0, 1)[which]
        return self.put(src, g, o, half, self.s_sib.at[self.a, which, o], self.r_sib.at[self.a, which, o], p.dev(p.gs, p.t))

    def own(self):
        p = self.p
        src, t = self.shard, p.t
        pltpu.make_async_copy(src, self.view(p.g, t), self.loc.at[self.a]).start()

        @pl.when(t < p.length - 1)
        def _():
            self.c_up(src, t).start()

        @pl.when(t > 0)
        def _():
            self.c_down(src, t).start()

        self.c_xy(src, 0, t).start()
        self.c_xy(src, 1, t).start()
        self.c_sib(src, 0, t).start()

    def spread(self, o):
        src = self.view(self.p.g, o)
        self.c_xy(src, 0, o).start()
        self.c_xy(src, 1, o).start()
        self.c_sib(src, 0, o).start()

    def z(self, d):
        p = self.p
        t, last = p.t, p.length - 1

        @pl.when(t - d >= 0)
        def _():
            o = t - d
            src = self.view(p.g, o)
            self.c_up(src, o).wait_recv()

            @pl.when(t < last)
            def _():
                self.c_up(src, o).start()

            self.spread(o)

        @pl.when(t + d <= last)
        def _():
            o = t + d
            src = self.view(p.g, o)
            self.c_down(src, o).wait_recv()

            @pl.when(t > 0)
            def _():
                self.c_down(src, o).start()

            self.spread(o)

    def side(self, which, i):
        p = self.p
        o = p.order(i)
        g = (p.gx, p.gy)[which]
        full = self.view(g, o)
        self.wait_xy(which, g, o, None)
        self.c_xy(self.view(g, o, which), 2 + which, o).start()
        self.c_sib(full, 1 + which, o).start()

    def wait_xy(self, which, g, o, half):
        v = self.view(g, o, half)
        p = self.p
        remote(v, v, self.s_xy.at[self.a, which, o], self.r_xy.at[self.a, which, o], p.dev(p.gx, p.t)).wait_recv()

    def diag(self, which, i):
        p = self.p
        o = p.order(i)
        self.wait_xy(2 + which, p.gd, o, which)
        self.c_sib(self.view(p.gd, o, which), 3 + which, o).start()

    def finish(self):
        p = self.p

        @pl.loop(0, p.length)
        def _(o):
            for which in range(5):
                g = p.sib((p.g, p.gx, p.gy, p.gd, p.gd)[which])
                half = (None, None, None, 0, 1)[which]
                v = self.view(g, o, half)
                remote(v, v, self.s_sib.at[self.a, which, o], self.r_sib.at[self.a, which, o], p.dev(p.gs, p.t)).wait_recv()

        pltpu.make_async_copy(self.shard, self.view(p.g, p.t), self.loc.at[self.a]).wait()

    def drain(self):
        p = self.p

        @pl.loop(0, p.length)
        def _(o):
            src = self.view(p.g, o)

            @pl.when(jnp.logical_and(o <= p.t, p.t < p.length - 1))
            def _():
                self.c_up(src, o).wait_send()

            @pl.when(jnp.logical_and(o >= p.t, p.t > 0))
            def _():
                self.c_down(src, o).wait_send()

            self.c_xy(src, 0, o).wait_send()
            self.c_xy(src, 1, o).wait_send()
            self.c_xy(self.view(p.gx, o, 0), 2, o).wait_send()
            self.c_xy(self.view(p.gy, o, 1), 3, o).wait_send()
            for which in range(5):
                g = (p.g, p.gx, p.gy, p.gd, p.gd)[which]
                half = (None, None, None, 0, 1)[which]
                self.c_sib(self.view(g, o, half), which, o).wait_send()

    def middle(self):
        for d in range(1, self.p.length):
            yield self.z(d)
        for i in range(self.p.length):
            yield self.side(0, i)
            yield self.side(1, i)
        for i in range(self.p.length):
            yield self.diag(0, i)
            yield self.diag(1, i)


def gather_sems(arrays, length):
    dma = pltpu.SemaphoreType.DMA
    return [
        dma((arrays, 2, length)),
        dma((arrays, 4, length)),
        dma((arrays, 5, length)),
        dma((arrays, length)),
        dma((arrays, 4, length)),
        dma((arrays, 5, length)),
        dma((arrays,)),
    ]


def step(gen, count=1):
    for _ in range(count):
        next(gen, None)


def chain(*gens):
    for g in gens:
        yield from g


def statistics(tokens):
    average = jnp.mean(tokens, axis=-1, keepdims=True)
    centred = tokens - average
    inverse = lax.rsqrt(jnp.mean(centred * centred, axis=-1, keepdims=True) + epsilon)
    return centred * inverse, inverse


def nt(a, b):
    return lax.dot_general(a, b, (((1,), (1,)), ((), ())), preferred_element_type=f32)


def tn(a, b):
    return lax.dot_general(a, b, (((0,), (0,)), ((), ())), preferred_element_type=f32)


def nn(a, b):
    return jnp.dot(a, b, preferred_element_type=f32)


def wide(ref, lead, rows=slice(None)):
    return jnp.concatenate([ref[i, rows, :] for i in lead], axis=1)


def store_out(copies, src, dst, sem):
    c = pltpu.make_async_copy(src, dst, sem)
    c.start()
    copies.append(c)


def forward_kernel(ratio, length, x, mask, s_s, q_s, o_s, u_s, d_s,
                   vec_o, wq_o, wo_o, wu_o, wd_o, hid1_o, qkv_o, att_o, lse_o, mid_o, hid2_o, act_o, g_o, out_o,
                   ws, wq, wo, wu, wd, smf, vec, hid1, qkv, att, lse, mid, hid2, act, gg, pre, outb,
                   s_z, s_xy, s_sib, r_z, r_xy, r_sib, loc, outs):
    place = Place(ratio, length)
    rows, width = hid1.shape
    keys = qkv.shape[1]
    hidden = act.shape[1]
    nb = rows // 16
    sems = (s_z, s_xy, s_sib, r_z, r_xy, r_sib, loc)
    small = Gather(place, 0, "s", s_s, ws, s_s.shape[0], sems)
    gq = Gather(place, 1, "q", q_s, wq, q_s.shape[1], sems)
    go = Gather(place, 2, "o", o_s, wo, o_s.shape[0], sems)
    gu = Gather(place, 3, "u", u_s, wu, u_s.shape[0], sems)
    gd = Gather(place, 4, "d", d_s, wd, d_s.shape[0], sems)
    everything = (small, gq, go, gu, gd)
    enter(place, neighbours(place))
    small.own()
    gq.own()
    go.own()
    for _ in small.middle():
        pass
    gu.own()
    first = gq.middle()
    step(first, 3)
    small.finish()
    copies = []

    for g in range(GROUPS):
        for t in range(length):
            smf[g, t] = ws[g, t].astype(f32)
    per = width // GROUPS
    for row in range(6):
        vec[row : row + 1, 0:width] = jnp.concatenate([smf[g, 0, row : row + 1, :] for g in range(GROUPS)], axis=1)
    local = width // length
    for c in range(2):
        parts = []
        for t in range(length):
            for j in range(local // 128):
                r = 6 + c * (local // 128) + j
                parts.append(smf[0, t, r : r + 1, :])
        vec[6 + c : 7 + c, 0:width] = jnp.concatenate(parts, axis=1)
    base = 6 + 2 * (local // 128)
    nh = hidden // length // 128
    for t in range(length):
        vec[8 : 9, t * (hidden // length) : (t + 1) * (hidden // length)] = jnp.concatenate(
            [smf[0, t, base + j : base + j + 1, :] for j in range(nh)], axis=1
        )
    store_out(copies, vec, vec_o, outs.at[13])

    gain, shift = vec[0:1, 0:width], vec[2:3, 0:width]

    @pl.loop(0, nb)
    def _(i):
        r = pl.ds(aligned(i * 16, 16), 16)
        n, _inv = statistics(x[r, :].astype(f32))
        hid1[r, :] = (n * gain + shift).astype(bf16)

    store_out(copies, hid1, hid1_o, outs.at[0])
    qkv[:, rows:keys, :] = jnp.zeros((3, keys - rows, width), bf16)
    for _ in first:
        pass
    second = chain(go.middle(), gu.middle(), gd.middle())
    step(second, 3)
    gq.finish()
    store_out(copies, wq, wq_o, outs.at[1])
    step(second, 8)
    gd.own()

    scale = HEAD ** (-0.5)
    for c in range(3):
        r = nn(hid1[...], wide(wq.at[c], range(length)))
        if c == 0:
            r = (r + vec[6:7, 0:width]).astype(bf16) * jnp.asarray(scale, bf16)
        elif c == 2:
            r = (r + vec[7:8, 0:width]).astype(bf16)
        else:
            r = r.astype(bf16)
        qkv[c, 0:rows, :] = r
        step(second, 3)
    store_out(copies, qkv, qkv_o, outs.at[2])

    pairs = width // 128
    low = lax.broadcasted_iota(jnp.int32, (128, 128), 1) < HEAD

    def attend(p):
        cols = pl.ds(aligned(p * 128, 128), 128)
        k2 = qkv[1, :, cols]
        v2 = qkv[2, :, cols]
        for r0 in range(0, keys, 128):
            n = min(128, rows - r0)
            q2 = qkv[0, r0 : r0 + 128, cols]
            done = []
            for h in range(2):
                mine = low if h == 0 else jnp.logical_not(low)
                s = nt(jnp.where(mine, q2, jnp.zeros_like(q2)), k2) + mask[...]
                m = jnp.max(s, axis=-1, keepdims=True)
                e = jnp.exp(s - m)
                total = jnp.sum(e, axis=-1, keepdims=True)
                done.append(nn(e.astype(bf16), v2) * (1.0 / total))
                flat = jnp.transpose(jnp.broadcast_to(m + jnp.log(total), (128, 128)))
                lse[p, h : h + 1, r0 : r0 + 128] = flat[0:1, :]
            a2 = jnp.where(low, done[0], done[1]).astype(bf16)
            att[r0 : r0 + n, cols] = a2[0:n, :]

    for part in range(4):

        @pl.loop(0, pairs // 4)
        def _(j):
            attend(part * (pairs // 4) + j)

        step(second, 6)
    store_out(copies, att, att_o, outs.at[3])
    store_out(copies, lse, lse_o, outs.at[4])
    go.finish()
    store_out(copies, wo, wo_o, outs.at[5])
    step(second, 2)

    mid[...] = nn(att[...], wide(wo, range(GROUPS))) + vec[4:5, 0:width]
    step(second, 2)
    gain2, shift2 = vec[1:2, 0:width], vec[3:4, 0:width]

    @pl.loop(0, nb)
    def _(i):
        r = pl.ds(aligned(i * 16, 16), 16)
        m = x[r, :].astype(f32) + mid[r, :]
        mid[r, :] = m
        n, _inv = statistics(m)
        hid2[r, :] = (n * gain2 + shift2).astype(bf16)

    store_out(copies, mid, mid_o, outs.at[6])
    store_out(copies, hid2, hid2_o, outs.at[7])
    left = length * 4 + length - 1
    for _ in range(200):
        step(second)
    gu.finish()
    store_out(copies, wu, wu_o, outs.at[8])

    part = pre.shape[1]
    for t in range(hidden // part):
        cols = slice(t * part, (t + 1) * part)
        each = wu.shape[2]
        blk, off = (t * part) // each, (t * part) % each
        pre[...] = nn(hid2[...], wu[blk, :, off : off + part])

        @pl.loop(0, nb)
        def _(i):
            r = pl.ds(aligned(i * 16, 16), 16)
            z = pre[r, :] + vec[8:9, cols]
            cdf = 0.5 * (1.0 + lax.erf(z * half_root))
            act[r, cols] = (z * cdf).astype(bf16)
            gg[r, cols] = (cdf + z * (jnp.exp(-0.5 * z * z) * density_scale)).astype(bf16)

    store_out(copies, act, act_o, outs.at[9])
    store_out(copies, gg, g_o, outs.at[10])
    gd.finish()
    store_out(copies, wd, wd_o, outs.at[11])

    for j in range(GROUPS // 2):
        cols = slice(2 * j * per, 2 * (j + 1) * per)
        r = nn(act[...], wide(wd, (2 * j, 2 * j + 1)))
        outb[:, cols] = (mid[:, cols] + (r + vec[5:6, cols])).astype(bf16)
    store_out(copies, outb, out_o, outs.at[12])
    for a in everything:
        a.drain()
    for c in copies:
        c.wait()


def any_spec():
    return pl.BlockSpec(memory_space=pl.ANY)


def vmem_spec():
    return pl.BlockSpec(memory_space=pltpu.VMEM)


def forward(ratio, length, x, mask, small, q_s, o_s, u_s, d_s):
    rows, width = x.shape
    keys = mask.shape[1]
    hidden = u_s.shape[1] * length
    sds = jax.ShapeDtypeStruct
    n_q, n_o, n_u, n_d = q_s.shape[1], o_s.shape[0], u_s.shape[0], d_s.shape[0]
    wq = ((3, length, GROUPS * n_q, q_s.shape[2]), bf16)
    wo = ((GROUPS, length * n_o, o_s.shape[1]), bf16)
    wu = ((length, GROUPS * n_u, u_s.shape[1]), bf16)
    wd = ((GROUPS, length * n_d, d_s.shape[1]), bf16)
    pairs = width // 128
    vec = ((16, hidden), f32)
    hid = ((rows, width), bf16)
    qkv = ((3, keys, width), bf16)
    lse = ((pairs, 8, keys), f32)
    mid = ((rows, width), f32)
    act = ((rows, hidden), bf16)
    outs = [vec, wq, wo, wu, wd, hid, qkv, hid, lse, mid, hid, act, act, hid]
    scratch = [((GROUPS, length) + small.shape, bf16), wq, wo, wu, wd, ((GROUPS, length) + small.shape, f32), vec,
               hid, qkv, hid, lse, mid, hid, act, act, ((rows, 512), f32), hid]
    return pl.pallas_call(
        functools.partial(forward_kernel, ratio, length),
        out_shape=[sds(*o) for o in outs],
        in_specs=[vmem_spec(), vmem_spec()] + [any_spec()] * 5,
        out_specs=[any_spec()] * len(outs),
        scratch_shapes=[pltpu.VMEM(*s) for s in scratch] + gather_sems(5, length) + [pltpu.SemaphoreType.DMA((14,))],
        compiler_params=pltpu.CompilerParams(collective_id=0, has_side_effects=True, vmem_limit_bytes=VMEM_LIMIT),
        name="forward",
    )(x, mask, small, q_s, o_s, u_s, d_s)


def prepare(length, inputs, lengths, norm_gains, norm_shifts, w_qkv, bias_qv, w_out, out_bias, w_up, b_up, w_down, cotangent, fsdp):
    ratio = fsdp // GROUPS
    if ratio > 1:
        groups = [[g * ratio + r for r in range(ratio)] for g in range(GROUPS)]

        def join(a, axis):
            return lax.all_gather(a, "fsdp", axis=axis, tiled=True, axis_index_groups=groups)

        norm_gains, norm_shifts, out_bias = join(norm_gains, 1), join(norm_shifts, 1), join(out_bias, 1)
        w_qkv, w_out, w_up, w_down = join(w_qkv, 1), join(w_out, 1), join(w_up, 0), join(w_down, 1)
    t = lax.axis_index("tensor")
    batch, seq, width = inputs.shape
    rows = -(-seq // 16) * 16
    keys = -(-seq // 128) * 128

    def mine(a):
        a = lax.dynamic_index_in_dim(a, t, 0, keepdims=False)
        return jnp.pad(a, ((0, rows - seq), (0, 0)))

    count = lax.dynamic_index_in_dim(lengths, t, 0, keepdims=False)
    mask = jnp.where(jnp.arange(keys) < count, 0.0, -jnp.inf).astype(f32)
    small = jnp.concatenate(
        [norm_gains, norm_shifts, out_bias, bias_qv.reshape(-1, 128), b_up.reshape(-1, 128)], axis=0
    )
    small = jnp.pad(small, ((0, 32 - small.shape[0]), (0, 0)))
    return ratio, mine(inputs), mine(cotangent), mask, small, w_qkv, w_out, w_up, w_down


class Line:
    def __init__(self, place, full, send, recv):
        self.p, self.full, self.send, self.recv = place, full, send, recv

    def up(self, src, o):
        p = self.p
        return remote(src, self.full.at[o], self.send.at[0, o], self.recv.at[o], p.dev(p.g, p.t + 1))

    def down(self, src, o):
        p = self.p
        return remote(src, self.full.at[o], self.send.at[1, o], self.recv.at[o], p.dev(p.g, p.t - 1))

    def pass_on(self, d, src=None):
        p = self.p
        t, last = p.t, p.length - 1

        @pl.when(jnp.logical_and(t - d >= 0, t < last))
        def _():
            o = t - d
            self.up(self.full.at[o] if src is None else src, o).start()

        @pl.when(jnp.logical_and(t + d <= last, t > 0))
        def _():
            o = t + d
            self.down(self.full.at[o] if src is None else src, o).start()

    def arrive(self, d):
        p = self.p
        t, last = p.t, p.length - 1

        @pl.when(t - d >= 0)
        def _():
            self.up(self.full.at[t - d], t - d).wait_recv()

        @pl.when(t + d <= last)
        def _():
            self.down(self.full.at[t + d], t + d).wait_recv()

    def drain(self, d, src=None):
        p = self.p
        t, last = p.t, p.length - 1

        @pl.when(jnp.logical_and(t - d >= 0, t < last))
        def _():
            self.up(self.full.at[t - d] if src is None else src, t - d).wait_send()

        @pl.when(jnp.logical_and(t + d <= last, t > 0))
        def _():
            self.down(self.full.at[t + d] if src is None else src, t + d).wait_send()


def add_into(dst, src):
    shape = dst.shape
    n = shape[-2]
    lead = 1
    for s in shape[:-2]:
        lead *= s
    rows = min(n, 65536 // shape[-1])
    per = n // rows

    @pl.loop(0, lead * per)
    def _(i):
        r = pl.ds(aligned(lax.rem(i, per) * rows, rows), rows)
        j = lax.div(i, per)
        idx = []
        for s in reversed(shape[:-2]):
            idx.append(lax.rem(j, s))
            j = lax.div(j, s)
        idx = tuple(reversed(idx)) + (r, slice(None))
        dst[idx] = dst[idx] + src[idx]


class Scatter:
    def __init__(self, place, index, kind, plane, bufs, out, sems):
        self.p, self.a, self.kind, self.plane, self.out = place, index, kind, plane, out
        self.ra, self.rb, self.xa, self.xb, self.below, self.above = bufs
        self.send, self.recv = sems

    def half(self, k, h):
        n = self.plane.shape[-2] // 2
        r = pl.ds(h * n, n)
        if self.kind in ("o", "d"):
            return self.plane.at[k, :, r, :]
        if self.kind == "u":
            return self.plane.at[:, k, r, :]
        return self.plane.at[:, :, k, r, :]

    def block(self, o):
        k = self.k()
        if self.kind in ("o", "d"):
            return self.plane.at[k, o]
        if self.kind == "u":
            return self.plane.at[o, k]
        return self.plane.at[:, o, k]

    def k(self):
        return self.p.y * 2 + self.p.x

    def copy(self, slot, src, dst, dev):
        return remote(src, dst, self.send.at[self.a, slot], self.recv.at[self.a, slot], dev)

    def stage(self, slot):
        p = self.p
        ox, oy = 1 - p.x, 1 - p.y
        to_x, to_y = p.dev(p.gx, p.t), p.dev(p.gy, p.t)
        if slot == 0:
            return self.copy(0, self.half(oy * 2 + ox, 0), self.ra.at[0], to_y)
        if slot == 1:
            return self.copy(1, self.half(oy * 2 + p.x, 0), self.ra.at[1], to_y)
        if slot == 2:
            return self.copy(2, self.half(oy * 2 + ox, 1), self.rb.at[0], to_x)
        if slot == 3:
            return self.copy(3, self.half(p.y * 2 + ox, 1), self.rb.at[1], to_x)
        if slot == 4:
            return self.copy(4, self.half(p.y * 2 + ox, 0), self.xa, to_x)
        return self.copy(5, self.half(oy * 2 + p.x, 1), self.xb, to_y)

    def first(self):
        for slot in (0, 2, 1, 3):
            self.stage(slot).start()

    def cross(self):
        p = self.p
        ox, oy = 1 - p.x, 1 - p.y
        self.stage(0).wait_recv()
        add_into(self.half(p.y * 2 + ox, 0), self.ra.at[0])
        self.stage(4).start()
        yield
        self.stage(2).wait_recv()
        add_into(self.half(oy * 2 + p.x, 1), self.rb.at[0])
        self.stage(5).start()
        yield
        self.stage(1).wait_recv()
        add_into(self.half(self.k(), 0), self.ra.at[1])
        yield
        self.stage(3).wait_recv()
        add_into(self.half(self.k(), 1), self.rb.at[1])
        yield

    def meet(self):
        self.stage(4).wait_recv()
        add_into(self.half(self.k(), 0), self.xa)
        yield
        self.stage(5).wait_recv()
        add_into(self.half(self.k(), 1), self.xb)
        yield

    def up(self, o):
        p = self.p
        return self.copy(6 + o, self.block(o), self.below.at[o], p.dev(p.g, p.t + 1))

    def down(self, o):
        p = self.p
        return self.copy(6 + p.length + o, self.block(o), self.above.at[o], p.dev(p.g, p.t - 1))

    def line(self):
        p = self.p
        t, last = p.t, p.length - 1
        for j in range(last):
            o, q = last - j, j

            @pl.when(o > t)
            def _():
                @pl.when(t > 0)
                def _():
                    self.up(o).wait_recv()
                    add_into(self.block(o), self.below.at[o])

                self.up(o).start()

            @pl.when(q < t)
            def _():
                @pl.when(t < last)
                def _():
                    self.down(q).wait_recv()
                    add_into(self.block(q), self.above.at[q])

                self.down(q).start()

            yield

    def final(self, staged, sem):
        p = self.p
        t, last = p.t, p.length - 1

        @pl.when(t > 0)
        def _():
            self.up(t).wait_recv()
            add_into(self.block(t), self.below.at[t])

        @pl.when(t < last)
        def _():
            self.down(t).wait_recv()
            add_into(self.block(t), self.above.at[t])

        c = pltpu.make_async_copy(self.block(t), self.out, sem)
        c.start()
        return c

    def drain(self):
        p = self.p
        for slot in range(6):
            self.stage(slot).wait_send()
        for o in range(p.length):

            @pl.when(jnp.logical_and(o > p.t, p.t < p.length - 1))
            def _():
                self.up(o).wait_send()

            @pl.when(jnp.logical_and(o < p.t, p.t > 0))
            def _():
                self.down(o).wait_send()


def scatter_buffers(kind, n, w, length):
    half = {"q": (3, length, n // 2, w)}.get(kind, (length, n // 2, w))
    full = {"q": (3, n, w)}.get(kind, (n, w))
    return [pltpu.VMEM(s, bf16) for s in ((2,) + half, (2,) + half, half, half, (length,) + full, (length,) + full)]


def load(src, dst, sem):
    c = pltpu.make_async_copy(src, dst, sem)
    c.start()
    return c


def mlp_back_kernel(ratio, length, vec_i, wd_i, wu_i, act_i, g_i, hid2_i, mid_i, ct_i, out_i,
                    all_o, pd_o, pu_o, dmid_o, sums_o,
                    vec, wd, wu, act, gg, hid2, mid, ct, acc, gds, gus, cd, cu, sums, red,
                    line_s, line_r, core_s, core_r, ins, outs):
    place = Place(ratio, length)
    rows, width = ct.shape
    nb = rows // 16
    each = wu.shape[2]
    enter(place, neighbours(place))
    line = Line(place, all_o, line_s, line_r)
    line.pass_on(0, out_i)
    own = load(out_i, all_o.at[place.t], outs.at[0])
    l_ct = load(ct_i, ct, ins.at[0])
    l_wd = [load(wd_i.at[:, pl.ds(t * each, each), :], wd.at[:, pl.ds(t * each, each), :], ins.at[1 + t]) for t in range(length)]
    l_g = load(g_i, gg, ins.at[5])
    l_act = load(act_i, act, ins.at[6])
    l_h = load(hid2_i, hid2, ins.at[7])
    l_vec = load(vec_i, vec, ins.at[8])
    l_wu = [load(wu_i.at[t], wu.at[t], ins.at[9 + t]) for t in range(length)]
    l_mid = load(mid_i, mid, ins.at[13])
    sums[...] = jnp.zeros_like(sums)
    red[...] = jnp.zeros_like(red)
    l_ct.wait()
    l_g.wait()
    other = 1 - place.core
    writes = []

    def sib(src, dst, a, t):
        return remote(src, dst, core_s.at[a, t], core_r.at[a, t], place.dev(place.gs, place.t))

    def to_d(t):
        return sib(gds.at[t % 2, :, other], cd.at[:, t], 0, t)

    def to_u(t):
        return sib(gus.at[t % 2, :, other], cu.at[t], 1, t)

    def settle(t):
        to_d(t).wait_recv()
        add_into(cd.at[:, t], gds.at[t % 2, :, place.core])
        store_out(writes, cd.at[:, t], pd_o.at[:, t], outs.at[1 + t])
        to_u(t).wait_recv()
        add_into(cu.at[t], gus.at[t % 2, :, place.core])
        store_out(writes, cu.at[t], pu_o.at[t], outs.at[5 + t])

    for t in range(length):
        cols = slice(t * each, (t + 1) * each)
        l_wd[t].wait()
        d = nt(ct[...], wide(wd, range(GROUPS), cols)) * gg[:, cols].astype(f32)
        sums[8 + t : 9 + t, :] = jnp.sum(d, axis=0, keepdims=True)
        gg[:, cols] = d.astype(bf16)
        if t == 0:
            l_act.wait()
            l_h.wait()
        if t >= 2:
            to_d(t - 2).wait_send()
            to_u(t - 2).wait_send()
        down = tn(act[:, cols], ct[...]).astype(bf16)
        for g in range(GROUPS):
            gds[t % 2, g // 2, g % 2] = down[:, g * 128 : (g + 1) * 128]
        to_d(t).start()
        gus[t % 2] = tn(hid2[...], gg[:, cols]).astype(bf16).reshape(gus.shape[1:])
        to_u(t).start()
        if t > 0:
            settle(t - 1)
        l_wu[t].wait()
        part = nt(gg[:, cols], wu[t])
        if t == 0:
            acc[...] = part
        else:
            acc[...] += part
    settle(length - 1)
    l_vec.wait()
    l_mid.wait()
    gain = vec[1:2, 0:width]

    @pl.loop(0, nb)
    def _(i):
        r = pl.ds(aligned(i * 16, 16), 16)
        n, inverse = statistics(mid[r, :])
        dh = acc[r, :]
        e = dh * gain
        c = ct[r, :].astype(f32)
        dm = c + inverse * (e - jnp.mean(e, axis=-1, keepdims=True) - n * jnp.mean(e * n, axis=-1, keepdims=True))
        mid[r, :] = dm
        for j, v in enumerate((dh * n, dh, dm, c)):
            red[j] += v[0:8] + v[8:16]

    for j, row in enumerate((1, 3, 4, 5)):
        sums[row : row + 1, :] = jnp.sum(red[j], axis=0, keepdims=True)
    store_out(writes, mid, dmid_o, outs.at[9])
    store_out(writes, sums, sums_o, outs.at[10])
    for t in (length - 2, length - 1):
        to_d(t).wait_send()
        to_u(t).wait_send()
    line.arrive(1)
    line.drain(0, out_i)
    own.wait()
    for c in writes:
        c.wait()


def mlp_back(ratio, length, vec, wd, wu, act, g, hid2, mid, ct, out):
    rows, width = ct.shape
    sds = jax.ShapeDtypeStruct
    each = wu.shape[2]
    n_u = wu.shape[1] // GROUPS
    pd = ((GROUPS // 2, length, each, 128), bf16)
    pu = ((length, GROUPS // 2, n_u, each), bf16)
    sums = ((16, width), f32)
    tok = ((rows, width), f32)
    hid = ((rows, width), bf16)
    scratch = [(vec.shape, f32), (wd.shape, bf16), (wu.shape, bf16), (act.shape, bf16), (act.shape, bf16), hid, tok, hid, tok,
               ((2, GROUPS // 2, 2, each, 128), bf16), ((2, GROUPS // 2, 2, n_u, each), bf16), pd, pu, sums, ((4, 8, width), f32)]
    dma = pltpu.SemaphoreType.DMA
    outs = [((length, rows, width), bf16), pd, pu, tok, sums]
    return pl.pallas_call(
        functools.partial(mlp_back_kernel, ratio, length),
        out_shape=[sds(*o) for o in outs],
        in_specs=[any_spec()] * 9,
        out_specs=[any_spec()] * len(outs),
        scratch_shapes=[pltpu.VMEM(*s) for s in scratch]
        + [dma((2, length)), dma((length,)), dma((2, length)), dma((2, length)), dma((14,)), dma((11,))],
        compiler_params=pltpu.CompilerParams(collective_id=1, has_side_effects=True, vmem_limit_bytes=VMEM_LIMIT),
        name="mlp_back",
    )(vec, wd, wu, act, g, hid2, mid, ct, out)


def attn_back_kernel(ratio, length, vec_i, wo_i, wq_i, hid1_i, qkv_i, att_i, lse_i, dmid_i, x_i, maskc_i, pd_i, pu_i, sums_i, all_i,
                     all_o, gi_o, od_o, ou_o, oo_o, oq_o, sums_o,
                     vec, wo, wq, hid1, qkv, att, lse, dmid, dmb, da, x, maskc, dh, gi, pd, pu, gos, gqs, co, cq, sums, got, red,
                     *rest):
    nbuf = 6
    d_b, u_b, o_b, q_b = (rest[i * nbuf : (i + 1) * nbuf] for i in range(4))
    rest = rest[4 * nbuf :]
    line_s, line_r, gi_s, gi_r, core_s, core_r, sc_s, sc_r, sum_s, sum_r, ins, outs = rest
    place = Place(ratio, length)
    rows, width = dmid.shape
    keys = qkv.shape[1]
    nb = rows // 16
    t = place.t
    far = place.dev(place.g, t + 2 - 4 * lax.div(t, 2))
    near = place.dev(place.g, t + 1 - 2 * lax.rem(t, 2))
    enter(place, neighbours(place) + [(None, far)])
    line = Line(place, all_o, line_s, line_r)
    line.pass_on(1)
    names = [(vec_i, vec), (pd_i, pd), (pu_i, pu), (dmid_i, dmid), (wo_i, wo), (att_i, att.at[pl.ds(0, rows)]), (lse_i, lse),
             (qkv_i, qkv), (maskc_i, maskc), (wq_i, wq), (hid1_i, hid1), (x_i, x), (sums_i, sums.at[0])]
    loads = [load(a, b, ins.at[i]) for i, (a, b) in enumerate(names)]
    sd = Scatter(place, 0, "d", pd, d_b, od_o, (sc_s, sc_r))
    su = Scatter(place, 1, "u", pu, u_b, ou_o, (sc_s, sc_r))
    so = Scatter(place, 2, "o", co, o_b, oo_o, (sc_s, sc_r))
    sq = Scatter(place, 3, "q", cq, q_b, oq_o, (sc_s, sc_r))
    loads[1].wait()
    sd.first()
    loads[2].wait()
    su.first()
    for i in (0, 3, 4, 5, 6, 7, 8):
        loads[i].wait()
    other = 1 - place.core
    writes = []
    red[...] = jnp.zeros_like(red)
    att[rows:keys, :] = jnp.zeros((keys - rows, width), bf16)
    da[rows:keys, :] = jnp.zeros((keys - rows, width), bf16)
    mlp = chain(sd.cross(), su.cross(), sd.meet(), sd.line(), su.meet(), su.line())

    def sib(src, dst, a):
        return remote(src, dst, core_s.at[a], core_r.at[a], place.dev(place.gs, t))

    dmb[...] = dmid[...].astype(bf16)
    da[0:rows, :] = nt(dmb[...], wide(wo, range(GROUPS))).astype(bf16)
    g_out = tn(att[0:rows, :], dmb[...]).astype(bf16)
    for g in range(GROUPS):
        gos[g // 2, g % 2] = g_out[:, g * 128 : (g + 1) * 128].reshape(gos.shape[2:])
    to_o = sib(gos.at[:, other], co, 0)
    to_o.start()

    pairs = width // 128
    scale = HEAD ** (-0.5)

    def back(p):
        cols = pl.ds(aligned(p * 128, 128), 128)
        k2 = qkv[1, :, cols]
        v2 = qkv[2, :, cols]
        low_k = lax.broadcasted_iota(jnp.int32, k2.shape, 1) < HEAD
        dk = [None, None]
        dv = [None, None]
        total = jnp.zeros((1, 128), f32)
        for r0, n in ((0, 256), (256, 256), (512, 128)):
            q2 = qkv[0, r0 : r0 + n, cols]
            da2 = da[r0 : r0 + n, cols]
            prod = da2.astype(f32) * att[r0 : r0 + n, cols].astype(f32)
            low = lax.broadcasted_iota(jnp.int32, (n, 128), 1) < HEAD
            mc = jnp.concatenate([maskc[...]] * (n // 128), axis=1)
            dq = []
            for h in range(2):
                mine = low if h == 0 else jnp.logical_not(low)
                mine_k = low_k if h == 0 else jnp.logical_not(low_k)
                delta = jnp.sum(jnp.where(mine, prod, 0.0), axis=-1, keepdims=True)
                delta = jnp.concatenate(
                    [jnp.transpose(jnp.broadcast_to(delta[i : i + 128], (128, 128)))[0:1, :] for i in range(0, n, 128)], axis=1
                )
                s = nt(jnp.where(mine_k, k2, jnp.zeros_like(k2)), q2)
                prob = jnp.exp(s + mc - lse[p, h : h + 1, r0 : r0 + n])
                dp = nt(jnp.where(mine_k, v2, jnp.zeros_like(v2)), da2)
                ds = (prob * (dp - delta)).astype(bf16)
                dq.append(tn(ds, k2))
                a, b = nn(ds, q2), nn(prob.astype(bf16), da2)
                dk[h] = a if dk[h] is None else dk[h] + a
                dv[h] = b if dv[h] is None else dv[h] + b
            d = jnp.where(low, dq[0], dq[1]) * scale
            total = total + jnp.sum(d, axis=0, keepdims=True)
            qkv[0, r0 : r0 + n, cols] = d.astype(bf16)
        v = jnp.where(low_k, dv[0], dv[1])
        qkv[1, :, cols] = jnp.where(low_k, dk[0], dk[1]).astype(bf16)
        qkv[2, :, cols] = v.astype(bf16)
        red[2, 0:1, cols] = total
        red[2, 1:2, cols] = jnp.sum(v, axis=0, keepdims=True)

    for part in range(pairs):

        @pl.loop(0, 1)
        def _(j):
            back(part + j)

        if part in (3, 5, 6):
            step(mlp, 2)
        if part == 4:
            to_o.wait_recv()
            add_into(co, gos.at[:, place.core])
            so.first()

    loads[9].wait()
    for c in range(3):
        part = nt(qkv[c, 0:rows, :], wide(wq.at[c], range(length)))
        if c == 0:
            dh[...] = part
        else:
            dh[...] += part
    loads[11].wait()
    gain = vec[0:1, 0:width]

    @pl.loop(0, nb)
    def _(i):
        r = pl.ds(aligned(i * 16, 16), 16)
        n, inverse = statistics(x[r, :].astype(f32))
        d = dh[r, :]
        e = d * gain
        gi[r, :] = (
            dmid[r, :] + inverse * (e - jnp.mean(e, axis=-1, keepdims=True) - n * jnp.mean(e * n, axis=-1, keepdims=True))
        ).astype(bf16)
        for j, v in enumerate((d * n, d)):
            red[j] += v[0:8] + v[8:16]

    gline = Line(place, gi_o, gi_s, gi_r)
    gline.pass_on(0, gi)
    own = load(gi, gi_o.at[t], outs.at[0])
    loads[12].wait()
    sums[0, 0:1, :] = jnp.sum(red[0], axis=0, keepdims=True)
    sums[0, 2:3, :] = jnp.sum(red[1], axis=0, keepdims=True)
    sums[0, 6:8, :] = red[2, 0:2, :]

    loads[10].wait()
    to_q = []
    for c in range(3):
        g_c = tn(hid1[...], qkv[c, 0:rows, :]).astype(bf16)
        for o in range(length):
            w = gqs.shape[-1]
            gqs[c, o] = g_c[:, o * w : (o + 1) * w].reshape(gqs.shape[2:])
        q = sib(gqs.at[c, :, :, other], cq.at[c], 1 + c)
        q.start()
        to_q.append(q)
        step(mlp, 2)
    for c in range(3):
        to_q[c].wait_recv()
        add_into(cq.at[c], gqs.at[c, :, :, place.core])
    sq.first()

    partners = [place.dev(place.gs, t), place.dev(place.gx, t), place.dev(place.gy, t), near, far]
    pair = [remote(sums.at[i], got.at[i], sum_s.at[i], sum_r.at[i], dev) for i, dev in enumerate(partners)]

    def add_sums(i):
        pair[i].wait_recv()
        sums[i + 1] = sums[i] + got[i]
        if i + 1 < len(pair):
            pair[i + 1].start()

    line.arrive(2)
    line.pass_on(2)
    pair[0].start()
    tail = chain(so.cross(), so.meet(), so.line())
    for i in range(len(pair)):
        step(mlp)
        add_sums(i)
    for _ in range(10):
        step(mlp)
        step(tail)
    for _ in mlp:
        pass
    for _ in tail:
        pass
    store_out(writes, sums.at[len(pair)], sums_o, outs.at[5])
    writes.append(sd.final(None, outs.at[1]))
    writes.append(su.final(None, outs.at[2]))
    for _ in chain(sq.cross(), sq.meet()):
        pass
    line.arrive(3)
    gline.arrive(1)
    gline.pass_on(1)
    for _ in sq.line():
        pass
    writes.append(so.final(None, outs.at[3]))
    writes.append(sq.final(None, outs.at[4]))
    gline.arrive(2)
    gline.pass_on(2)
    gline.arrive(3)
    for s in (sd, su, so, sq):
        s.drain()
    to_o.wait_send()
    for q in to_q + pair:
        q.wait_send()
    line.drain(1)
    line.drain(2)
    gline.drain(0, gi)
    gline.drain(1)
    gline.drain(2)
    own.wait()
    for c in writes:
        c.wait()


def attn_back(ratio, length, vec, wo, wq, hid1, qkv, att, lse, dmid, x, maskc, pd, pu, sums, out_all):
    rows, width = x.shape
    keys = qkv.shape[1]
    sds = jax.ShapeDtypeStruct
    each = pu.shape[3]
    n_o, n_q, w_q = wo.shape[1] // length, wq.shape[2] // GROUPS, wq.shape[3]
    n_u, n_d = pu.shape[2], pd.shape[2]
    half = GROUPS // 2
    hid, tok = ((rows, width), bf16), ((rows, width), f32)
    tall = ((keys, width), bf16)
    outs = [(out_all.shape, bf16), (out_all.shape, bf16), ((n_d, 128), bf16), ((n_u, each), bf16), ((n_o, 128), bf16),
            ((3, n_q, w_q), bf16), (sums.shape, f32)]
    scratch = [(vec.shape, f32), (wo.shape, bf16), (wq.shape, bf16), hid, (qkv.shape, bf16), tall, (lse.shape, f32), tok, hid, tall, hid,
               (maskc.shape, f32), tok, hid, (pd.shape, bf16), (pu.shape, bf16),
               ((half, 2, length, n_o, 128), bf16), ((3, length, half, 2, n_q, w_q), bf16),
               ((half, length, n_o, 128), bf16), ((3, length, half, n_q, w_q), bf16),
               ((6,) + sums.shape, f32), ((5,) + sums.shape, f32), ((3, 8, width), f32)]
    bufs = (scatter_buffers("d", n_d, 128, length) + scatter_buffers("u", n_u, each, length)
            + scatter_buffers("o", n_o, 128, length) + scatter_buffers("q", n_q, w_q, length))
    dma = pltpu.SemaphoreType.DMA
    return pl.pallas_call(
        functools.partial(attn_back_kernel, ratio, length),
        out_shape=[sds(*o) for o in outs],
        in_specs=[any_spec()] * 14,
        out_specs=[any_spec()] * len(outs),
        scratch_shapes=[pltpu.VMEM(*s) for s in scratch] + bufs
        + [dma((2, length)), dma((length,)), dma((2, length)), dma((length,)), dma((4,)), dma((4,)),
           dma((4, 6 + 2 * length)), dma((4, 6 + 2 * length)), dma((5,)), dma((5,)), dma((13,)), dma((6,))],
        input_output_aliases={13: 0},
        compiler_params=pltpu.CompilerParams(collective_id=2, has_side_effects=True, vmem_limit_bytes=VMEM_LIMIT),
        name="attn_back",
    )(vec, wo, wq, hid1, qkv, att, lse, dmid, x, maskc, pd, pu, sums, out_all)


def place_kernel(out_i, gi_i, out_o, gi_o, buf_a, buf_b):
    length, rows, width = out_i.shape
    lanes = width // 128
    for r0 in range(0, rows, 16):
        base = r0 * lanes * length
        for b in range(length):
            a = out_i[b, r0 : r0 + 16, :].astype(f32)
            g = gi_i[b, r0 : r0 + 16, :].astype(f32)
            for j in range(lanes):
                at = pl.ds(base + j * length + b, 16, stride=lanes * length)
                buf_a[at, :] = a[:, j * 128 : (j + 1) * 128]
                gi_o[at, :] = g[:, j * 128 : (j + 1) * 128]
    out_o[...] = buf_a[...].astype(bf16)


def place_out(out_all, gi_all, seq):
    length, rows, width = out_all.shape
    lanes = width // 128
    blk = 64
    flat = seq * lanes * length
    spec_i = pl.BlockSpec((length, blk, width), lambda i: (0, i, 0))
    spec_o = pl.BlockSpec((blk * lanes * length, 128), lambda i: (i, 0))
    out, gi = pl.pallas_call(
        place_kernel,
        grid=(-(-seq // blk),),
        out_shape=[jax.ShapeDtypeStruct((flat, 128), bf16), jax.ShapeDtypeStruct((flat, 128), f32)],
        in_specs=[spec_i, spec_i],
        out_specs=[spec_o, spec_o],
        scratch_shapes=[pltpu.VMEM((blk * lanes * length, 128), f32), pltpu.VMEM((8, 128), f32)],
        name="place_out",
    )(out_all, gi_all)

    def shape(a):
        return a.reshape(seq, lanes, length, 128).transpose(2, 0, 1, 3).reshape(length, seq, width)

    return shape(out), shape(gi)


def local(inputs, lengths, norm_gains, norm_shifts, w_qkv, bias_qv, w_out, out_bias, w_up, b_up, w_down, cotangent):
    length = lax.axis_size("tensor")
    fsdp = lax.axis_size("fsdp")
    seq = inputs.shape[1]
    ratio, x, ct, mask, small, q_s, o_s, u_s, d_s = prepare(
        length, inputs, lengths, norm_gains, norm_shifts, w_qkv, bias_qv, w_out, out_bias, w_up, b_up, w_down, cotangent, fsdp
    )
    vec, wq, wo, wu, wd, hid1, qkv, att, lse, mid, hid2, act, gate, out = forward(
        ratio, length, x, mask[None, :], small, q_s, o_s, u_s, d_s
    )
    out_all, pd, pu, dmid, sums = mlp_back(ratio, length, vec, wd, wu, act, gate, hid2, mid, ct, out)
    maskc = jnp.broadcast_to(mask[:, None], (mask.shape[0], 128))
    out_all, gi_all, od, ou, oo, oq, sums = attn_back(
        ratio, length, vec, wo, wq, hid1, qkv, att, lse, dmid, x, maskc, pd, pu, sums, out_all
    )
    output, grad_input = place_out(out_all, gi_all, seq)
    if ratio > 1:
        groups = [[g * ratio + r for r in range(ratio)] for g in range(GROUPS)]
        across = [[g * ratio + r for g in range(GROUPS)] for r in range(ratio)]

        def cut(a, axis):
            return lax.psum_scatter(a, "fsdp", scatter_dimension=axis, tiled=True, axis_index_groups=groups)

        od, ou, oo, oq = cut(od, 1), cut(ou, 0), cut(oo, 1), cut(oq, 1)
        sums = lax.psum(sums, "fsdp", axis_index_groups=groups)
    width = inputs.shape[2]
    f, t = lax.axis_index("fsdp"), lax.axis_index("tensor")
    own = lax.dynamic_slice_in_dim(sums[0:6], f * (width // fsdp), width // fsdp, 1)
    heads = width // length
    return (
        output,
        grad_input,
        own[0:2],
        own[2:4],
        oq.astype(f32),
        lax.dynamic_slice_in_dim(sums[6:8], t * heads, heads, 1),
        oo.astype(f32),
        own[4:6],
        ou.astype(f32),
        lax.dynamic_index_in_dim(sums, 8 + t, 0, keepdims=False),
        od.astype(f32),
    )


def solution(mesh):
    placed = (
        P("fsdp", None, None),
        P("fsdp"),
        P(None, "fsdp"),
        P(None, "fsdp"),
        P(None, "fsdp", "tensor"),
        P(None, "tensor"),
        P("tensor", "fsdp"),
        P(None, "fsdp"),
        P("fsdp", "tensor"),
        P("tensor"),
        P("tensor", "fsdp"),
        P("fsdp", None, None),
    )
    return jax.shard_map(
        local,
        mesh=mesh,
        in_specs=placed,
        out_specs=(
            P("fsdp", None, None),
            P("fsdp", None, None),
            P(None, "fsdp"),
            P(None, "fsdp"),
            P(None, "fsdp", "tensor"),
            P(None, "tensor"),
            P("tensor", "fsdp"),
            P(None, "fsdp"),
            P("fsdp", "tensor"),
            P("tensor"),
            P("tensor", "fsdp"),
        ),
        check_vma=False,
    )
```

```python
import functools

import jax
import jax.numpy as jnp
from jax import lax
from jax.experimental import pallas as pl
from jax.experimental.pallas import tpu as pltpu
from jax.sharding import PartitionSpec as P

HEAD = 64
GROUPS = 8
epsilon = 1e-06
half_root = 0.7071067811865476
density_scale = 0.3989422804014327
MESH = pl.DeviceIdType.MESH
bf16 = jnp.bfloat16
f32 = jnp.float32
VMEM_LIMIT = 66_500_000
ATT_STEPS = 3


def aligned(value, multiple):
    return pl.multiple_of(value, multiple)


class Place:
    def __init__(self, ratio, length):
        f = lax.axis_index("fsdp")
        self.t = lax.axis_index("tensor")
        self.length = length
        self.ratio = ratio
        self.r = lax.rem(f, ratio)
        g = lax.div(f, ratio)
        self.g = g
        self.core = lax.rem(g, 2)
        self.x = lax.rem(lax.div(g, 2), 2)
        self.y = lax.div(g, 4)
        self.gs = self.sib(g)
        self.gx = g + 2 - 4 * self.x
        self.gy = g + 4 - 8 * self.y
        self.gd = self.gx + 4 - 8 * self.y

    def sib(self, g):
        return g + 1 - 2 * self.core

    def dev(self, g, t):
        return (g * self.ratio + self.r, t)

    def order(self, i):
        half = self.length // 2
        step = 1 - 2 * lax.div(self.t, half)
        return lax.rem(self.t + i * step + self.length, self.length)


def remote(src, dst, send, recv, dev):
    return pltpu.make_async_remote_copy(
        src_ref=src, dst_ref=dst, send_sem=send, recv_sem=recv, device_id=dev, device_id_type=MESH
    )


def enter(place, partners):
    barrier = pltpu.get_barrier_semaphore()
    count = 0
    for cond, dev in partners:
        if cond is None:
            pl.semaphore_signal(barrier, inc=1, device_id=dev, device_id_type=MESH)
            count = count + 1
        else:

            @pl.when(cond)
            def _(dev=dev):
                pl.semaphore_signal(barrier, inc=1, device_id=dev, device_id_type=MESH)

            count = count + jnp.where(cond, 1, 0)
    pl.semaphore_wait(barrier, count)


def neighbours(place):
    g, t = place.g, place.t
    return [
        (None, place.dev(place.gs, t)),
        (None, place.dev(place.gx, t)),
        (None, place.dev(place.gy, t)),
        (t < place.length - 1, place.dev(g, t + 1)),
        (t > 0, place.dev(g, t - 1)),
    ]


def piece(kind, ref, g, t, n, half=None):
    size = n if half is None else n // 2
    off = 0 if half in (None, 0) else n // 2
    if kind == "q":
        return ref.at[:, t, pl.ds(aligned(g * n + off, size), size), :]
    if kind == "u":
        return ref.at[t, pl.ds(aligned(g * n + off, size), size), :]
    if kind in ("o", "d"):
        return ref.at[g, pl.ds(aligned(t * n + off, size), size), :]
    return ref.at[g, t, pl.ds(off, size), :]


class Gather:
    def __init__(self, place, index, kind, shard, full, n, sems, lined=False):
        self.p, self.a, self.kind, self.shard, self.full, self.n = place, index, kind, shard, full, n
        self.s_z, self.s_xy, self.s_sib, self.r_z, self.r_xy, self.r_sib, self.loc = sems
        self.lined = lined

    def view(self, g, o, half=None):
        return piece(self.kind, self.full, g, o, self.n, half)

    def put(self, src, g, o, half, send, recv, dev):
        return remote(src, self.view(g, o, half), send, recv, dev)

    def c_up(self, src, o, far=0):
        p = self.p
        g = p.gd if far else p.g
        return self.put(src, g, o, None, self.s_z.at[self.a, far, 0, o], self.r_z.at[self.a, far, o], p.dev(p.g, p.t + 1))

    def c_down(self, src, o, far=0):
        p = self.p
        g = p.gd if far else p.g
        return self.put(src, g, o, None, self.s_z.at[self.a, far, 1, o], self.r_z.at[self.a, far, o], p.dev(p.g, p.t - 1))

    def c_xy(self, src, which, o):
        p = self.p
        g = (p.g, p.g, p.gx, p.gy)[which]
        half = (None, None, 0, 1)[which]
        to = (p.gx, p.gy, p.gy, p.gx)[which]
        return self.put(src, g, o, half, self.s_xy.at[self.a, which, o], self.r_xy.at[self.a, which, o], p.dev(to, p.t))

    def c_sib(self, src, which, o):
        p = self.p
        g = (p.g, p.gx, p.gy, p.gd, p.gd)[which]
        half = (None, None, None, None if self.lined else 0, 1)[which]
        return self.put(src, g, o, half, self.s_sib.at[self.a, which, o], self.r_sib.at[self.a, which, o], p.dev(p.gs, p.t))

    def own(self):
        p = self.p
        src, t = self.shard, p.t
        pltpu.make_async_copy(src, self.view(p.g, t), self.loc.at[self.a]).start()

        @pl.when(t < p.length - 1)
        def _():
            self.c_up(src, t).start()

        @pl.when(t > 0)
        def _():
            self.c_down(src, t).start()

        self.c_xy(src, 0, t).start()
        self.c_xy(src, 1, t).start()
        self.c_sib(src, 0, t).start()

    def spread(self, o):
        src = self.view(self.p.g, o)
        self.c_xy(src, 0, o).start()
        self.c_xy(src, 1, o).start()
        self.c_sib(src, 0, o).start()

    def z(self, d, far=0):
        p = self.p
        t, last = p.t, p.length - 1
        g = p.gd if far else p.g

        def take(o, copy, cond):
            src = self.view(g, o)
            copy(src, o, far).wait_recv()

            @pl.when(cond)
            def _():
                copy(src, o, far).start()

            if far:
                self.c_sib(src, 3, o).start()
            else:
                self.spread(o)

        @pl.when(t - d >= 0)
        def _():
            take(t - d, self.c_up, t < last)

        @pl.when(t + d <= last)
        def _():
            take(t + d, self.c_down, t > 0)

    def corner(self):
        p = self.p
        t, last = p.t, p.length - 1
        self.wait_xy(2, p.gd, t, 0)
        self.wait_xy(3, p.gd, t, 1)
        src = self.view(p.gd, t)

        @pl.when(t < last)
        def _():
            self.c_up(src, t, 1).start()

        @pl.when(t > 0)
        def _():
            self.c_down(src, t, 1).start()

        self.c_sib(src, 3, t).start()

    def side(self, which, i):
        p = self.p
        o = p.order(i)
        g = (p.gx, p.gy)[which]
        full = self.view(g, o)
        self.wait_xy(which, g, o, None)
        if i == 0 or not self.lined:
            self.c_xy(self.view(g, o, which), 2 + which, o).start()
        self.c_sib(full, 1 + which, o).start()

    def wait_xy(self, which, g, o, half):
        v = self.view(g, o, half)
        p = self.p
        remote(v, v, self.s_xy.at[self.a, which, o], self.r_xy.at[self.a, which, o], p.dev(p.gx, p.t)).wait_recv()

    def diag(self, which, i):
        p = self.p
        o = p.order(i)
        self.wait_xy(2 + which, p.gd, o, which)
        self.c_sib(self.view(p.gd, o, which), 3 + which, o).start()

    def finish(self):
        p = self.p

        @pl.loop(0, p.length)
        def _(o):
            for which in range(4 if self.lined else 5):
                g = p.sib((p.g, p.gx, p.gy, p.gd, p.gd)[which])
                half = (None, None, None, None if self.lined else 0, 1)[which]
                v = self.view(g, o, half)
                remote(v, v, self.s_sib.at[self.a, which, o], self.r_sib.at[self.a, which, o], p.dev(p.gs, p.t)).wait_recv()

        pltpu.make_async_copy(self.shard, self.view(p.g, p.t), self.loc.at[self.a]).wait()

    def drain(self):
        p = self.p

        @pl.loop(0, p.length)
        def _(o):
            src = self.view(p.g, o)

            for far in (0, 1) if self.lined else (0,):

                @pl.when(jnp.logical_and(o <= p.t, p.t < p.length - 1))
                def _():
                    self.c_up(src, o, far).wait_send()

                @pl.when(jnp.logical_and(o >= p.t, p.t > 0))
                def _():
                    self.c_down(src, o, far).wait_send()

            self.c_xy(src, 0, o).wait_send()
            self.c_xy(src, 1, o).wait_send()
            if not self.lined:
                self.c_xy(self.view(p.gx, o, 0), 2, o).wait_send()
                self.c_xy(self.view(p.gy, o, 1), 3, o).wait_send()
            for which in range(4 if self.lined else 5):
                g = (p.g, p.gx, p.gy, p.gd, p.gd)[which]
                half = (None, None, None, None if self.lined else 0, 1)[which]
                self.c_sib(self.view(g, o, half), which, o).wait_send()

        if self.lined:
            self.c_xy(self.view(p.gx, p.t, 0), 2, p.t).wait_send()
            self.c_xy(self.view(p.gy, p.t, 1), 3, p.t).wait_send()

    def line(self):
        for d in range(1, self.p.length):
            yield self.z(d)

    def sides(self):
        for i in range(self.p.length):
            yield self.side(0, i)
            yield self.side(1, i)
            if i == 0 and self.lined:
                yield self.corner()

    def last(self):
        if self.lined:
            for d in range(1, self.p.length):
                yield self.z(d, 1)
        else:
            for i in range(self.p.length):
                yield self.diag(0, i)
                yield self.diag(1, i)


def gather_sems(arrays, length):
    dma = pltpu.SemaphoreType.DMA
    return [
        dma((arrays, 2, 2, length)),
        dma((arrays, 4, length)),
        dma((arrays, 5, length)),
        dma((arrays, 2, length)),
        dma((arrays, 4, length)),
        dma((arrays, 5, length)),
        dma((arrays,)),
    ]


def step(gen, count=1):
    for _ in range(count):
        next(gen, None)


def chain(*gens):
    for g in gens:
        yield from g


def blend(*gens):
    gens = list(gens)
    while gens:
        for g in list(gens):
            try:
                yield next(g)
            except StopIteration:
                gens.remove(g)


def row_loop(rows, step, body):
    full = rows // step

    @pl.loop(0, full)
    def _(i):
        body(pl.ds(aligned(i * step, step), step))

    for r in range(full * step, rows, 16):
        body(pl.ds(r, 16))


class Images:
    def __init__(self, place, src, dst, stage, flat, sems, seq):
        self.p, self.src, self.dst, self.stage, self.flat, self.sems, self.seq = place, src, dst, stage, flat, sems, seq
        self.per = dst.shape[1] // 128 * place.length
        self.chunk = stage.shape[1] // self.per
        self.full = seq // self.chunk

    def fetch(self, i):
        n = self.chunk * self.per
        return pltpu.make_async_copy(self.src.at[pl.ds(aligned(i * n, n), n)], self.stage.at[lax.rem(i, 2)], self.sems.at[lax.rem(i, 2)])

    def start(self):
        self.fetch(0).start()

    def spread(self, row, tokens):
        length = self.p.length
        for j in range(self.per // length):
            got = self.flat[pl.ds(j * length + self.p.t, tokens, stride=self.per), :]
            self.dst[pl.ds(aligned(row, 16), tokens), j * 128 : (j + 1) * 128] = got.astype(bf16)

    def run(self):
        @pl.loop(0, self.full)
        def _(i):
            @pl.when(i + 1 < self.full)
            def _():
                self.fetch(i + 1).start()

            self.fetch(i).wait()
            self.flat[...] = self.stage[lax.rem(i, 2)].astype(f32)
            self.spread(i * self.chunk, self.chunk)

        done, rows = self.full * self.chunk, self.dst.shape[0]
        left = (self.seq - done) * self.per
        if left:
            c = pltpu.make_async_copy(self.src.at[pl.ds(done * self.per, left)], self.stage.at[0, pl.ds(0, left)], self.sems.at[0])
            c.start()
            self.flat[...] = jnp.zeros_like(self.flat)
            c.wait()
            self.flat[0:left, :] = self.stage[0, 0:left, :].astype(f32)
        else:
            self.flat[...] = jnp.zeros_like(self.flat)
        if rows > done:
            self.spread(done, rows - done)


def statistics(tokens):
    average = jnp.mean(tokens, axis=-1, keepdims=True)
    centred = tokens - average
    inverse = lax.rsqrt(jnp.mean(centred * centred, axis=-1, keepdims=True) + epsilon)
    return centred * inverse, inverse


def nt(a, b):
    return lax.dot_general(a, b, (((1,), (1,)), ((), ())), preferred_element_type=f32)


def tn(a, b):
    return lax.dot_general(a, b, (((0,), (0,)), ((), ())), preferred_element_type=f32)


def nn(a, b):
    return jnp.dot(a, b, preferred_element_type=f32)


def wide(ref, lead, rows=slice(None)):
    return jnp.concatenate([ref[i, rows, :] for i in lead], axis=1)


def store_out(copies, src, dst, sem):
    c = pltpu.make_async_copy(src, dst, sem)
    c.start()
    copies.append(c)


def forward_kernel(ratio, length, seq, x_i, ct_i, mask, s_s, q_s, o_s, u_s, d_s,
                   vec_o, wq_o, wo_o, wu_o, wd_o, hid1_o, qkv_o, att_o, lse_o, mid_o, hid2_o, act_o, g_o, out_o, x_o, ct_o,
                   ws, wq, wo, wu, wd, smf, vec, hid1, qkv, att, lse, mid, hid2, act, gg, pre, outb, x, ct, stage, flat,
                   s_z, s_xy, s_sib, r_z, r_xy, r_sib, loc, outs, ins):
    place = Place(ratio, length)
    rows, width = hid1.shape
    keys = qkv.shape[1]
    hidden = act.shape[1]
    sems = (s_z, s_xy, s_sib, r_z, r_xy, r_sib, loc)
    small = Gather(place, 0, "s", s_s, ws, s_s.shape[0], sems)
    gq = Gather(place, 1, "q", q_s, wq, q_s.shape[1], sems)
    go = Gather(place, 2, "o", o_s, wo, o_s.shape[0], sems)
    gu = Gather(place, 3, "u", u_s, wu, u_s.shape[0], sems, True)
    gd = Gather(place, 4, "d", d_s, wd, d_s.shape[0], sems, True)
    everything = (small, gq, go, gu, gd)
    enter(place, neighbours(place))
    gx = Images(place, x_i, x, stage, flat, ins, seq)
    gc = Images(place, ct_i, ct, stage, flat, ins, seq)
    gx.start()
    small.own()
    gq.own()
    go.own()
    gu.own()
    copies = []
    gx.run()
    store_out(copies, x, x_o, outs.at[14])
    for _ in blend(small.line(), gq.line()):
        pass
    first = chain(blend(small.sides(), gq.sides()), go.line(), blend(small.last(), gu.line()))
    step(first, 4)
    gc.start()
    gd.own()
    step(first, 4)
    gc.run()
    store_out(copies, ct, ct_o, outs.at[15])
    for _ in first:
        pass
    small.finish()

    for g in range(GROUPS):
        for t in range(length):
            smf[g, t] = ws[g, t].astype(f32)
    per = width // GROUPS
    for row in range(6):
        vec[row : row + 1, 0:width] = jnp.concatenate([smf[g, 0, row : row + 1, :] for g in range(GROUPS)], axis=1)
    local = width // length
    for c in range(2):
        parts = []
        for t in range(length):
            for j in range(local // 128):
                r = 6 + c * (local // 128) + j
                parts.append(smf[0, t, r : r + 1, :])
        vec[6 + c : 7 + c, 0:width] = jnp.concatenate(parts, axis=1)
    base = 6 + 2 * (local // 128)
    nh = hidden // length // 128
    for t in range(length):
        vec[8 : 9, t * (hidden // length) : (t + 1) * (hidden // length)] = jnp.concatenate(
            [smf[0, t, base + j : base + j + 1, :] for j in range(nh)], axis=1
        )
    store_out(copies, vec, vec_o, outs.at[13])

    gain, shift = vec[0:1, 0:width], vec[2:3, 0:width]

    def norm_one(r):
        n, _inv = statistics(x[r, :].astype(f32))
        hid1[r, :] = (n * gain + shift).astype(bf16)

    row_loop(rows, 32, norm_one)
    store_out(copies, hid1, hid1_o, outs.at[0])
    qkv[:, rows:keys, :] = jnp.zeros((3, keys - rows, width), bf16)
    for _ in blend(gq.last(), gd.line()):
        pass
    gq.finish()
    store_out(copies, wq, wq_o, outs.at[1])
    second = chain(go.sides(), blend(gu.sides(), gd.sides(), go.last()), blend(gu.last(), gd.last()))
    step(second, 4)

    scale = HEAD ** (-0.5)
    for c in range(3):
        r = nn(hid1[...], wide(wq.at[c], range(length)))
        if c == 0:
            r = (r + vec[6:7, 0:width]).astype(bf16) * jnp.asarray(scale, bf16)
        elif c == 2:
            r = (r + vec[7:8, 0:width]).astype(bf16)
        else:
            r = r.astype(bf16)
        qkv[c, 0:rows, :] = r
        step(second, 2)
    store_out(copies, qkv, qkv_o, outs.at[2])

    pairs = width // 128
    low = lax.broadcasted_iota(jnp.int32, (128, 128), 1) < HEAD

    def attend(p):
        cols = pl.ds(aligned(p * 128, 128), 128)
        k2 = qkv[1, :, cols]
        v2 = qkv[2, :, cols]
        for r0 in range(0, keys, 128):
            n = min(128, rows - r0)
            q2 = qkv[0, r0 : r0 + 128, cols]
            done = []
            for h in range(2):
                mine = low if h == 0 else jnp.logical_not(low)
                s = nt(jnp.where(mine, q2, jnp.zeros_like(q2)), k2) + mask[...]
                m = jnp.max(s, axis=-1, keepdims=True)
                e = jnp.exp(s - m)
                total = jnp.sum(e, axis=-1, keepdims=True)
                done.append(nn(e.astype(bf16), v2) * (1.0 / total))
                flat = jnp.transpose(jnp.broadcast_to(m + jnp.log(total), (128, 128)))
                lse[p, h : h + 1, r0 : r0 + 128] = flat[0:1, :]
            a2 = jnp.where(low, done[0], done[1]).astype(bf16)
            att[r0 : r0 + n, cols] = a2[0:n, :]

    @pl.loop(0, pairs)
    def _(j):
        attend(j)
        for k in range(pairs):

            @pl.when(j == k)
            def _():
                step(second, ATT_STEPS)

    store_out(copies, att, att_o, outs.at[3])
    store_out(copies, lse, lse_o, outs.at[4])
    go.finish()
    store_out(copies, wo, wo_o, outs.at[5])

    mid[...] = nn(att[...], wide(wo, range(GROUPS))) + vec[4:5, 0:width]
    step(second, 2)
    gain2, shift2 = vec[1:2, 0:width], vec[3:4, 0:width]

    def norm_two(r):
        m = x[r, :].astype(f32) + mid[r, :]
        mid[r, :] = m
        n, _inv = statistics(m)
        hid2[r, :] = (n * gain2 + shift2).astype(bf16)

    row_loop(rows, 32, norm_two)
    store_out(copies, mid, mid_o, outs.at[6])
    store_out(copies, hid2, hid2_o, outs.at[7])
    for _ in second:
        pass
    gu.finish()
    store_out(copies, wu, wu_o, outs.at[8])

    part = pre.shape[1]
    for t in range(hidden // part):
        cols = slice(t * part, (t + 1) * part)
        each = wu.shape[2]
        blk, off = (t * part) // each, (t * part) % each
        pre[...] = nn(hid2[...], wu[blk, :, off : off + part])

        def gelu(r):
            z = pre[r, :] + vec[8:9, cols]
            cdf = 0.5 * (1.0 + lax.erf(z * half_root))
            act[r, cols] = (z * cdf).astype(bf16)
            gg[r, cols] = (cdf + z * (jnp.exp(-0.5 * z * z) * density_scale)).astype(bf16)

        row_loop(rows, 32, gelu)

    store_out(copies, act, act_o, outs.at[9])
    store_out(copies, gg, g_o, outs.at[10])
    gd.finish()
    store_out(copies, wd, wd_o, outs.at[11])

    for j in range(GROUPS // 2):
        cols = slice(2 * j * per, 2 * (j + 1) * per)
        r = nn(act[...], wide(wd, (2 * j, 2 * j + 1)))
        outb[:, cols] = (mid[:, cols] + (r + vec[5:6, cols])).astype(bf16)
    store_out(copies, outb, out_o.at[place.t], outs.at[12])
    for a in everything:
        a.drain()
    for c in copies:
        c.wait()


def any_spec():
    return pl.BlockSpec(memory_space=pl.ANY)


def vmem_spec():
    return pl.BlockSpec(memory_space=pltpu.VMEM)


def forward(ratio, length, seq, width, x_i, ct_i, mask, small, q_s, o_s, u_s, d_s):
    rows = -(-seq // 16) * 16
    keys = mask.shape[1]
    hidden = u_s.shape[1] * length
    sds = jax.ShapeDtypeStruct
    n_q, n_o, n_u, n_d = q_s.shape[1], o_s.shape[0], u_s.shape[0], d_s.shape[0]
    wq = ((3, length, GROUPS * n_q, q_s.shape[2]), bf16)
    wo = ((GROUPS, length * n_o, o_s.shape[1]), bf16)
    wu = ((length, GROUPS * n_u, u_s.shape[1]), bf16)
    wd = ((GROUPS, length * n_d, d_s.shape[1]), bf16)
    pairs = width // 128
    vec = ((16, hidden), f32)
    hid = ((rows, width), bf16)
    qkv = ((3, keys, width), bf16)
    lse = ((pairs, 8, keys), f32)
    mid = ((rows, width), f32)
    act = ((rows, hidden), bf16)
    outs = [vec, wq, wo, wu, wd, hid, qkv, hid, lse, mid, hid, act, act, ((length, rows, width), bf16), hid, hid]
    chunk = 64 * length * width // 128
    scratch = [((GROUPS, length) + small.shape, bf16), wq, wo, wu, wd, ((GROUPS, length) + small.shape, f32), vec,
               hid, qkv, hid, lse, mid, hid, act, act, ((rows, 512), f32), hid, hid, hid,
               ((2, chunk, 128), bf16), ((chunk, 128), f32)]
    return pl.pallas_call(
        functools.partial(forward_kernel, ratio, length, seq),
        out_shape=[sds(*o) for o in outs],
        in_specs=[any_spec(), any_spec(), vmem_spec()] + [any_spec()] * 5,
        out_specs=[any_spec()] * len(outs),
        scratch_shapes=[pltpu.VMEM(*s) for s in scratch] + gather_sems(5, length) + [pltpu.SemaphoreType.DMA((16,)), pltpu.SemaphoreType.DMA((2,))],
        compiler_params=pltpu.CompilerParams(collective_id=0, has_side_effects=True, vmem_limit_bytes=VMEM_LIMIT),
        name="forward",
    )(x_i, ct_i, mask, small, q_s, o_s, u_s, d_s)


def prepare(length, inputs, lengths, norm_gains, norm_shifts, w_qkv, bias_qv, w_out, out_bias, w_up, b_up, w_down, cotangent, fsdp):
    ratio = fsdp // GROUPS
    if ratio > 1:
        groups = [[g * ratio + r for r in range(ratio)] for g in range(GROUPS)]

        def join(a, axis):
            return lax.all_gather(a, "fsdp", axis=axis, tiled=True, axis_index_groups=groups)

        norm_gains, norm_shifts, out_bias = join(norm_gains, 1), join(norm_shifts, 1), join(out_bias, 1)
        w_qkv, w_out, w_up, w_down = join(w_qkv, 1), join(w_out, 1), join(w_up, 0), join(w_down, 1)
    t = lax.axis_index("tensor")
    batch, seq, width = inputs.shape
    keys = -(-seq // 128) * 128

    def flat(a):
        return a.reshape(batch, seq, width // 128, 128).transpose(1, 2, 0, 3).reshape(-1, 128)

    count = lax.dynamic_index_in_dim(lengths, t, 0, keepdims=False)
    mask = jnp.where(jnp.arange(keys) < count, 0.0, -jnp.inf).astype(f32)
    small = jnp.concatenate(
        [norm_gains, norm_shifts, out_bias, bias_qv.reshape(-1, 128), b_up.reshape(-1, 128)], axis=0
    )
    small = jnp.pad(small, ((0, 32 - small.shape[0]), (0, 0)))
    return ratio, flat(inputs), flat(cotangent), mask, small, w_qkv, w_out, w_up, w_down


class Line:
    def __init__(self, place, full, send, recv):
        self.p, self.full, self.send, self.recv = place, full, send, recv

    def up(self, src, o):
        p = self.p
        return remote(src, self.full.at[o], self.send.at[0, o], self.recv.at[o], p.dev(p.g, p.t + 1))

    def down(self, src, o):
        p = self.p
        return remote(src, self.full.at[o], self.send.at[1, o], self.recv.at[o], p.dev(p.g, p.t - 1))

    def pass_on(self, d, src=None):
        p = self.p
        t, last = p.t, p.length - 1

        @pl.when(jnp.logical_and(t - d >= 0, t < last))
        def _():
            o = t - d
            self.up(self.full.at[o] if src is None else src, o).start()

        @pl.when(jnp.logical_and(t + d <= last, t > 0))
        def _():
            o = t + d
            self.down(self.full.at[o] if src is None else src, o).start()

    def arrive(self, d):
        p = self.p
        t, last = p.t, p.length - 1

        @pl.when(t - d >= 0)
        def _():
            self.up(self.full.at[t - d], t - d).wait_recv()

        @pl.when(t + d <= last)
        def _():
            self.down(self.full.at[t + d], t + d).wait_recv()

    def drain(self, d, src=None):
        p = self.p
        t, last = p.t, p.length - 1

        @pl.when(jnp.logical_and(t - d >= 0, t < last))
        def _():
            self.up(self.full.at[t - d] if src is None else src, t - d).wait_send()

        @pl.when(jnp.logical_and(t + d <= last, t > 0))
        def _():
            self.down(self.full.at[t + d] if src is None else src, t + d).wait_send()


def add_into(dst, src):
    shape = dst.shape
    n = shape[-2]
    lead = 1
    for s in shape[:-2]:
        lead *= s
    rows = min(n, 65536 // shape[-1])
    per = n // rows

    @pl.loop(0, lead * per)
    def _(i):
        r = pl.ds(aligned(lax.rem(i, per) * rows, rows), rows)
        j = lax.div(i, per)
        idx = []
        for s in reversed(shape[:-2]):
            idx.append(lax.rem(j, s))
            j = lax.div(j, s)
        idx = tuple(reversed(idx)) + (r, slice(None))
        dst[idx] = dst[idx] + src[idx]


class Scatter:
    def __init__(self, place, index, owner, plane, bufs, lines, sems):
        self.p, self.a, self.o, self.plane = place, index, owner, plane
        self.ra, self.rb, self.xa, self.xb = bufs
        self.below, self.above = lines
        self.send, self.recv, self.l_send, self.l_recv = sems

    def half(self, k, h):
        n = self.plane.shape[-2] // 2
        r = pl.ds(h * n, n)
        return self.plane.at[k, r, :] if len(self.plane.shape) == 3 else self.plane.at[k, :, r, :]

    def k(self):
        return self.p.y * 2 + self.p.x

    def block(self):
        return self.plane.at[self.k()]

    def copy(self, slot, src, dst, dev):
        return remote(src, dst, self.send.at[self.a, slot], self.recv.at[self.a, slot], dev)

    def stage(self, slot):
        p = self.p
        ox, oy = 1 - p.x, 1 - p.y
        to_x, to_y = p.dev(p.gx, p.t), p.dev(p.gy, p.t)
        if slot == 0:
            return self.copy(0, self.half(oy * 2 + ox, 0), self.ra.at[0], to_y)
        if slot == 1:
            return self.copy(1, self.half(oy * 2 + p.x, 0), self.ra.at[1], to_y)
        if slot == 2:
            return self.copy(2, self.half(oy * 2 + ox, 1), self.rb.at[0], to_x)
        if slot == 3:
            return self.copy(3, self.half(p.y * 2 + ox, 1), self.rb.at[1], to_x)
        if slot == 4:
            return self.copy(4, self.half(p.y * 2 + ox, 0), self.xa, to_x)
        return self.copy(5, self.half(oy * 2 + p.x, 1), self.xb, to_y)

    def first(self):
        for slot in (0, 2, 1, 3):
            self.stage(slot).start()

    def cross(self):
        p = self.p
        self.stage(0).wait_recv()
        add_into(self.half(p.y * 2 + 1 - p.x, 0), self.ra.at[0])
        self.stage(4).start()
        self.stage(2).wait_recv()
        add_into(self.half((1 - p.y) * 2 + p.x, 1), self.rb.at[0])
        self.stage(5).start()

    def join(self):
        self.stage(1).wait_recv()
        add_into(self.half(self.k(), 0), self.ra.at[1])
        self.stage(3).wait_recv()
        add_into(self.half(self.k(), 1), self.rb.at[1])

    def meet(self):
        self.stage(4).wait_recv()
        add_into(self.half(self.k(), 0), self.xa)
        self.stage(5).wait_recv()
        add_into(self.half(self.k(), 1), self.xb)

    def up(self):
        p = self.p
        return remote(self.block(), self.below, self.l_send.at[self.a], self.l_recv.at[self.a, 0], p.dev(p.g, p.t + 1))

    def down(self):
        p = self.p
        return remote(self.block(), self.above, self.l_send.at[self.a], self.l_recv.at[self.a, 1], p.dev(p.g, p.t - 1))

    def hop(self, h):
        p = self.p
        t, last = p.t, p.length - 1
        if h < self.o:

            @pl.when(t == h)
            def _():
                if h > 0:
                    self.up().wait_recv()
                    add_into(self.block(), self.below)
                self.up().start()

        if last - h > self.o:

            @pl.when(t == last - h)
            def _():
                if h > 0:
                    self.down().wait_recv()
                    add_into(self.block(), self.above)
                self.down().start()

    def final(self, out, sem):
        p = self.p

        @pl.when(p.t == self.o)
        def _():
            if self.o > 0:
                self.up().wait_recv()
                add_into(self.block(), self.below)
            if self.o < p.length - 1:
                self.down().wait_recv()
                add_into(self.block(), self.above)
            pltpu.make_async_copy(self.block(), out, sem).start()

    def drain(self, out, sem):
        p = self.p
        for slot in range(6):
            self.stage(slot).wait_send()

        @pl.when(p.t < self.o)
        def _():
            self.up().wait_send()

        @pl.when(p.t > self.o)
        def _():
            self.down().wait_send()

        @pl.when(p.t == self.o)
        def _():
            pltpu.make_async_copy(self.block(), out, sem).wait()


def load(src, dst, sem):
    c = pltpu.make_async_copy(src, dst, sem)
    c.start()
    return c


def back_kernel(ratio, length, vec_i, wd_i, wu_i, wo_i, wq_i, g_i, mid_i, ct_i, x_i, qkv_i, att_i, lse_i, maskc_i, all_i,
                all_o, dpre_o, dqkv_o, dmb_o, gi_o, sums_o,
                vec, wd, wu, wo, wq, gg, mid, ct, x, qkv, att, lse, maskc, acc, dmb, da, gi, sums, red,
                line_s, line_r, ins, outs):
    place = Place(ratio, length)
    rows, width = ct.shape
    keys = qkv.shape[1]
    each = wu.shape[2]
    enter(place, neighbours(place))
    line = Line(place, all_o, line_s, line_r)
    line.pass_on(0)
    writes = []

    def block(t):
        return pl.ds(t * each, each)

    l_ct = load(ct_i, ct, ins.at[0])
    l_g, l_wd, l_wu = [], [], []
    for t in range(length):
        l_g.append(load(g_i.at[:, block(t)], gg.at[:, block(t)], ins.at[1 + t]))
        l_wd.append(load(wd_i.at[:, block(t), :], wd.at[:, block(t), :], ins.at[1 + length + t]))
        l_wu.append(load(wu_i.at[t], wu.at[t], ins.at[1 + 2 * length + t]))
    base = 1 + 3 * length
    names = [(vec_i, vec), (mid_i, mid), (wo_i, wo), (att_i, att.at[pl.ds(0, rows)]), (lse_i, lse), (qkv_i, qkv),
             (maskc_i, maskc), (wq_i, wq), (x_i, x)]
    loads = [load(a, b, ins.at[base + i]) for i, (a, b) in enumerate(names)]
    sums[...] = jnp.zeros_like(sums)
    red[...] = jnp.zeros_like(red)
    da[rows:keys, :] = jnp.zeros((keys - rows, width), bf16)
    att[rows:keys, :] = jnp.zeros((keys - rows, width), bf16)

    l_ct.wait()
    for t in range(length):
        cols = slice(t * each, (t + 1) * each)
        l_wd[t].wait()
        l_g[t].wait()
        d = nt(ct[...], wide(wd, range(GROUPS), cols)) * gg[:, cols].astype(f32)
        sums[8 + t : 9 + t, :] = jnp.sum(d, axis=0, keepdims=True)
        gg[:, cols] = d.astype(bf16)
        store_out(writes, gg.at[:, block(t)], dpre_o.at[:, block(t)], outs.at[5 + t])
        l_wu[t].wait()
        part = nt(gg[:, cols], wu[t])
        if t == 0:
            acc[...] = part
        else:
            acc[...] += part
    for c in loads[0:2]:
        c.wait()
    gain = vec[1:2, 0:width]

    def norm_two(r):
        n, inverse = statistics(mid[r, :])
        dh = acc[r, :]
        e = dh * gain
        c = ct[r, :].astype(f32)
        dm = c + inverse * (e - jnp.mean(e, axis=-1, keepdims=True) - n * jnp.mean(e * n, axis=-1, keepdims=True))
        mid[r, :] = dm
        dmb[r, :] = dm.astype(bf16)
        for j, v in enumerate((dh * n, dh, dm, c)):
            red[j] += sum(v[i : i + 8] for i in range(0, v.shape[0], 8))

    row_loop(rows, 32, norm_two)
    for j, row in enumerate((1, 3, 4, 5)):
        sums[row : row + 1, :] = jnp.sum(red[j], axis=0, keepdims=True)
    red[...] = jnp.zeros_like(red)
    store_out(writes, dmb, dmb_o, outs.at[0])
    line.arrive(1)
    line.pass_on(1)

    for c in loads[2:7]:
        c.wait()
    da[0:rows, :] = nt(dmb[...], wide(wo, range(GROUPS))).astype(bf16)
    pairs = width // 128
    scale = HEAD ** (-0.5)

    def back(p):
        cols = pl.ds(aligned(p * 128, 128), 128)
        k2 = qkv[1, :, cols]
        v2 = qkv[2, :, cols]
        low_k = lax.broadcasted_iota(jnp.int32, k2.shape, 1) < HEAD
        dk = [None, None]
        dv = [None, None]
        total = jnp.zeros((1, 128), f32)
        for r0, n in ((0, 256), (256, 256), (512, 128)):
            q2 = qkv[0, r0 : r0 + n, cols]
            da2 = da[r0 : r0 + n, cols]
            prod = da2.astype(f32) * att[r0 : r0 + n, cols].astype(f32)
            low = lax.broadcasted_iota(jnp.int32, (n, 128), 1) < HEAD
            mc = jnp.concatenate([maskc[...]] * (n // 128), axis=1)
            dq = []
            for h in range(2):
                mine = low if h == 0 else jnp.logical_not(low)
                mine_k = low_k if h == 0 else jnp.logical_not(low_k)
                delta = jnp.sum(jnp.where(mine, prod, 0.0), axis=-1, keepdims=True)
                delta = jnp.concatenate(
                    [jnp.transpose(jnp.broadcast_to(delta[i : i + 128], (128, 128)))[0:1, :] for i in range(0, n, 128)], axis=1
                )
                s = nt(jnp.where(mine_k, k2, jnp.zeros_like(k2)), q2)
                prob = jnp.exp(s + mc - lse[p, h : h + 1, r0 : r0 + n])
                dp = nt(jnp.where(mine_k, v2, jnp.zeros_like(v2)), da2)
                ds = (prob * (dp - delta)).astype(bf16)
                dq.append(tn(ds, k2))
                a, b = nn(ds, q2), nn(prob.astype(bf16), da2)
                dk[h] = a if dk[h] is None else dk[h] + a
                dv[h] = b if dv[h] is None else dv[h] + b
            d = jnp.where(low, dq[0], dq[1]) * scale
            total = total + jnp.sum(d, axis=0, keepdims=True)
            qkv[0, r0 : r0 + n, cols] = d.astype(bf16)
        v = jnp.where(low_k, dv[0], dv[1])
        qkv[1, :, cols] = jnp.where(low_k, dk[0], dk[1]).astype(bf16)
        qkv[2, :, cols] = v.astype(bf16)
        red[2, 0:1, cols] = total
        red[2, 1:2, cols] = jnp.sum(v, axis=0, keepdims=True)

    @pl.loop(0, pairs)
    def _(j):
        back(j)

        @pl.when(j == pairs - 2)
        def _():
            line.arrive(2)
            line.pass_on(2)

    store_out(writes, qkv, dqkv_o, outs.at[1])

    loads[7].wait()
    for c in range(3):
        part = nt(qkv[c, 0:rows, :], wide(wq.at[c], range(length)))
        if c == 0:
            acc[...] = part
        else:
            acc[...] += part
    loads[8].wait()
    gain1 = vec[0:1, 0:width]

    def norm_one(r):
        n, inverse = statistics(x[r, :].astype(f32))
        d = acc[r, :]
        e = d * gain1
        gi[r, :] = (
            mid[r, :] + inverse * (e - jnp.mean(e, axis=-1, keepdims=True) - n * jnp.mean(e * n, axis=-1, keepdims=True))
        ).astype(bf16)
        for j, v in enumerate((d * n, d)):
            red[j] += sum(v[i : i + 8] for i in range(0, v.shape[0], 8))

    row_loop(rows, 32, norm_one)
    store_out(writes, gi, gi_o.at[place.t], outs.at[2])
    sums[0:1, :] = jnp.sum(red[0], axis=0, keepdims=True)
    sums[2:3, :] = jnp.sum(red[1], axis=0, keepdims=True)
    sums[6:8, :] = red[2, 0:2, :]
    store_out(writes, sums, sums_o, outs.at[3])
    line.arrive(3)
    for d in range(length - 1):
        line.drain(d)
    for c in writes:
        c.wait()


def back(ratio, length, vec, wd, wu, wo, wq, g, mid, ct, x, qkv, att, lse, maskc, out_all):
    rows, width = ct.shape
    keys = qkv.shape[1]
    sds = jax.ShapeDtypeStruct
    sums = ((16, width), f32)
    tok, hid, tall = ((rows, width), f32), ((rows, width), bf16), ((keys, width), bf16)
    outs = [(out_all.shape, bf16), (g.shape, bf16), (qkv.shape, bf16), hid, (out_all.shape, bf16), sums]
    scratch = [(vec.shape, f32), (wd.shape, bf16), (wu.shape, bf16), (wo.shape, bf16), (wq.shape, bf16), (g.shape, bf16), tok, hid, hid,
               (qkv.shape, bf16), tall, (lse.shape, f32), (maskc.shape, f32), tok, hid, tall, hid, sums, ((4, 8, width), f32)]
    dma = pltpu.SemaphoreType.DMA
    return pl.pallas_call(
        functools.partial(back_kernel, ratio, length),
        out_shape=[sds(*o) for o in outs],
        in_specs=[any_spec()] * 14,
        out_specs=[any_spec()] * len(outs),
        scratch_shapes=[pltpu.VMEM(*s) for s in scratch] + [dma((2, length)), dma((length,)), dma((10 + 3 * length,)), dma((5 + length,))],
        input_output_aliases={13: 0},
        compiler_params=pltpu.CompilerParams(collective_id=1, has_side_effects=True, vmem_limit_bytes=VMEM_LIMIT),
        name="back",
    )(vec, wd, wu, wo, wq, g, mid, ct, x, qkv, att, lse, maskc, out_all)


def grads_kernel(ratio, length, act_i, ct_i, hid2_i, dpre_i, hid1_i, dqkv_i, att_i, dmb_i, sums_i, all_i,
                 all_o, od_o, ou_o, oo_o, oq_o, sums_o,
                 act, ct, hid2, dpre, hid1, dqkv, att, dmb, sums, got, *rest):
    kinds = ("d", "u", "q", "o")
    held = {k: rest[8 * i : 8 * (i + 1)] for i, k in enumerate(kinds)}
    line_s, line_r, core_s, core_r, sc_s, sc_r, ls_s, ls_r, sum_s, sum_r, ins, outs = rest[32:]
    place = Place(ratio, length)
    rows, width = ct.shape
    each = act.shape[1] // length
    t = place.t
    far = place.dev(place.g, t + 2 - 4 * lax.div(t, 2))
    near = place.dev(place.g, t + 1 - 2 * lax.rem(t, 2))
    enter(place, neighbours(place) + [(None, far)])
    line = Line(place, all_o, line_s, line_r)
    line.pass_on(0)
    owners = sorted(range(length), key=lambda o: -abs(2 * o - length + 1))
    loads = {}

    def block(o):
        return pl.ds(o * each, each)

    def fetch(name, a, b):
        loads[name] = load(a, b, ins.at[len(loads)])

    fetch("ct", ct_i, ct)
    fetch(("d", owners[0]), act_i.at[:, block(owners[0])], act.at[:, block(owners[0])])
    fetch("hid2", hid2_i, hid2)
    fetch(("u", owners[0]), dpre_i.at[:, block(owners[0])], dpre.at[:, block(owners[0])])
    fetch("hid1", hid1_i, hid1)
    fetch("dqkv", dqkv_i, dqkv)
    fetch("att", att_i, att)
    fetch("dmb", dmb_i, dmb)
    fetch("sums", sums_i, sums.at[0])
    for o in owners[1:]:
        fetch(("d", o), act_i.at[:, block(o)], act.at[:, block(o)])
        fetch(("u", o), dpre_i.at[:, block(o)], dpre.at[:, block(o)])
    seen = set()

    def ready(*keys):
        for key in keys:
            if key not in seen:
                seen.add(key)
                loads[key].wait()

    other = 1 - place.core
    units = [(k, o) for o in owners for k in kinds]
    out_of = {"d": od_o, "u": ou_o, "q": oq_o, "o": oo_o}
    scat = []
    for n, (k, o) in enumerate(units):
        gs, plane, ra, rb, xa, xb, below, above = held[k]
        scat.append(Scatter(place, n, o, plane.at[o], (ra.at[o], rb.at[o], xa.at[o], xb.at[o]), (below.at[o], above.at[o]),
                            (sc_s, sc_r, ls_s, ls_r)))

    def core(n):
        k, o = units[n]
        gs, plane = held[k][0], held[k][1]
        return remote(gs.at[:, other], plane.at[o], core_s.at[n], core_r.at[n], place.dev(place.gs, t))

    def compute(n):
        k, o = units[n]
        gs = held[k][0]
        if n >= len(kinds):
            core(n - len(kinds)).wait_send()
        cols = slice(o * each, (o + 1) * each)
        if k == "d":
            ready("ct", ("d", o))
            r = tn(act[:, cols], ct[...]).astype(bf16)
            for g in range(GROUPS):
                gs[g // 2, g % 2] = r[:, g * 128 : (g + 1) * 128]
        elif k == "u":
            ready("hid2", ("u", o))
            gs[...] = tn(hid2[...], dpre[:, cols]).astype(bf16).reshape(gs.shape)
        elif k == "q":
            ready("hid1", "dqkv")
            w = gs.shape[-1]
            for c in range(3):
                r = tn(hid1[...], dqkv[c, 0:rows, o * w : (o + 1) * w]).astype(bf16)
                gs[:, :, c] = r.reshape(gs.shape[:2] + gs.shape[3:])
        else:
            ready("att", "dmb")
            m = gs.shape[2]
            r = tn(att[:, o * m : (o + 1) * m], dmb[...]).astype(bf16)
            for g in range(GROUPS):
                gs[g // 2, g % 2] = r[:, g * 128 : (g + 1) * 128]
        core(n).start()

    def settle(n):
        k, o = units[n]
        gs, plane = held[k][0], held[k][1]
        core(n).wait_recv()
        add_into(plane.at[o], gs.at[:, place.core])
        scat[n].first()

    partners = [place.dev(place.gs, t), place.dev(place.gx, t), place.dev(place.gy, t), near, far]
    pair = [remote(sums.at[i], got.at[i], sum_s.at[i], sum_r.at[i], dev) for i, dev in enumerate(partners)]

    def add_sums(i):
        pair[i].wait_recv()
        sums[i + 1] = sums[i] + got[i]
        if i + 1 < len(pair):
            pair[i + 1].start()

    count = len(units)
    for n in range(count + TAIL):
        if n < count:
            compute(n)
        if n == 3:
            ready("sums")
            pair[0].start()
        if 0 <= n - 1 < count:
            settle(n - 1)
        if 4 <= n < 4 + len(pair):
            add_sums(n - 4)
        if 0 <= n - LAG[0] < count:
            scat[n - LAG[0]].cross()
        if 0 <= n - LAG[1] < count:
            scat[n - LAG[1]].join()
            scat[n - LAG[1]].meet()
        for h in range(length - 1):
            m = n - LAG[1] - LAG[2] * h
            if 0 <= m < count:
                scat[m].hop(h)
        m = n - LAG[1] - LAG[2] * (length - 1)
        if 0 <= m < count:
            k, o = units[m]
            scat[m].final(out_of[k], outs.at[kinds.index(k)])
        if n == WHEN[0]:
            line.arrive(1)
            line.pass_on(1)
        if n == WHEN[1]:
            line.arrive(2)
            line.pass_on(2)
    write = load(sums.at[len(pair)], sums_o, outs.at[len(kinds)])
    for n, (k, o) in enumerate(units):
        scat[n].drain(out_of[k], outs.at[kinds.index(k)])
    for n in range(count - len(kinds), count):
        core(n).wait_send()
    for q in pair:
        q.wait_send()
    line.arrive(3)
    for d in range(length - 1):
        line.drain(d)
    write.wait()


LAG = (3, 4, 2)
WHEN = (5, 11)
TAIL = 11


def grads(ratio, length, blocks, act, ct, hid2, dpre, hid1, dqkv, att, dmb, sums, gi_all):
    rows, width = ct.shape
    sds = jax.ShapeDtypeStruct
    hid = ((rows, width), bf16)
    outs = [(gi_all.shape, bf16)] + [(blocks[k], bf16) for k in ("d", "u", "o", "q")] + [(sums.shape, f32)]
    scratch = [(act.shape, bf16), hid, hid, (act.shape, bf16), hid, (dqkv.shape, bf16), hid, hid,
               ((6,) + sums.shape, f32), ((5,) + sums.shape, f32)]
    for k in ("d", "u", "q", "o"):
        b = tuple(blocks[k])
        h = b[:-2] + (b[-2] // 2, b[-1])
        for s in ((GROUPS // 2, 2) + b, (length, GROUPS // 2) + b, (length, 2) + h, (length, 2) + h, (length,) + h, (length,) + h,
                  (length,) + b, (length,) + b):
            scratch.append((s, bf16))
    n = 4 * length
    dma = pltpu.SemaphoreType.DMA
    return pl.pallas_call(
        functools.partial(grads_kernel, ratio, length),
        out_shape=[sds(*o) for o in outs],
        in_specs=[any_spec()] * 10,
        out_specs=[any_spec()] * len(outs),
        scratch_shapes=[pltpu.VMEM(*s) for s in scratch]
        + [dma((2, length)), dma((length,)), dma((n,)), dma((n,)), dma((n, 6)), dma((n, 6)), dma((n,)), dma((n, 2)), dma((5,)), dma((5,)),
           dma((7 + 2 * length,)), dma((5,))],
        input_output_aliases={9: 0},
        compiler_params=pltpu.CompilerParams(collective_id=2, has_side_effects=True, vmem_limit_bytes=VMEM_LIMIT),
        name="grads",
    )(act, ct, hid2, dpre, hid1, dqkv, att, dmb, sums, gi_all)


def place_kernel(out_i, gi_i, out_o, gi_o, buf_a, buf_b):
    length, rows, width = out_i.shape
    lanes = width // 128
    for r0 in range(0, rows, 16):
        base = r0 * lanes * length
        for b in range(length):
            a = out_i[b, r0 : r0 + 16, :].astype(f32)
            g = gi_i[b, r0 : r0 + 16, :].astype(f32)
            for j in range(lanes):
                at = pl.ds(base + j * length + b, 16, stride=lanes * length)
                buf_a[at, :] = a[:, j * 128 : (j + 1) * 128]
                gi_o[at, :] = g[:, j * 128 : (j + 1) * 128]
    out_o[...] = buf_a[...].astype(bf16)


def place_out(out_all, gi_all, seq):
    length, rows, width = out_all.shape
    lanes = width // 128
    blk = 64
    flat = seq * lanes * length
    spec_i = pl.BlockSpec((length, blk, width), lambda i: (0, i, 0))
    spec_o = pl.BlockSpec((blk * lanes * length, 128), lambda i: (i, 0))
    out, gi = pl.pallas_call(
        place_kernel,
        grid=(-(-seq // blk),),
        out_shape=[jax.ShapeDtypeStruct((flat, 128), bf16), jax.ShapeDtypeStruct((flat, 128), f32)],
        in_specs=[spec_i, spec_i],
        out_specs=[spec_o, spec_o],
        scratch_shapes=[pltpu.VMEM((blk * lanes * length, 128), f32), pltpu.VMEM((8, 128), f32)],
        name="place_out",
    )(out_all, gi_all)

    def shape(a):
        return a.reshape(seq, lanes, length, 128).transpose(2, 0, 1, 3).reshape(length, seq, width)

    return shape(out), shape(gi)


def local(inputs, lengths, norm_gains, norm_shifts, w_qkv, bias_qv, w_out, out_bias, w_up, b_up, w_down, cotangent):
    length = lax.axis_size("tensor")
    fsdp = lax.axis_size("fsdp")
    seq = inputs.shape[1]
    ratio, x_i, ct_i, mask, small, q_s, o_s, u_s, d_s = prepare(
        length, inputs, lengths, norm_gains, norm_shifts, w_qkv, bias_qv, w_out, out_bias, w_up, b_up, w_down, cotangent, fsdp
    )
    vec, wq, wo, wu, wd, hid1, qkv, att, lse, mid, hid2, act, gate, out_all, x, ct = forward(
        ratio, length, seq, inputs.shape[2], x_i, ct_i, mask[None, :], small, q_s, o_s, u_s, d_s
    )
    maskc = jnp.broadcast_to(mask[:, None], (mask.shape[0], 128))
    out_all, dpre, dqkv, dmb, gi_all, sums = back(
        ratio, length, vec, wd, wu, wo, wq, gate, mid, ct, x, qkv, att, lse, maskc, out_all
    )
    blocks = {"d": d_s.shape, "u": u_s.shape, "o": o_s.shape, "q": q_s.shape}
    gi_all, od, ou, oo, oq, sums = grads(ratio, length, blocks, act, ct, hid2, dpre, hid1, dqkv, att, dmb, sums, gi_all)
    output, grad_input = place_out(out_all, gi_all, seq)
    if ratio > 1:
        groups = [[g * ratio + r for r in range(ratio)] for g in range(GROUPS)]
        across = [[g * ratio + r for g in range(GROUPS)] for r in range(ratio)]

        def cut(a, axis):
            return lax.psum_scatter(a, "fsdp", scatter_dimension=axis, tiled=True, axis_index_groups=groups)

        od, ou, oo, oq = cut(od, 1), cut(ou, 0), cut(oo, 1), cut(oq, 1)
        sums = lax.psum(sums, "fsdp", axis_index_groups=groups)
    width = inputs.shape[2]
    f, t = lax.axis_index("fsdp"), lax.axis_index("tensor")
    own = lax.dynamic_slice_in_dim(sums[0:6], f * (width // fsdp), width // fsdp, 1)
    heads = width // length
    return (
        output,
        grad_input,
        own[0:2],
        own[2:4],
        oq.astype(f32),
        lax.dynamic_slice_in_dim(sums[6:8], t * heads, heads, 1),
        oo.astype(f32),
        own[4:6],
        ou.astype(f32),
        lax.dynamic_index_in_dim(sums, 8 + t, 0, keepdims=False),
        od.astype(f32),
    )


def solution(mesh):
    placed = (
        P("fsdp", None, None),
        P("fsdp"),
        P(None, "fsdp"),
        P(None, "fsdp"),
        P(None, "fsdp", "tensor"),
        P(None, "tensor"),
        P("tensor", "fsdp"),
        P(None, "fsdp"),
        P("fsdp", "tensor"),
        P("tensor"),
        P("tensor", "fsdp"),
        P("fsdp", None, None),
    )
    return jax.shard_map(
        local,
        mesh=mesh,
        in_specs=placed,
        out_specs=(
            P("fsdp", None, None),
            P("fsdp", None, None),
            P(None, "fsdp"),
            P(None, "fsdp"),
            P(None, "fsdp", "tensor"),
            P(None, "tensor"),
            P("tensor", "fsdp"),
            P(None, "fsdp"),
            P("fsdp", "tensor"),
            P("tensor"),
            P("tensor", "fsdp"),
        ),
        check_vma=False,
    )
```

```python
import functools

import jax
import jax.numpy as jnp
from jax import lax
from jax.experimental import pallas as pl
from jax.experimental.pallas import tpu as pltpu
from jax.sharding import PartitionSpec as P

HEAD = 64
GROUPS = 8
epsilon = 1e-06
half_root = 0.7071067811865476
density_scale = 0.3989422804014327
MESH = pl.DeviceIdType.MESH
bf16 = jnp.bfloat16
f32 = jnp.float32
VMEM_LIMIT = 66_500_000


def aligned(value, multiple):
    return pl.multiple_of(value, multiple)


class Place:
    def __init__(self, ratio, length):
        f = lax.axis_index("fsdp")
        self.t = lax.axis_index("tensor")
        self.length = length
        self.ratio = ratio
        self.r = lax.rem(f, ratio)
        g = lax.div(f, ratio)
        self.g = g
        self.core = lax.rem(g, 2)
        self.x = lax.rem(lax.div(g, 2), 2)
        self.y = lax.div(g, 4)
        self.gs = self.sib(g)
        self.gx = g + 2 - 4 * self.x
        self.gy = g + 4 - 8 * self.y
        self.gd = self.gx + 4 - 8 * self.y

    def sib(self, g):
        return g + 1 - 2 * self.core

    def dev(self, g, t):
        return (g * self.ratio + self.r, t)

    def order(self, i):
        half = self.length // 2
        step = 1 - 2 * lax.div(self.t, half)
        return lax.rem(self.t + i * step + self.length, self.length)


def remote(src, dst, send, recv, dev):
    return pltpu.make_async_remote_copy(
        src_ref=src, dst_ref=dst, send_sem=send, recv_sem=recv, device_id=dev, device_id_type=MESH
    )


def enter(place, partners):
    barrier = pltpu.get_barrier_semaphore()
    count = 0
    for cond, dev in partners:
        if cond is None:
            pl.semaphore_signal(barrier, inc=1, device_id=dev, device_id_type=MESH)
            count = count + 1
        else:

            @pl.when(cond)
            def _(dev=dev):
                pl.semaphore_signal(barrier, inc=1, device_id=dev, device_id_type=MESH)

            count = count + jnp.where(cond, 1, 0)
    pl.semaphore_wait(barrier, count)


def neighbours(place):
    g, t = place.g, place.t
    return [
        (None, place.dev(place.gs, t)),
        (None, place.dev(place.gx, t)),
        (None, place.dev(place.gy, t)),
        (t < place.length - 1, place.dev(g, t + 1)),
        (t > 0, place.dev(g, t - 1)),
    ]


def piece(kind, ref, g, t, n, half=None):
    size = n if half is None else n // 2
    off = 0 if half in (None, 0) else n // 2
    if kind == "q":
        return ref.at[:, t, pl.ds(aligned(g * n + off, size), size), :]
    if kind == "u":
        return ref.at[t, pl.ds(aligned(g * n + off, size), size), :]
    if kind in ("o", "d"):
        return ref.at[g, pl.ds(aligned(t * n + off, size), size), :]
    return ref.at[g, t, pl.ds(off, size), :]


class Gather:
    def __init__(self, place, index, kind, shard, full, n, sems, lined=False):
        self.p, self.a, self.kind, self.shard, self.full, self.n = place, index, kind, shard, full, n
        self.s_z, self.s_xy, self.s_sib, self.r_z, self.r_xy, self.r_sib, self.loc = sems
        self.lined = lined

    def view(self, g, o, half=None):
        return piece(self.kind, self.full, g, o, self.n, half)

    def put(self, src, g, o, half, send, recv, dev):
        return remote(src, self.view(g, o, half), send, recv, dev)

    def c_up(self, src, o, far=0):
        p = self.p
        g = p.gd if far else p.g
        return self.put(src, g, o, None, self.s_z.at[self.a, far, 0, o], self.r_z.at[self.a, far, o], p.dev(p.g, p.t + 1))

    def c_down(self, src, o, far=0):
        p = self.p
        g = p.gd if far else p.g
        return self.put(src, g, o, None, self.s_z.at[self.a, far, 1, o], self.r_z.at[self.a, far, o], p.dev(p.g, p.t - 1))

    def c_xy(self, src, which, o):
        p = self.p
        g = (p.g, p.g, p.gx, p.gy)[which]
        half = (None, None, 0, 1)[which]
        to = (p.gx, p.gy, p.gy, p.gx)[which]
        return self.put(src, g, o, half, self.s_xy.at[self.a, which, o], self.r_xy.at[self.a, which, o], p.dev(to, p.t))

    def c_sib(self, src, which, o):
        p = self.p
        g = (p.g, p.gx, p.gy, p.gd, p.gd)[which]
        half = (None, None, None, None if self.lined else 0, 1)[which]
        return self.put(src, g, o, half, self.s_sib.at[self.a, which, o], self.r_sib.at[self.a, which, o], p.dev(p.gs, p.t))

    def own(self):
        p = self.p
        src, t = self.shard, p.t
        pltpu.make_async_copy(src, self.view(p.g, t), self.loc.at[self.a]).start()

        @pl.when(t < p.length - 1)
        def _():
            self.c_up(src, t).start()

        @pl.when(t > 0)
        def _():
            self.c_down(src, t).start()

        self.c_xy(src, 0, t).start()
        self.c_xy(src, 1, t).start()
        self.c_sib(src, 0, t).start()

    def spread(self, o):
        src = self.view(self.p.g, o)
        self.c_xy(src, 0, o).start()
        self.c_xy(src, 1, o).start()
        self.c_sib(src, 0, o).start()

    def z(self, d, far=0):
        p = self.p
        t, last = p.t, p.length - 1
        g = p.gd if far else p.g

        def take(o, copy, cond):
            src = self.view(g, o)
            copy(src, o, far).wait_recv()

            @pl.when(cond)
            def _():
                copy(src, o, far).start()

            if far:
                self.c_sib(src, 3, o).start()
            else:
                self.spread(o)

        @pl.when(t - d >= 0)
        def _():
            take(t - d, self.c_up, t < last)

        @pl.when(t + d <= last)
        def _():
            take(t + d, self.c_down, t > 0)

    def corner(self):
        p = self.p
        t, last = p.t, p.length - 1
        self.wait_xy(2, p.gd, t, 0)
        self.wait_xy(3, p.gd, t, 1)
        src = self.view(p.gd, t)

        @pl.when(t < last)
        def _():
            self.c_up(src, t, 1).start()

        @pl.when(t > 0)
        def _():
            self.c_down(src, t, 1).start()

        self.c_sib(src, 3, t).start()

    def side(self, which, i):
        p = self.p
        o = p.order(i)
        g = (p.gx, p.gy)[which]
        full = self.view(g, o)
        self.wait_xy(which, g, o, None)
        if i == 0 or not self.lined:
            self.c_xy(self.view(g, o, which), 2 + which, o).start()
        self.c_sib(full, 1 + which, o).start()

    def wait_xy(self, which, g, o, half):
        v = self.view(g, o, half)
        p = self.p
        remote(v, v, self.s_xy.at[self.a, which, o], self.r_xy.at[self.a, which, o], p.dev(p.gx, p.t)).wait_recv()

    def diag(self, which, i):
        p = self.p
        o = p.order(i)
        self.wait_xy(2 + which, p.gd, o, which)
        self.c_sib(self.view(p.gd, o, which), 3 + which, o).start()

    def finish(self):
        p = self.p

        @pl.loop(0, p.length)
        def _(o):
            for which in range(4 if self.lined else 5):
                g = p.sib((p.g, p.gx, p.gy, p.gd, p.gd)[which])
                half = (None, None, None, None if self.lined else 0, 1)[which]
                v = self.view(g, o, half)
                remote(v, v, self.s_sib.at[self.a, which, o], self.r_sib.at[self.a, which, o], p.dev(p.gs, p.t)).wait_recv()

        pltpu.make_async_copy(self.shard, self.view(p.g, p.t), self.loc.at[self.a]).wait()

    def drain(self):
        p = self.p

        @pl.loop(0, p.length)
        def _(o):
            src = self.view(p.g, o)

            for far in (0, 1) if self.lined else (0,):

                @pl.when(jnp.logical_and(o <= p.t, p.t < p.length - 1))
                def _():
                    self.c_up(src, o, far).wait_send()

                @pl.when(jnp.logical_and(o >= p.t, p.t > 0))
                def _():
                    self.c_down(src, o, far).wait_send()

            self.c_xy(src, 0, o).wait_send()
            self.c_xy(src, 1, o).wait_send()
            if not self.lined:
                self.c_xy(self.view(p.gx, o, 0), 2, o).wait_send()
                self.c_xy(self.view(p.gy, o, 1), 3, o).wait_send()
            for which in range(4 if self.lined else 5):
                g = (p.g, p.gx, p.gy, p.gd, p.gd)[which]
                half = (None, None, None, None if self.lined else 0, 1)[which]
                self.c_sib(self.view(g, o, half), which, o).wait_send()

        if self.lined:
            self.c_xy(self.view(p.gx, p.t, 0), 2, p.t).wait_send()
            self.c_xy(self.view(p.gy, p.t, 1), 3, p.t).wait_send()

    def line(self):
        for d in range(1, self.p.length):
            yield self.z(d)

    def sides(self):
        for i in range(self.p.length):
            yield self.side(0, i)
            yield self.side(1, i)
            if i == 0 and self.lined:
                yield self.corner()

    def last(self):
        if self.lined:
            for d in range(1, self.p.length):
                yield self.z(d, 1)
        else:
            for i in range(self.p.length):
                yield self.diag(0, i)
                yield self.diag(1, i)


def gather_sems(arrays, length):
    dma = pltpu.SemaphoreType.DMA
    return [
        dma((arrays, 2, 2, length)),
        dma((arrays, 4, length)),
        dma((arrays, 5, length)),
        dma((arrays, 2, length)),
        dma((arrays, 4, length)),
        dma((arrays, 5, length)),
        dma((arrays,)),
    ]


def step(gen, count=1):
    for _ in range(count):
        next(gen, None)


def chain(*gens):
    for g in gens:
        yield from g


def blend(*gens):
    gens = list(gens)
    while gens:
        for g in list(gens):
            try:
                yield next(g)
            except StopIteration:
                gens.remove(g)


def row_loop(rows, step, body):
    full = rows // step

    @pl.loop(0, full)
    def _(i):
        body(pl.ds(aligned(i * step, step), step))

    for r in range(full * step, rows, 16):
        body(pl.ds(r, 16))


class Images:
    def __init__(self, place, src, dst, stage, flat, sems, seq):
        self.p, self.src, self.dst, self.stage, self.flat, self.sems, self.seq = place, src, dst, stage, flat, sems, seq
        self.per = dst.shape[1] // 128 * place.length
        self.chunk = stage.shape[1] // self.per
        self.full = seq // self.chunk

    def fetch(self, i):
        n = self.chunk * self.per
        return pltpu.make_async_copy(self.src.at[pl.ds(aligned(i * n, n), n)], self.stage.at[lax.rem(i, 2)], self.sems.at[lax.rem(i, 2)])

    def start(self):
        self.fetch(0).start()

    def spread(self, row, tokens):
        length = self.p.length
        for j in range(self.per // length):
            got = self.flat[pl.ds(j * length + self.p.t, tokens, stride=self.per), :]
            self.dst[pl.ds(aligned(row, 16), tokens), j * 128 : (j + 1) * 128] = got.astype(bf16)

    def run(self):
        @pl.loop(0, self.full)
        def _(i):
            @pl.when(i + 1 < self.full)
            def _():
                self.fetch(i + 1).start()

            self.fetch(i).wait()
            self.flat[...] = self.stage[lax.rem(i, 2)].astype(f32)
            self.spread(i * self.chunk, self.chunk)

        done, rows = self.full * self.chunk, self.dst.shape[0]
        left = (self.seq - done) * self.per
        if left:
            c = pltpu.make_async_copy(self.src.at[pl.ds(done * self.per, left)], self.stage.at[0, pl.ds(0, left)], self.sems.at[0])
            c.start()
            self.flat[...] = jnp.zeros_like(self.flat)
            c.wait()
            self.flat[0:left, :] = self.stage[0, 0:left, :].astype(f32)
        else:
            self.flat[...] = jnp.zeros_like(self.flat)
        if rows > done:
            self.spread(done, rows - done)


def statistics(tokens):
    average = jnp.mean(tokens, axis=-1, keepdims=True)
    centred = tokens - average
    inverse = lax.rsqrt(jnp.mean(centred * centred, axis=-1, keepdims=True) + epsilon)
    return centred * inverse, inverse


def nt(a, b):
    return lax.dot_general(a, b, (((1,), (1,)), ((), ())), preferred_element_type=f32)


def tn(a, b):
    return lax.dot_general(a, b, (((0,), (0,)), ((), ())), preferred_element_type=f32)


def nn(a, b):
    return jnp.dot(a, b, preferred_element_type=f32)


def wide(ref, lead, rows=slice(None)):
    return jnp.concatenate([ref[i, rows, :] for i in lead], axis=1)


def store_out(copies, src, dst, sem):
    c = pltpu.make_async_copy(src, dst, sem)
    c.start()
    copies.append(c)


PLAN = (
    ("w", "s"), ("w", "u"), ("s", "s", 1, 0), ("z", "s", 1), ("w", "q"), ("s", "u", 0, 0), ("s", "u", 1, 0), ("z", "s", 2),
    ("g", "s", 1, 0), ("gx",), ("s", "s", 1, 1), ("z", "s", 3), ("z", "q", 1), ("s", "s", 1, 3), ("s", "s", 1, 2),
    ("s", "s", 0, 3), ("s", "s", 0, 0), ("s", "s", 0, 2), ("z", "q", 2), ("gc",), ("s", "q", 1, 0), ("s", "s", 0, 1),
    ("k", "u"), ("g", "s", 0, 2), ("s", "q", 0, 1), ("g", "s", 1, 1), ("g", "s", 1, 3), ("g", "s", 0, 3), ("s", "q", 0, 0),
    ("s", "q", 1, 1), ("z", "q", 3), ("w", "o"), ("g", "s", 1, 2), ("g", "s", 0, 1), ("s", "q", 0, 2), ("g", "s", 0, 0),
    ("f", "u", 1), ("s", "q", 0, 3), ("g", "q", 1, 1), ("s", "q", 1, 2), ("s", "q", 1, 3), ("g", "q", 0, 0),
    ("g", "q", 1, 0), ("z", "o", 1), ("n", "s"), ("g", "q", 0, 1), ("w", "d"), ("ln",), ("g", "q", 0, 2), ("g", "q", 1, 2),
    ("g", "q", 0, 3), ("g", "q", 1, 3), ("z", "o", 2), ("z", "u", 1), ("n", "q"), ("qkv",), ("qkv",), ("s", "o", 0, 1),
    ("qkv",), ("s", "o", 0, 0), ("f", "u", 2), ("att",), ("z", "o", 3), ("s", "o", 1, 1), ("s", "o", 1, 0), ("s", "o", 1, 2),
    ("s", "d", 0, 0), ("att",), ("s", "o", 0, 2), ("s", "d", 1, 0), ("z", "u", 2), ("att",), ("s", "o", 1, 3),
    ("s", "o", 0, 3), ("z", "d", 1), ("att",), ("s", "u", 1, 1), ("att",), ("k", "d"), ("z", "u", 3), ("g", "o", 1, 2),
    ("att",), ("z", "d", 2), ("g", "o", 1, 0), ("att",), ("g", "o", 0, 0), ("f", "u", 3), ("g", "o", 0, 3), ("f", "d", 1),
    ("g", "o", 1, 3), ("g", "o", 0, 2), ("g", "o", 1, 1), ("g", "o", 0, 1), ("s", "u", 1, 2), ("att",), ("s", "u", 0, 2),
    ("s", "u", 0, 3), ("s", "u", 0, 1), ("s", "u", 1, 3), ("n", "o"), ("mid",), ("z", "d", 3), ("lm",), ("n", "u"),
    ("gelu",), ("s", "d", 1, 1), ("f", "d", 2), ("s", "d", 0, 1), ("gelu",), ("gelu",), ("gelu",), ("s", "d", 1, 3),
    ("s", "d", 1, 2), ("gelu",), ("s", "d", 0, 2), ("gelu",), ("f", "d", 3), ("s", "d", 0, 3), ("gelu",), ("gelu",),
    ("n", "d"), ("down",),
)


def forward_kernel(ratio, length, seq, x_i, ct_i, mask, s_s, q_s, o_s, u_s, d_s,
                   vec_o, wq_o, wo_o, wu_o, wd_o, hid1_o, qkv_o, att_o, lse_o, mid_o, hid2_o, act_o, g_o, out_o, x_o, ct_o,
                   ws, wq, wo, wu, wd, smf, vec, hid1, qkv, att, lse, mid, hid2, act, gg, pre, outb, x, ct, stage, flat,
                   s_z, s_xy, s_sib, r_z, r_xy, r_sib, loc, outs, ins):
    place = Place(ratio, length)
    rows, width = hid1.shape
    keys = qkv.shape[1]
    hidden = act.shape[1]
    sems = (s_z, s_xy, s_sib, r_z, r_xy, r_sib, loc)
    small = Gather(place, 0, "s", s_s, ws, s_s.shape[0], sems)
    gq = Gather(place, 1, "q", q_s, wq, q_s.shape[1], sems)
    go = Gather(place, 2, "o", o_s, wo, o_s.shape[0], sems)
    gu = Gather(place, 3, "u", u_s, wu, u_s.shape[0], sems, True)
    gd = Gather(place, 4, "d", d_s, wd, d_s.shape[0], sems, True)
    everything = (small, gq, go, gu, gd)
    enter(place, neighbours(place))
    gx = Images(place, x_i, x, stage, flat, ins, seq)
    gc = Images(place, ct_i, ct, stage, flat, ins, seq)
    gx.start()
    gathers = {"s": small, "q": gq, "o": go, "u": gu, "d": gd}
    full = {"q": (wq, wq_o, 1), "o": (wo, wo_o, 5), "u": (wu, wu_o, 8), "d": (wd, wd_o, 11)}
    copies = []

    def act_on(ev):
        g = gathers[ev[1]]
        if ev[0] == "w":
            g.own()
        elif ev[0] == "z":
            g.z(ev[2])
        elif ev[0] == "f":
            g.z(ev[2], 1)
        elif ev[0] == "s":
            g.side(ev[2], ev[3])
        elif ev[0] == "k":
            g.corner()
        elif ev[0] == "g":
            g.diag(ev[2], ev[3])
        else:
            g.finish()
            if ev[1] in full:
                src, dst, i = full[ev[1]]
                store_out(copies, src, dst, outs.at[i])

    events = list(PLAN)

    def until(name):
        while events[0][0] != name:
            act_on(events.pop(0))
        events.pop(0)

    until("gx")
    gx.run()
    store_out(copies, x, x_o, outs.at[14])
    until("gc")
    gc.start()
    gc.run()
    store_out(copies, ct, ct_o, outs.at[15])
    until("ln")

    for g in range(GROUPS):
        for t in range(length):
            smf[g, t] = ws[g, t].astype(f32)
    per = width // GROUPS
    for row in range(6):
        vec[row : row + 1, 0:width] = jnp.concatenate([smf[g, 0, row : row + 1, :] for g in range(GROUPS)], axis=1)
    local = width // length
    for c in range(2):
        parts = []
        for t in range(length):
            for j in range(local // 128):
                r = 6 + c * (local // 128) + j
                parts.append(smf[0, t, r : r + 1, :])
        vec[6 + c : 7 + c, 0:width] = jnp.concatenate(parts, axis=1)
    base = 6 + 2 * (local // 128)
    nh = hidden // length // 128
    for t in range(length):
        vec[8 : 9, t * (hidden // length) : (t + 1) * (hidden // length)] = jnp.concatenate(
            [smf[0, t, base + j : base + j + 1, :] for j in range(nh)], axis=1
        )
    store_out(copies, vec, vec_o, outs.at[13])

    gain, shift = vec[0:1, 0:width], vec[2:3, 0:width]

    def norm_one(r):
        n, _inv = statistics(x[r, :].astype(f32))
        hid1[r, :] = (n * gain + shift).astype(bf16)

    row_loop(rows, 32, norm_one)
    store_out(copies, hid1, hid1_o, outs.at[0])
    qkv[:, rows:keys, :] = jnp.zeros((3, keys - rows, width), bf16)
    scale = HEAD ** (-0.5)
    for c in range(3):
        until("qkv")
        r = nn(hid1[...], wide(wq.at[c], range(length)))
        if c == 0:
            r = (r + vec[6:7, 0:width]).astype(bf16) * jnp.asarray(scale, bf16)
        elif c == 2:
            r = (r + vec[7:8, 0:width]).astype(bf16)
        else:
            r = r.astype(bf16)
        qkv[c, 0:rows, :] = r
    store_out(copies, qkv, qkv_o, outs.at[2])

    pairs = width // 128
    low = lax.broadcasted_iota(jnp.int32, (128, 128), 1) < HEAD

    def attend(p):
        cols = pl.ds(aligned(p * 128, 128), 128)
        k2 = qkv[1, :, cols]
        v2 = qkv[2, :, cols]
        for r0 in range(0, keys, 128):
            n = min(128, rows - r0)
            q2 = qkv[0, r0 : r0 + 128, cols]
            done = []
            for h in range(2):
                mine = low if h == 0 else jnp.logical_not(low)
                s = nt(jnp.where(mine, q2, jnp.zeros_like(q2)), k2) + mask[...]
                m = jnp.max(s, axis=-1, keepdims=True)
                e = jnp.exp(s - m)
                total = jnp.sum(e, axis=-1, keepdims=True)
                done.append(nn(e.astype(bf16), v2) * (1.0 / total))
                flat = jnp.transpose(jnp.broadcast_to(m + jnp.log(total), (128, 128)))
                lse[p, h : h + 1, r0 : r0 + 128] = flat[0:1, :]
            a2 = jnp.where(low, done[0], done[1]).astype(bf16)
            att[r0 : r0 + n, cols] = a2[0:n, :]

    until("att")
    between = [[] for _ in range(pairs)]
    for k in range(pairs - 1):
        while events[0][0] != "att":
            between[k].append(events.pop(0))
        events.pop(0)

    @pl.loop(0, pairs)
    def _(j):
        attend(j)
        for k in range(pairs):
            if between[k]:

                @pl.when(j == k)
                def _():
                    for ev in between[k]:
                        act_on(ev)

    store_out(copies, att, att_o, outs.at[3])
    store_out(copies, lse, lse_o, outs.at[4])

    until("mid")
    mid[...] = nn(att[...], wide(wo, range(GROUPS))) + vec[4:5, 0:width]
    until("lm")
    gain2, shift2 = vec[1:2, 0:width], vec[3:4, 0:width]

    def norm_two(r):
        m = x[r, :].astype(f32) + mid[r, :]
        mid[r, :] = m
        n, _inv = statistics(m)
        hid2[r, :] = (n * gain2 + shift2).astype(bf16)

    row_loop(rows, 32, norm_two)
    store_out(copies, mid, mid_o, outs.at[6])
    store_out(copies, hid2, hid2_o, outs.at[7])

    part = pre.shape[1]
    for t in range(hidden // part):
        until("gelu")
        cols = slice(t * part, (t + 1) * part)
        each = wu.shape[2]
        blk, off = (t * part) // each, (t * part) % each
        pre[...] = nn(hid2[...], wu[blk, :, off : off + part])

        def gelu(r):
            z = pre[r, :] + vec[8:9, cols]
            cdf = 0.5 * (1.0 + lax.erf(z * half_root))
            act[r, cols] = (z * cdf).astype(bf16)
            gg[r, cols] = (cdf + z * (jnp.exp(-0.5 * z * z) * density_scale)).astype(bf16)

        row_loop(rows, 32, gelu)

    store_out(copies, act, act_o, outs.at[9])
    store_out(copies, gg, g_o, outs.at[10])
    until("down")

    for j in range(GROUPS // 2):
        cols = slice(2 * j * per, 2 * (j + 1) * per)
        r = nn(act[...], wide(wd, (2 * j, 2 * j + 1)))
        outb[:, cols] = (mid[:, cols] + (r + vec[5:6, cols])).astype(bf16)
    store_out(copies, outb, out_o.at[place.t], outs.at[12])
    for a in everything:
        a.drain()
    for c in copies:
        c.wait()


def any_spec():
    return pl.BlockSpec(memory_space=pl.ANY)


def vmem_spec():
    return pl.BlockSpec(memory_space=pltpu.VMEM)


def forward(ratio, length, seq, width, x_i, ct_i, mask, small, q_s, o_s, u_s, d_s):
    rows = -(-seq // 16) * 16
    keys = mask.shape[1]
    hidden = u_s.shape[1] * length
    sds = jax.ShapeDtypeStruct
    n_q, n_o, n_u, n_d = q_s.shape[1], o_s.shape[0], u_s.shape[0], d_s.shape[0]
    wq = ((3, length, GROUPS * n_q, q_s.shape[2]), bf16)
    wo = ((GROUPS, length * n_o, o_s.shape[1]), bf16)
    wu = ((length, GROUPS * n_u, u_s.shape[1]), bf16)
    wd = ((GROUPS, length * n_d, d_s.shape[1]), bf16)
    pairs = width // 128
    vec = ((16, hidden), f32)
    hid = ((rows, width), bf16)
    qkv = ((3, keys, width), bf16)
    lse = ((pairs, 8, keys), f32)
    mid = ((rows, width), f32)
    act = ((rows, hidden), bf16)
    outs = [vec, wq, wo, wu, wd, hid, qkv, hid, lse, mid, hid, act, act, ((length, rows, width), bf16), hid, hid]
    chunk = 64 * length * width // 128
    scratch = [((GROUPS, length) + small.shape, bf16), wq, wo, wu, wd, ((GROUPS, length) + small.shape, f32), vec,
               hid, qkv, hid, lse, mid, hid, act, act, ((rows, 512), f32), hid, hid, hid,
               ((2, chunk, 128), bf16), ((chunk, 128), f32)]
    return pl.pallas_call(
        functools.partial(forward_kernel, ratio, length, seq),
        out_shape=[sds(*o) for o in outs],
        in_specs=[any_spec(), any_spec(), vmem_spec()] + [any_spec()] * 5,
        out_specs=[any_spec()] * len(outs),
        scratch_shapes=[pltpu.VMEM(*s) for s in scratch] + gather_sems(5, length) + [pltpu.SemaphoreType.DMA((16,)), pltpu.SemaphoreType.DMA((2,))],
        compiler_params=pltpu.CompilerParams(collective_id=0, has_side_effects=True, vmem_limit_bytes=VMEM_LIMIT),
        name="forward",
    )(x_i, ct_i, mask, small, q_s, o_s, u_s, d_s)


def prepare(length, inputs, lengths, norm_gains, norm_shifts, w_qkv, bias_qv, w_out, out_bias, w_up, b_up, w_down, cotangent, fsdp):
    ratio = fsdp // GROUPS
    if ratio > 1:
        groups = [[g * ratio + r for r in range(ratio)] for g in range(GROUPS)]

        def join(a, axis):
            return lax.all_gather(a, "fsdp", axis=axis, tiled=True, axis_index_groups=groups)

        norm_gains, norm_shifts, out_bias = join(norm_gains, 1), join(norm_shifts, 1), join(out_bias, 1)
        w_qkv, w_out, w_up, w_down = join(w_qkv, 1), join(w_out, 1), join(w_up, 0), join(w_down, 1)
    t = lax.axis_index("tensor")
    batch, seq, width = inputs.shape
    keys = -(-seq // 128) * 128

    def flat(a):
        return a.reshape(batch, seq, width // 128, 128).transpose(1, 2, 0, 3).reshape(-1, 128)

    count = lax.dynamic_index_in_dim(lengths, t, 0, keepdims=False)
    mask = jnp.where(jnp.arange(keys) < count, 0.0, -jnp.inf).astype(f32)
    small = jnp.concatenate(
        [norm_gains, norm_shifts, out_bias, bias_qv.reshape(-1, 128), b_up.reshape(-1, 128)], axis=0
    )
    small = jnp.pad(small, ((0, 32 - small.shape[0]), (0, 0)))
    return ratio, flat(inputs), flat(cotangent), mask, small, w_qkv, w_out, w_up, w_down


class Line:
    def __init__(self, place, full, send, recv):
        self.p, self.full, self.send, self.recv = place, full, send, recv

    def up(self, src, o):
        p = self.p
        return remote(src, self.full.at[o], self.send.at[0, o], self.recv.at[o], p.dev(p.g, p.t + 1))

    def down(self, src, o):
        p = self.p
        return remote(src, self.full.at[o], self.send.at[1, o], self.recv.at[o], p.dev(p.g, p.t - 1))

    def pass_on(self, d, src=None):
        p = self.p
        t, last = p.t, p.length - 1

        @pl.when(jnp.logical_and(t - d >= 0, t < last))
        def _():
            o = t - d
            self.up(self.full.at[o] if src is None else src, o).start()

        @pl.when(jnp.logical_and(t + d <= last, t > 0))
        def _():
            o = t + d
            self.down(self.full.at[o] if src is None else src, o).start()

    def arrive(self, d):
        p = self.p
        t, last = p.t, p.length - 1

        @pl.when(t - d >= 0)
        def _():
            self.up(self.full.at[t - d], t - d).wait_recv()

        @pl.when(t + d <= last)
        def _():
            self.down(self.full.at[t + d], t + d).wait_recv()

    def drain(self, d, src=None):
        p = self.p
        t, last = p.t, p.length - 1

        @pl.when(jnp.logical_and(t - d >= 0, t < last))
        def _():
            self.up(self.full.at[t - d] if src is None else src, t - d).wait_send()

        @pl.when(jnp.logical_and(t + d <= last, t > 0))
        def _():
            self.down(self.full.at[t + d] if src is None else src, t + d).wait_send()


def add_into(dst, src):
    shape = dst.shape
    n = shape[-2]
    lead = 1
    for s in shape[:-2]:
        lead *= s
    rows = min(n, 65536 // shape[-1])
    per = n // rows

    @pl.loop(0, lead * per)
    def _(i):
        r = pl.ds(aligned(lax.rem(i, per) * rows, rows), rows)
        j = lax.div(i, per)
        idx = []
        for s in reversed(shape[:-2]):
            idx.append(lax.rem(j, s))
            j = lax.div(j, s)
        idx = tuple(reversed(idx)) + (r, slice(None))
        dst[idx] = dst[idx] + src[idx]


class Scatter:
    def __init__(self, place, index, owner, plane, bufs, lines, sems):
        self.p, self.a, self.o, self.plane = place, index, owner, plane
        self.ra, self.rb, self.xa, self.xb = bufs
        self.below, self.above = lines
        self.send, self.recv, self.l_send, self.l_recv = sems

    def half(self, k, h):
        n = self.plane.shape[-2] // 2
        r = pl.ds(h * n, n)
        return self.plane.at[k, r, :] if len(self.plane.shape) == 3 else self.plane.at[k, :, r, :]

    def k(self):
        return self.p.y * 2 + self.p.x

    def block(self):
        return self.plane.at[self.k()]

    def copy(self, slot, src, dst, dev):
        return remote(src, dst, self.send.at[self.a, slot], self.recv.at[self.a, slot], dev)

    def stage(self, slot):
        p = self.p
        ox, oy = 1 - p.x, 1 - p.y
        to_x, to_y = p.dev(p.gx, p.t), p.dev(p.gy, p.t)
        if slot == 0:
            return self.copy(0, self.half(oy * 2 + ox, 0), self.ra.at[0], to_y)
        if slot == 1:
            return self.copy(1, self.half(oy * 2 + p.x, 0), self.ra.at[1], to_y)
        if slot == 2:
            return self.copy(2, self.half(oy * 2 + ox, 1), self.rb.at[0], to_x)
        if slot == 3:
            return self.copy(3, self.half(p.y * 2 + ox, 1), self.rb.at[1], to_x)
        if slot == 4:
            return self.copy(4, self.half(p.y * 2 + ox, 0), self.xa, to_x)
        return self.copy(5, self.half(oy * 2 + p.x, 1), self.xb, to_y)

    def first(self):
        for slot in (0, 2, 1, 3):
            self.stage(slot).start()

    def cross_x(self):
        p = self.p
        self.stage(0).wait_recv()
        add_into(self.half(p.y * 2 + 1 - p.x, 0), self.ra.at[0])
        self.stage(4).start()

    def cross_y(self):
        p = self.p
        self.stage(2).wait_recv()
        add_into(self.half((1 - p.y) * 2 + p.x, 1), self.rb.at[0])
        self.stage(5).start()

    def join(self):
        self.stage(1).wait_recv()
        add_into(self.half(self.k(), 0), self.ra.at[1])
        self.stage(3).wait_recv()
        add_into(self.half(self.k(), 1), self.rb.at[1])

    def meet(self):
        self.stage(4).wait_recv()
        add_into(self.half(self.k(), 0), self.xa)
        self.stage(5).wait_recv()
        add_into(self.half(self.k(), 1), self.xb)

    def up(self):
        p = self.p
        return remote(self.block(), self.below, self.l_send.at[self.a], self.l_recv.at[self.a, 0], p.dev(p.g, p.t + 1))

    def down(self):
        p = self.p
        return remote(self.block(), self.above, self.l_send.at[self.a], self.l_recv.at[self.a, 1], p.dev(p.g, p.t - 1))

    def hop(self, h):
        p = self.p
        t, last = p.t, p.length - 1
        if h < self.o:

            @pl.when(t == h)
            def _():
                if h > 0:
                    self.up().wait_recv()
                    add_into(self.block(), self.below)
                self.up().start()

        if last - h > self.o:

            @pl.when(t == last - h)
            def _():
                if h > 0:
                    self.down().wait_recv()
                    add_into(self.block(), self.above)
                self.down().start()

    def final(self, out, sem):
        p = self.p

        @pl.when(p.t == self.o)
        def _():
            if self.o > 0:
                self.up().wait_recv()
                add_into(self.block(), self.below)
            if self.o < p.length - 1:
                self.down().wait_recv()
                add_into(self.block(), self.above)
            pltpu.make_async_copy(self.block(), out, sem).start()

    def drain(self, out, sem):
        p = self.p
        for slot in range(6):
            self.stage(slot).wait_send()

        @pl.when(p.t < self.o)
        def _():
            self.up().wait_send()

        @pl.when(p.t > self.o)
        def _():
            self.down().wait_send()

        @pl.when(p.t == self.o)
        def _():
            pltpu.make_async_copy(self.block(), out, sem).wait()


def load(src, dst, sem):
    c = pltpu.make_async_copy(src, dst, sem)
    c.start()
    return c


def back_kernel(ratio, length, vec_i, wd_i, wu_i, wo_i, wq_i, g_i, mid_i, ct_i, x_i, qkv_i, att_i, lse_i, maskc_i, all_i,
                all_o, dpre_o, dqkv_o, dmb_o, gi_o, sums_o,
                vec, wd, wu, wo, wq, gg, mid, ct, x, qkv, att, lse, maskc, acc, dmb, da, gi, sums, red,
                line_s, line_r, ins, outs):
    place = Place(ratio, length)
    rows, width = ct.shape
    keys = qkv.shape[1]
    each = wu.shape[2]
    enter(place, neighbours(place))
    line = Line(place, all_o, line_s, line_r)
    line.pass_on(0)
    writes = []

    def block(t):
        return pl.ds(t * each, each)

    l_ct = load(ct_i, ct, ins.at[0])
    l_g, l_wd, l_wu = [], [], []
    for t in range(length):
        l_g.append(load(g_i.at[:, block(t)], gg.at[:, block(t)], ins.at[1 + t]))
        l_wd.append(load(wd_i.at[:, block(t), :], wd.at[:, block(t), :], ins.at[1 + length + t]))
        l_wu.append(load(wu_i.at[t], wu.at[t], ins.at[1 + 2 * length + t]))
    base = 1 + 3 * length
    names = [(vec_i, vec), (mid_i, mid), (wo_i, wo), (att_i, att.at[pl.ds(0, rows)]), (lse_i, lse), (qkv_i, qkv),
             (maskc_i, maskc), (wq_i, wq), (x_i, x)]
    loads = [load(a, b, ins.at[base + i]) for i, (a, b) in enumerate(names)]
    sums[...] = jnp.zeros_like(sums)
    red[...] = jnp.zeros_like(red)
    da[rows:keys, :] = jnp.zeros((keys - rows, width), bf16)
    att[rows:keys, :] = jnp.zeros((keys - rows, width), bf16)

    l_ct.wait()
    for t in range(length):
        cols = slice(t * each, (t + 1) * each)
        l_wd[t].wait()
        l_g[t].wait()
        d = nt(ct[...], wide(wd, range(GROUPS), cols)) * gg[:, cols].astype(f32)
        sums[8 + t : 9 + t, :] = jnp.sum(d, axis=0, keepdims=True)
        gg[:, cols] = d.astype(bf16)
        store_out(writes, gg.at[:, block(t)], dpre_o.at[:, block(t)], outs.at[5 + t])
        l_wu[t].wait()
        part = nt(gg[:, cols], wu[t])
        if t == 0:
            acc[...] = part
        else:
            acc[...] += part
    for c in loads[0:2]:
        c.wait()
    gain = vec[1:2, 0:width]

    def norm_two(r):
        n, inverse = statistics(mid[r, :])
        dh = acc[r, :]
        e = dh * gain
        c = ct[r, :].astype(f32)
        dm = c + inverse * (e - jnp.mean(e, axis=-1, keepdims=True) - n * jnp.mean(e * n, axis=-1, keepdims=True))
        mid[r, :] = dm
        dmb[r, :] = dm.astype(bf16)
        for j, v in enumerate((dh * n, dh, dm, c)):
            red[j] += sum(v[i : i + 8] for i in range(0, v.shape[0], 8))

    row_loop(rows, 32, norm_two)
    for j, row in enumerate((1, 3, 4, 5)):
        sums[row : row + 1, :] = jnp.sum(red[j], axis=0, keepdims=True)
    red[...] = jnp.zeros_like(red)
    store_out(writes, dmb, dmb_o, outs.at[0])
    line.arrive(1)
    line.pass_on(1)

    for c in loads[2:7]:
        c.wait()
    da[0:rows, :] = nt(dmb[...], wide(wo, range(GROUPS))).astype(bf16)
    pairs = width // 128
    scale = HEAD ** (-0.5)

    def back(p):
        cols = pl.ds(aligned(p * 128, 128), 128)
        k2 = qkv[1, :, cols]
        v2 = qkv[2, :, cols]
        low_k = lax.broadcasted_iota(jnp.int32, k2.shape, 1) < HEAD
        dk = [None, None]
        dv = [None, None]
        total = jnp.zeros((1, 128), f32)
        for r0, n in ((0, 256), (256, 256), (512, 128)):
            q2 = qkv[0, r0 : r0 + n, cols]
            da2 = da[r0 : r0 + n, cols]
            prod = da2.astype(f32) * att[r0 : r0 + n, cols].astype(f32)
            low = lax.broadcasted_iota(jnp.int32, (n, 128), 1) < HEAD
            mc = jnp.concatenate([maskc[...]] * (n // 128), axis=1)
            dq = []
            for h in range(2):
                mine = low if h == 0 else jnp.logical_not(low)
                mine_k = low_k if h == 0 else jnp.logical_not(low_k)
                delta = jnp.sum(jnp.where(mine, prod, 0.0), axis=-1, keepdims=True)
                delta = jnp.concatenate(
                    [jnp.transpose(jnp.broadcast_to(delta[i : i + 128], (128, 128)))[0:1, :] for i in range(0, n, 128)], axis=1
                )
                s = nt(jnp.where(mine_k, k2, jnp.zeros_like(k2)), q2)
                prob = jnp.exp(s + mc - lse[p, h : h + 1, r0 : r0 + n])
                dp = nt(jnp.where(mine_k, v2, jnp.zeros_like(v2)), da2)
                ds = (prob * (dp - delta)).astype(bf16)
                dq.append(tn(ds, k2))
                a, b = nn(ds, q2), nn(prob.astype(bf16), da2)
                dk[h] = a if dk[h] is None else dk[h] + a
                dv[h] = b if dv[h] is None else dv[h] + b
            d = jnp.where(low, dq[0], dq[1]) * scale
            total = total + jnp.sum(d, axis=0, keepdims=True)
            qkv[0, r0 : r0 + n, cols] = d.astype(bf16)
        v = jnp.where(low_k, dv[0], dv[1])
        qkv[1, :, cols] = jnp.where(low_k, dk[0], dk[1]).astype(bf16)
        qkv[2, :, cols] = v.astype(bf16)
        red[2, 0:1, cols] = total
        red[2, 1:2, cols] = jnp.sum(v, axis=0, keepdims=True)

    @pl.loop(0, pairs)
    def _(j):
        back(j)

        @pl.when(j == pairs - 2)
        def _():
            line.arrive(2)
            line.pass_on(2)

    store_out(writes, qkv, dqkv_o, outs.at[1])

    loads[7].wait()
    for c in range(3):
        part = nt(qkv[c, 0:rows, :], wide(wq.at[c], range(length)))
        if c == 0:
            acc[...] = part
        else:
            acc[...] += part
    loads[8].wait()
    gain1 = vec[0:1, 0:width]

    def norm_one(r):
        n, inverse = statistics(x[r, :].astype(f32))
        d = acc[r, :]
        e = d * gain1
        gi[r, :] = (
            mid[r, :] + inverse * (e - jnp.mean(e, axis=-1, keepdims=True) - n * jnp.mean(e * n, axis=-1, keepdims=True))
        ).astype(bf16)
        for j, v in enumerate((d * n, d)):
            red[j] += sum(v[i : i + 8] for i in range(0, v.shape[0], 8))

    row_loop(rows, 32, norm_one)
    store_out(writes, gi, gi_o.at[place.t], outs.at[2])
    sums[0:1, :] = jnp.sum(red[0], axis=0, keepdims=True)
    sums[2:3, :] = jnp.sum(red[1], axis=0, keepdims=True)
    sums[6:8, :] = red[2, 0:2, :]
    store_out(writes, sums, sums_o, outs.at[3])
    line.arrive(3)
    for d in range(length - 1):
        line.drain(d)
    for c in writes:
        c.wait()


def back(ratio, length, vec, wd, wu, wo, wq, g, mid, ct, x, qkv, att, lse, maskc, out_all):
    rows, width = ct.shape
    keys = qkv.shape[1]
    sds = jax.ShapeDtypeStruct
    sums = ((16, width), f32)
    tok, hid, tall = ((rows, width), f32), ((rows, width), bf16), ((keys, width), bf16)
    outs = [(out_all.shape, bf16), (g.shape, bf16), (qkv.shape, bf16), hid, (out_all.shape, bf16), sums]
    scratch = [(vec.shape, f32), (wd.shape, bf16), (wu.shape, bf16), (wo.shape, bf16), (wq.shape, bf16), (g.shape, bf16), tok, hid, hid,
               (qkv.shape, bf16), tall, (lse.shape, f32), (maskc.shape, f32), tok, hid, tall, hid, sums, ((4, 8, width), f32)]
    dma = pltpu.SemaphoreType.DMA
    return pl.pallas_call(
        functools.partial(back_kernel, ratio, length),
        out_shape=[sds(*o) for o in outs],
        in_specs=[any_spec()] * 14,
        out_specs=[any_spec()] * len(outs),
        scratch_shapes=[pltpu.VMEM(*s) for s in scratch] + [dma((2, length)), dma((length,)), dma((10 + 3 * length,)), dma((5 + length,))],
        input_output_aliases={13: 0},
        compiler_params=pltpu.CompilerParams(collective_id=1, has_side_effects=True, vmem_limit_bytes=VMEM_LIMIT),
        name="back",
    )(vec, wd, wu, wo, wq, g, mid, ct, x, qkv, att, lse, maskc, out_all)


GRADS = (
    ("c", "o", 0), ("c", "q", 3), ("t", "o", 0), ("c", "u", 3), ("b", "o", 0), ("a", "o", 0), ("t", "q", 3), ("t", "u", 3),
    ("c", "u", 2), ("t", "u", 2), ("b", "q", 3), ("c", "q", 0), ("t", "q", 0), ("a", "u", 3), ("b", "u", 3), ("c", "o", 1),
    ("c", "d", 0), ("P", 0), ("t", "d", 0), ("j", "u", 2), ("P", 1), ("t", "o", 1), ("c", "d", 1), ("j", "u", 3),
    ("b", "u", 2), ("L", 1), ("c", "u", 0), ("m", "u", 3), ("c", "q", 2), ("h", "u", 3, 0), ("a", "q", 3), ("P", 2),
    ("t", "d", 1), ("b", "d", 1), ("a", "q", 0), ("P", 3), ("b", "q", 0), ("a", "d", 1), ("j", "q", 3), ("j", "o", 0),
    ("c", "o", 3), ("b", "d", 0), ("a", "u", 2), ("t", "q", 2), ("m", "q", 3), ("a", "d", 0), ("j", "d", 1), ("t", "o", 3),
    ("t", "u", 0), ("j", "o", 1), ("j", "q", 0), ("m", "o", 0), ("h", "q", 3, 0), ("a", "o", 1), ("m", "d", 1),
    ("h", "d", 1, 0), ("h", "d", 1, 1), ("m", "q", 0), ("a", "q", 2), ("h", "q", 0, 0), ("b", "o", 1), ("c", "u", 1),
    ("L", 2), ("h", "q", 3, 1), ("m", "u", 2), ("h", "u", 2, 0), ("b", "q", 2), ("c", "d", 3), ("j", "q", 2), ("j", "d", 0),
    ("h", "o", 0, 0), ("j", "o", 3), ("m", "o", 1), ("b", "u", 0), ("h", "u", 3, 1), ("P", 4), ("h", "u", 2, 1),
    ("a", "u", 0), ("m", "q", 2), ("t", "d", 3), ("h", "q", 2, 0), ("c", "o", 2), ("h", "q", 2, 1), ("b", "o", 3),
    ("h", "o", 0, 1), ("a", "d", 3), ("P", 5), ("m", "d", 0), ("h", "o", 1, 0), ("h", "o", 0, 2), ("h", "q", 0, 1),
    ("a", "o", 3), ("t", "u", 1), ("h", "d", 0, 0), ("b", "d", 3), ("c", "d", 2), ("c", "q", 1), ("h", "q", 0, 2),
    ("m", "o", 3), ("a", "u", 1), ("h", "o", 3, 0), ("h", "o", 1, 1), ("h", "o", 3, 1), ("j", "u", 0), ("m", "u", 0),
    ("b", "u", 1), ("h", "u", 0, 0), ("h", "q", 3, 2), ("h", "d", 0, 1), ("h", "u", 3, 2), ("j", "d", 3), ("e", "u", 2),
    ("t", "d", 2), ("m", "d", 3), ("h", "d", 0, 2), ("h", "d", 3, 0), ("h", "u", 0, 1), ("j", "u", 1), ("b", "d", 2),
    ("m", "u", 1), ("e", "q", 2), ("a", "d", 2), ("h", "u", 1, 0), ("h", "d", 3, 1), ("h", "u", 0, 2), ("t", "q", 1),
    ("h", "o", 3, 2), ("j", "d", 2), ("m", "d", 2), ("e", "d", 1), ("e", "q", 0), ("h", "d", 2, 0), ("a", "q", 1),
    ("e", "q", 3), ("b", "q", 1), ("h", "d", 2, 1), ("h", "u", 1, 1), ("h", "d", 3, 2), ("e", "u", 3), ("j", "q", 1),
    ("t", "o", 2), ("m", "q", 1), ("h", "q", 1, 0), ("e", "o", 3), ("a", "o", 2), ("b", "o", 2), ("e", "d", 0),
    ("j", "o", 2), ("e", "o", 0), ("h", "q", 1, 1), ("e", "u", 0), ("m", "o", 2), ("h", "o", 2, 0), ("e", "u", 1),
    ("e", "o", 1), ("h", "o", 2, 1), ("e", "q", 1), ("e", "d", 2), ("e", "d", 3), ("L", 3), ("e", "o", 2),
)


def grads_kernel(ratio, length, act_i, ct_i, hid2_i, dpre_i, hid1_i, dqkv_i, att_i, dmb_i, sums_i, all_i,
                 all_o, od_o, ou_o, oo_o, oq_o, sums_o,
                 act, ct, hid2, dpre, hid1, dqkv, att, dmb, sums, got, *rest):
    kinds = ("d", "u", "q", "o")
    held = {k: rest[8 * i : 8 * (i + 1)] for i, k in enumerate(kinds)}
    line_s, line_r, core_s, core_r, sc_s, sc_r, ls_s, ls_r, sum_s, sum_r, ins, outs = rest[32:]
    place = Place(ratio, length)
    rows, width = ct.shape
    each = act.shape[1] // length
    t = place.t
    far = place.dev(place.g, t + 2 - 4 * lax.div(t, 2))
    near = place.dev(place.g, t + 1 - 2 * lax.rem(t, 2))
    enter(place, neighbours(place) + [(None, far)])
    line = Line(place, all_o, line_s, line_r)
    line.pass_on(0)
    loads = {}

    def block(o):
        return pl.ds(o * each, each)

    def fetch(name, a, b):
        loads[name] = load(a, b, ins.at[len(loads)])

    whole = {"d": (("ct", ct_i, ct),), "u": (("hid2", hid2_i, hid2),), "q": (("hid1", hid1_i, hid1), ("dqkv", dqkv_i, dqkv)),
             "o": (("att", att_i, att), ("dmb", dmb_i, dmb))}
    for ev in GRADS:
        if ev[0] == "c":
            k, o = ev[1:]
            for item in whole.pop(k, ()):
                fetch(*item)
            if k == "d":
                fetch((k, o), act_i.at[:, block(o)], act.at[:, block(o)])
            if k == "u":
                fetch((k, o), dpre_i.at[:, block(o)], dpre.at[:, block(o)])
    fetch("sums", sums_i, sums.at[0])
    seen = set()

    def ready(*keys):
        for key in keys:
            if key not in seen:
                seen.add(key)
                loads[key].wait()

    other = 1 - place.core
    units = [(k, o) for o in range(length) for k in kinds]
    out_of = {"d": od_o, "u": ou_o, "q": oq_o, "o": oo_o}
    scat = []
    for n, (k, o) in enumerate(units):
        gs, plane, ra, rb, xa, xb, below, above = held[k]
        scat.append(Scatter(place, n, o, plane.at[o], (ra.at[o], rb.at[o], xa.at[o], xb.at[o]), (below.at[o], above.at[o]),
                            (sc_s, sc_r, ls_s, ls_r)))

    def core(n):
        k, o = units[n]
        gs, plane = held[k][0], held[k][1]
        return remote(gs.at[:, other], plane.at[o], core_s.at[n], core_r.at[n], place.dev(place.gs, t))

    held_by = {}

    def compute(n):
        k, o = units[n]
        gs = held[k][0]
        if k in held_by:
            core(held_by[k]).wait_send()
        held_by[k] = n
        cols = slice(o * each, (o + 1) * each)
        if k == "d":
            ready("ct", ("d", o))
            r = tn(act[:, cols], ct[...]).astype(bf16)
            for g in range(GROUPS):
                gs[g // 2, g % 2] = r[:, g * 128 : (g + 1) * 128]
        elif k == "u":
            ready("hid2", ("u", o))
            gs[...] = tn(hid2[...], dpre[:, cols]).astype(bf16).reshape(gs.shape)
        elif k == "q":
            ready("hid1", "dqkv")
            w = gs.shape[-1]
            for c in range(3):
                r = tn(hid1[...], dqkv[c, 0:rows, o * w : (o + 1) * w]).astype(bf16)
                gs[:, :, c] = r.reshape(gs.shape[:2] + gs.shape[3:])
        else:
            ready("att", "dmb")
            m = gs.shape[2]
            r = tn(att[:, o * m : (o + 1) * m], dmb[...]).astype(bf16)
            for g in range(GROUPS):
                gs[g // 2, g % 2] = r[:, g * 128 : (g + 1) * 128]
        core(n).start()

    def settle(n):
        k, o = units[n]
        gs, plane = held[k][0], held[k][1]
        core(n).wait_recv()
        add_into(plane.at[o], gs.at[:, place.core])
        scat[n].first()

    partners = [place.dev(place.gs, t), place.dev(place.gx, t), place.dev(place.gy, t), near, far]
    pair = [remote(sums.at[i], got.at[i], sum_s.at[i], sum_r.at[i], dev) for i, dev in enumerate(partners)]

    def add_sums(i):
        pair[i].wait_recv()
        sums[i + 1] = sums[i] + got[i]
        if i + 1 < len(pair):
            pair[i + 1].start()

    def end(n):
        k, o = units[n]
        scat[n].final(out_of[k], outs.at[kinds.index(k)])

    steps = {"c": compute, "t": settle, "a": lambda n: scat[n].cross_x(), "b": lambda n: scat[n].cross_y(),
             "j": lambda n: scat[n].join(), "m": lambda n: scat[n].meet(), "e": end}
    for ev in GRADS:
        if ev[0] == "L":
            line.arrive(ev[1])
            if ev[1] < length - 1:
                line.pass_on(ev[1])
        elif ev[0] == "P":
            if ev[1] == 0:
                ready("sums")
                pair[0].start()
            else:
                add_sums(ev[1] - 1)
        elif ev[0] == "h":
            scat[units.index(ev[1:3])].hop(ev[3])
        else:
            steps[ev[0]](units.index(ev[1:3]))
    write = load(sums.at[len(pair)], sums_o, outs.at[len(kinds)])
    for n, (k, o) in enumerate(units):
        scat[n].drain(out_of[k], outs.at[kinds.index(k)])
    for n in held_by.values():
        core(n).wait_send()
    for q in pair:
        q.wait_send()
    for d in range(length - 1):
        line.drain(d)
    write.wait()


def grads(ratio, length, blocks, act, ct, hid2, dpre, hid1, dqkv, att, dmb, sums, gi_all):
    rows, width = ct.shape
    sds = jax.ShapeDtypeStruct
    hid = ((rows, width), bf16)
    outs = [(gi_all.shape, bf16)] + [(blocks[k], bf16) for k in ("d", "u", "o", "q")] + [(sums.shape, f32)]
    scratch = [(act.shape, bf16), hid, hid, (act.shape, bf16), hid, (dqkv.shape, bf16), hid, hid,
               ((6,) + sums.shape, f32), ((5,) + sums.shape, f32)]
    for k in ("d", "u", "q", "o"):
        b = tuple(blocks[k])
        h = b[:-2] + (b[-2] // 2, b[-1])
        for s in ((GROUPS // 2, 2) + b, (length, GROUPS // 2) + b, (length, 2) + h, (length, 2) + h, (length,) + h, (length,) + h,
                  (length,) + b, (length,) + b):
            scratch.append((s, bf16))
    n = 4 * length
    dma = pltpu.SemaphoreType.DMA
    return pl.pallas_call(
        functools.partial(grads_kernel, ratio, length),
        out_shape=[sds(*o) for o in outs],
        in_specs=[any_spec()] * 10,
        out_specs=[any_spec()] * len(outs),
        scratch_shapes=[pltpu.VMEM(*s) for s in scratch]
        + [dma((2, length)), dma((length,)), dma((n,)), dma((n,)), dma((n, 6)), dma((n, 6)), dma((n,)), dma((n, 2)), dma((5,)), dma((5,)),
           dma((7 + 2 * length,)), dma((5,))],
        input_output_aliases={9: 0},
        compiler_params=pltpu.CompilerParams(collective_id=2, has_side_effects=True, vmem_limit_bytes=VMEM_LIMIT),
        name="grads",
    )(act, ct, hid2, dpre, hid1, dqkv, att, dmb, sums, gi_all)


def place_kernel(out_i, gi_i, out_o, gi_o, buf_a, buf_b):
    length, rows, width = out_i.shape
    lanes = width // 128
    for r0 in range(0, rows, 16):
        base = r0 * lanes * length
        for b in range(length):
            a = out_i[b, r0 : r0 + 16, :].astype(f32)
            g = gi_i[b, r0 : r0 + 16, :].astype(f32)
            for j in range(lanes):
                at = pl.ds(base + j * length + b, 16, stride=lanes * length)
                buf_a[at, :] = a[:, j * 128 : (j + 1) * 128]
                gi_o[at, :] = g[:, j * 128 : (j + 1) * 128]
    out_o[...] = buf_a[...].astype(bf16)


def place_out(out_all, gi_all, seq):
    length, rows, width = out_all.shape
    lanes = width // 128
    blk = 64
    flat = seq * lanes * length
    spec_i = pl.BlockSpec((length, blk, width), lambda i: (0, i, 0))
    spec_o = pl.BlockSpec((blk * lanes * length, 128), lambda i: (i, 0))
    out, gi = pl.pallas_call(
        place_kernel,
        grid=(-(-seq // blk),),
        out_shape=[jax.ShapeDtypeStruct((flat, 128), bf16), jax.ShapeDtypeStruct((flat, 128), f32)],
        in_specs=[spec_i, spec_i],
        out_specs=[spec_o, spec_o],
        scratch_shapes=[pltpu.VMEM((blk * lanes * length, 128), f32), pltpu.VMEM((8, 128), f32)],
        name="place_out",
    )(out_all, gi_all)

    def shape(a):
        return a.reshape(seq, lanes, length, 128).transpose(2, 0, 1, 3).reshape(length, seq, width)

    return shape(out), shape(gi)


def local(inputs, lengths, norm_gains, norm_shifts, w_qkv, bias_qv, w_out, out_bias, w_up, b_up, w_down, cotangent):
    length = lax.axis_size("tensor")
    fsdp = lax.axis_size("fsdp")
    seq = inputs.shape[1]
    ratio, x_i, ct_i, mask, small, q_s, o_s, u_s, d_s = prepare(
        length, inputs, lengths, norm_gains, norm_shifts, w_qkv, bias_qv, w_out, out_bias, w_up, b_up, w_down, cotangent, fsdp
    )
    vec, wq, wo, wu, wd, hid1, qkv, att, lse, mid, hid2, act, gate, out_all, x, ct = forward(
        ratio, length, seq, inputs.shape[2], x_i, ct_i, mask[None, :], small, q_s, o_s, u_s, d_s
    )
    maskc = jnp.broadcast_to(mask[:, None], (mask.shape[0], 128))
    out_all, dpre, dqkv, dmb, gi_all, sums = back(
        ratio, length, vec, wd, wu, wo, wq, gate, mid, ct, x, qkv, att, lse, maskc, out_all
    )
    blocks = {"d": d_s.shape, "u": u_s.shape, "o": o_s.shape, "q": q_s.shape}
    gi_all, od, ou, oo, oq, sums = grads(ratio, length, blocks, act, ct, hid2, dpre, hid1, dqkv, att, dmb, sums, gi_all)
    output, grad_input = place_out(out_all, gi_all, seq)
    if ratio > 1:
        groups = [[g * ratio + r for r in range(ratio)] for g in range(GROUPS)]
        across = [[g * ratio + r for g in range(GROUPS)] for r in range(ratio)]

        def cut(a, axis):
            return lax.psum_scatter(a, "fsdp", scatter_dimension=axis, tiled=True, axis_index_groups=groups)

        od, ou, oo, oq = cut(od, 1), cut(ou, 0), cut(oo, 1), cut(oq, 1)
        sums = lax.psum(sums, "fsdp", axis_index_groups=groups)
    width = inputs.shape[2]
    f, t = lax.axis_index("fsdp"), lax.axis_index("tensor")
    own = lax.dynamic_slice_in_dim(sums[0:6], f * (width // fsdp), width // fsdp, 1)
    heads = width // length
    return (
        output,
        grad_input,
        own[0:2],
        own[2:4],
        oq.astype(f32),
        lax.dynamic_slice_in_dim(sums[6:8], t * heads, heads, 1),
        oo.astype(f32),
        own[4:6],
        ou.astype(f32),
        lax.dynamic_index_in_dim(sums, 8 + t, 0, keepdims=False),
        od.astype(f32),
    )


def solution(mesh):
    placed = (
        P("fsdp", None, None),
        P("fsdp"),
        P(None, "fsdp"),
        P(None, "fsdp"),
        P(None, "fsdp", "tensor"),
        P(None, "tensor"),
        P("tensor", "fsdp"),
        P(None, "fsdp"),
        P("fsdp", "tensor"),
        P("tensor"),
        P("tensor", "fsdp"),
        P("fsdp", None, None),
    )
    return jax.shard_map(
        local,
        mesh=mesh,
        in_specs=placed,
        out_specs=(
            P("fsdp", None, None),
            P("fsdp", None, None),
            P(None, "fsdp"),
            P(None, "fsdp"),
            P(None, "fsdp", "tensor"),
            P(None, "tensor"),
            P("tensor", "fsdp"),
            P(None, "fsdp"),
            P("fsdp", "tensor"),
            P("tensor"),
            P("tensor", "fsdp"),
        ),
        check_vma=False,
    )
```
